256 devices in a mesh: rep: 16 (over x, z_lo), tp: 16 (over z_hi, y, core).
Axes of the slice: x: 4, y: 4, z: 8 (z_hi: 2, z_lo: 4; z = z_hi * 4 + z_lo), core: 2. Of those that a mesh axis runs over, the one named last changes fastest.
Arguments:
- hidden: bfloat16 [16384, 4096], P('rep'), may hold values from -6 to 6
- norm_gain: bfloat16 [4096], replicated, may hold values from 0.099609375 to 1.8984375
- w_query: bfloat16 [4096, 4096], P('rep', 'tp'), may hold values from -0.09375 to 0.09375
- w_keyval: bfloat16 [4096, 1024], P('rep', 'tp'), may hold values from -0.09375 to 0.09375
- w_output: bfloat16 [4096, 4096], P('tp', 'rep'), may hold values from -0.09375 to 0.09375
- cache: bfloat16 [32768, 1024], P('rep'), may hold values from -190 to 190
- lengths: int32 [16, 4], P('rep'), may hold values from 1 to 640, 1024 in all within a row
- prefix: int32 [64], P('rep'), may hold values from 1 to 512, 16384 in all
- out_gain: bfloat16 [4096], replicated, may hold values from 0.099609375 to 1.8984375
Outputs:
- resid: bfloat16 [16384, 4096], P('rep', 'tp')
- normed: bfloat16 [16384, 4096], P('rep', 'tp')
The draws below stay inside these ranges and needn't reach their ends.
Inputs may be any that keep to these rules, and one draw needn't show every extreme that they name: `lengths`: each row sums to 1024, and some request has 640 new tokens. All prefixes sum to 16384, and some request has a prefix of 512.
All inputs are finite; a program needn't handle non-finite values. No bound on the sum of `prefix` on one device may be relied on, other than what follows from the above.
Results may differ from the reference program's by a relative error of at most 0.0095.
Values may be sent and summed in bfloat16 or wider, within the bound.
A program may use at most 128 MiB of HBM per device.

```python
import math
import jax
import jax.numpy as jnp
import numpy as np
from jax import lax

D = 4096
H = 32
KV = 4
HD = 128
TOK_REP = 1024
REQ_REP = 4
PREF_MAX = 512
MOST_LEN = 640
REPS = 16
REQUESTS = 64
TOKENS = 16384
PREF_TOTAL = 16384
N_REP = 16
N_TP = 16


def draw_cache(key, part):
    key_noise, key_sign, key_strength, key_head = jax.random.split(jax.random.fold_in(key, 11), 4)
    shape = (REQUESTS, PREF_MAX, KV, 2, HD)
    noise = jnp.clip(jax.random.normal(key_noise, shape, jnp.float32), -6.0, 6.0)
    strength = jax.random.uniform(key_strength, (REQUESTS,), jnp.float32, 60.0, 160.0)
    sign_pattern = jnp.where(jax.random.bernoulli(key_sign, 0.5, (REQUESTS, HD)), 1.0, -1.0)
    sink_head = jax.random.randint(key_head, (REQUESTS,), 0, KV)
    slot_ids = jnp.arange(PREF_MAX, dtype=jnp.int32)
    head_ids = jnp.arange(KV, dtype=jnp.int32)
    stretch = jnp.where(slot_ids == 0, 1.0, 1.012).astype(jnp.float32)
    sink = strength[:, None, None, None] * stretch[None, :, None, None] * sign_pattern[:, None, None, :]
    chosen = (slot_ids[None, :, None] < 2) & (head_ids[None, None, :] == sink_head[:, None, None])
    key_part = jnp.where(chosen[..., None], sink, noise[:, :, :, 0, :])
    stacked = jnp.stack([key_part, noise[:, :, :, 1, :]], axis=3)
    return stacked.reshape(REQUESTS * PREF_MAX, 2 * KV * HD).astype(jnp.bfloat16)


def levels(rng, shape, cuts, smallest, high):
    def one(dim, blocks):
        heights = jax.random.uniform(jax.random.fold_in(jax.random.fold_in(rng, 6), dim), (blocks,), jnp.float32, smallest / len(cuts), high / len(cuts))
        return jnp.repeat(jnp.exp(heights), shape[dim] // blocks).reshape((-1,) + (1,) * (len(shape) - dim - 1))

    factor_of = one(*cuts[0])
    for cut in cuts[1:]:
        factor_of = factor_of * one(*cut)
    return factor_of


def split_up(number_of, total, bound, lean):
    portions = [(1 << 20) // math.isqrt(grade ** lean) + 1 for grade in range(2, number_of + 1)]
    spare, counts = total - bound - (number_of - 1), [1] * (number_of - 1)
    while spare > 0:
        candidates = [i for i in range(number_of - 1) if counts[i] < bound]
        mass, budget = sum([portions[i] for i in candidates]), spare
        for i in candidates:
            addition = min(bound - counts[i], max(1, budget * portions[i] // mass), spare)
            counts[i] = counts[i] + addition
            spare = spare - addition
    return np.array([bound] + counts)


def uneven(rng, amount, total, reach, slope):
    if amount == 2:
        one = jax.random.randint(rng, (), max(1, total - reach), min(reach, total - 1) + 1)
        return jnp.stack([one, total - one])
    tallies = jnp.asarray(split_up(amount, total, reach, slope), jnp.int32)
    twos = (amount - 1) // 2
    donor, receiver = tallies[1:1 + 2 * twos:2], tallies[2:2 + 2 * twos:2]
    slack = jnp.minimum(donor - 1, reach - receiver)
    moved = jax.random.randint(jax.random.fold_in(rng, 1), (twos,), 0, 1 << 20) % (slack + 1)
    tallies = tallies.at[1:1 + 2 * twos:2].set(donor - moved).at[2:2 + 2 * twos:2].set(receiver + moved)
    return tallies[jax.random.permutation(jax.random.fold_in(rng, 2), amount)]


def centred(stream_key, shape, scale, reach, shards=(), kind=jnp.bfloat16):
    result = jax.random.normal(stream_key, shape, jnp.float32) * scale
    if len(shards) > 0:
        result = levels(stream_key, shape, shards, -0.22, 0.18) * result
    return jnp.clip(result, min=-reach, max=reach).astype(kind)


def setup_inputs(seed: int = 0) -> dict:
    seeds = jax.random.split(jax.random.key(seed), 10)
    return {
        "hidden": centred(seeds[0], (TOKENS, D), 1.0, 6.0, ((0, 16),)),
        "norm_gain": jnp.clip(1.0 + 0.18 * jax.random.normal(seeds[1], (D,), jnp.float32), 0.099609375, 1.8984375).astype(jnp.bfloat16),
        "w_query": centred(seeds[2], (D, H * HD), D ** -0.5, 0.09375, ((0, 16), (1, 16))),
        "w_keyval": centred(seeds[3], (D, 2 * KV * HD), D ** -0.5, 0.09375, ((0, 16), (1, 16))),
        "w_output": centred(seeds[4], (H * HD, D), (H * HD) ** -0.5, 0.09375, ((0, 16), (1, 16))),
        "cache": draw_cache(jax.random.fold_in(seeds[9], 71), 0),
        "lengths": jax.vmap(lambda own: uneven(own, REQ_REP, TOK_REP, MOST_LEN, 1))(jax.random.split(seeds[6], REPS)).reshape((REPS, REQ_REP)).astype(jnp.int32),
        "prefix": uneven(seeds[7], REQUESTS, PREF_TOTAL, PREF_MAX, 2).astype(jnp.int32),
        "out_gain": jnp.clip(1.0 + 0.18 * jax.random.normal(seeds[8], (D,), jnp.float32), 0.099609375, 1.8984375).astype(jnp.bfloat16),
    }


norm_eps = 1e-05
rope_base = 5000000.0
masked_score = -1e+30

def rms_scale(values, weights):
    meansq = lax.optimization_barrier(jnp.mean(values * values, axis=-1, keepdims=True))
    return values * lax.rsqrt(meansq + norm_eps) * weights

def rotate(values, positions):
    half_dim = values.shape[-1] // 2
    freqs = rope_base ** (-(jnp.arange(half_dim, dtype=jnp.float32) * 2.0 / values.shape[-1]))
    angles = positions.astype(jnp.float32)[:, None] * freqs[None, :]
    cosine = jnp.cos(angles)[:, None, :]
    sine = jnp.sin(angles)[:, None, :]
    first = values[..., :half_dim]
    second = values[..., half_dim:]
    return jnp.concatenate([first * cosine - second * sine, second * cosine + first * sine], axis=-1)

def request_layout(lens, prefs, count):
    token_ids = jnp.arange(count, dtype=jnp.int32)
    ends = jnp.cumsum(lens).astype(jnp.int32)
    starts = ends - lens
    segment = lax.optimization_barrier(jnp.sum((token_ids[:, None] >= ends[None, :]).astype(jnp.int32), axis=1))
    onehot = segment[:, None] == jnp.arange(lens.shape[0], dtype=jnp.int32)[None, :]
    offset = token_ids - lax.optimization_barrier(jnp.sum(jnp.where(onehot, starts[None, :], 0), axis=1))
    position = offset + lax.optimization_barrier(jnp.sum(jnp.where(onehot, prefs[None, :], 0), axis=1))
    return (token_ids, segment, position)

def reference(hidden, norm_gain, w_query, w_keyval, w_output, cache, lengths, prefix, out_gain):
    group_size = H // KV
    blocks_hidden = hidden.reshape(N_REP, TOK_REP, D)
    blocks_pref = prefix.reshape(N_REP, REQ_REP)
    blocks_cache = cache.reshape(N_REP, REQ_REP * PREF_MAX, 2 * KV * HD)
    wo_groups = w_output.reshape(N_TP, H * HD // N_TP, D).astype(jnp.float32)

    def one_group(items):
        block, lens, prefs, cached = items
        normed_in = rms_scale(block.astype(jnp.float32), norm_gain.astype(jnp.float32)).astype(jnp.bfloat16)
        queries = jnp.dot(normed_in, w_query, preferred_element_type=jnp.float32).reshape(TOK_REP, H, HD)
        fresh = jnp.dot(normed_in, w_keyval, preferred_element_type=jnp.float32).astype(jnp.bfloat16)
        fresh = fresh.reshape(TOK_REP, 2, HD, KV).transpose(0, 3, 1, 2)
        token_ids, segment, position = request_layout(lens, prefs, TOK_REP)
        queries = rotate(queries, position).astype(jnp.bfloat16)
        new_keys = rotate(fresh[:, :, 0, :].astype(jnp.float32), position).astype(jnp.bfloat16)
        new_vals = fresh[:, :, 1, :]
        stored = cached.reshape(REQ_REP * PREF_MAX, KV, 2, HD)
        slot_ids = jnp.arange(REQ_REP * PREF_MAX, dtype=jnp.int32)
        slot_req = slot_ids // PREF_MAX
        slot_pos = slot_ids % PREF_MAX
        req_ids = jnp.arange(REQ_REP, dtype=jnp.int32)
        slot_len = lax.optimization_barrier(jnp.sum(jnp.where(slot_req[:, None] == req_ids[None, :], prefs[None, :], 0), axis=1))
        cache_ok = (segment[:, None] == slot_req[None, :]) & (slot_pos < slot_len)[None, :]
        own_ok = (segment[:, None] == segment[None, :]) & (token_ids[None, :] <= token_ids[:, None])
        allowed = jnp.concatenate([cache_ok, own_ok], axis=1)
        all_keys = jnp.concatenate([stored[:, :, 0, :], new_keys], axis=0).astype(jnp.float32)
        all_vals = jnp.concatenate([stored[:, :, 1, :], new_vals], axis=0).astype(jnp.float32)
        grouped = queries.reshape(TOK_REP, KV, group_size, HD).astype(jnp.float32)
        scores = jnp.einsum('tkgd,skd->kgts', grouped, all_keys) * HD ** (-0.5)
        scores = jnp.where(allowed[None, None], scores, masked_score)
        peak = lax.optimization_barrier(jnp.max(scores, axis=-1, keepdims=True))
        expo = jnp.where(allowed[None, None], jnp.exp(scores - peak), 0.0)
        total = lax.optimization_barrier(jnp.sum(expo, axis=-1))
        rounded = lax.optimization_barrier(expo.astype(jnp.bfloat16)).astype(jnp.float32)
        summed = jnp.einsum('kgts,skd->kgtd', rounded, all_vals)
        attended = (summed / total[..., None]).transpose(2, 0, 1, 3).reshape(TOK_REP, H * HD)
        attended = attended.astype(jnp.bfloat16)
        groups = attended.reshape(TOK_REP, N_TP, H * HD // N_TP).astype(jnp.float32)
        parts = jnp.einsum('tnc,ncd->ntd', groups, wo_groups)
        parts = lax.optimization_barrier(parts.astype(jnp.bfloat16)).astype(jnp.float32)
        proj = lax.optimization_barrier(jnp.sum(parts, axis=0))
        resid = (block.astype(jnp.float32) + proj).astype(jnp.bfloat16)
        normed = rms_scale(resid.astype(jnp.float32), out_gain.astype(jnp.float32)).astype(jnp.bfloat16)
        return (resid, normed)
    resid, normed = lax.map(one_group, (blocks_hidden, lengths, blocks_pref, blocks_cache))
    return (resid.reshape(TOKENS, D), normed.reshape(TOKENS, D))
```

```python
import functools
import math

import jax
import jax.numpy as jnp
from jax import lax
from jax.experimental import pallas as pl
from jax.experimental.pallas import tpu as pltpu
from jax.sharding import PartitionSpec as P

H = 32
KV = 4
HD = 128
REQ_REP = 4
PREF_MAX = 512

norm_eps = 1e-05
rope_base = 5000000.0
TQ = 128
KB = 256
NEG_START = -1e30
NEG_MASK = -2e30


def rms_scale(values, weights):
    meansq = jnp.mean(values * values, axis=-1, keepdims=True)
    return values * lax.rsqrt(meansq + norm_eps) * weights


def rotate(values, positions):
    half_dim = values.shape[-1] // 2
    freqs = rope_base ** (-(jnp.arange(half_dim, dtype=jnp.float32) * 2.0 / values.shape[-1]))
    angles = positions.astype(jnp.float32)[:, None] * freqs[None, :]
    cosine = jnp.cos(angles)[:, None, :]
    sine = jnp.sin(angles)[:, None, :]
    first = values[..., :half_dim]
    second = values[..., half_dim:]
    return jnp.concatenate(
        [first * cosine - second * sine, second * cosine + first * sine], axis=-1
    )


def request_layout(lens, prefs, count):
    token_ids = jnp.arange(count, dtype=jnp.int32)
    ends = jnp.cumsum(lens)
    starts = ends - lens
    segment = jnp.sum((token_ids[:, None] >= ends[None, :]).astype(jnp.int32), axis=1)
    onehot = segment[:, None] == jnp.arange(lens.shape[0], dtype=jnp.int32)[None, :]
    offset = token_ids - jnp.sum(jnp.where(onehot, starts[None, :], 0), axis=1)
    position = offset + jnp.sum(jnp.where(onehot, prefs[None, :], 0), axis=1)
    return position, starts, ends


def attention_kernel(meta, q_ref, k_ref, v_ref, cache_ref, o_ref, stored, m_ref, l_ref, acc_ref, sems):
    kv_head = meta[12]
    column = pl.multiple_of(kv_head * 2 * HD, 2 * HD)
    copies = []
    for request in range(REQ_REP):
        rows = pl.ds(request * PREF_MAX, PREF_MAX)
        copies.append(
            pltpu.make_async_copy(
                cache_ref.at[rows, pl.ds(column, 2 * HD)], stored.at[rows, :], sems.at[request]
            )
        )
        copies[-1].start()
    factor = HD ** (-0.5) * math.log2(math.e)
    heads = q_ref.shape[1] // HD

    def step(q, key, value, mask):
        s = lax.dot_general(q, key, (((1,), (1,)), ((), ())), preferred_element_type=jnp.float32)
        if mask is not None:
            s = jnp.where(mask, s, NEG_MASK)
        old = m_ref[...]
        new = jnp.maximum(old, jnp.max(s, axis=1, keepdims=True))
        shrink = jnp.exp2((old - new) * factor)
        m_ref[...] = new
        p = jnp.exp2((s - new[:, :1]) * factor)
        folded = p[:, :HD]
        for part in range(1, KB // HD):
            folded = folded + p[:, part * HD : (part + 1) * HD]
        l_ref[...] = l_ref[...] * shrink + folded
        acc_ref[...] = acc_ref[...] * shrink + jnp.dot(
            p.astype(jnp.bfloat16), value, preferred_element_type=jnp.float32
        )

    shape = (heads * TQ, KB)
    lane = lax.broadcasted_iota(jnp.int32, shape, 1)
    row = lax.rem(lax.broadcasted_iota(jnp.int32, shape, 0), TQ)
    for request in range(REQ_REP):
        start, end, prefix = meta[request], meta[4 + request], meta[8 + request]
        base = request * PREF_MAX
        copies[request].wait()

        def tile_body(tile, _):
            first = pl.multiple_of(tile * TQ, TQ)
            rows = pl.ds(first, TQ)
            q = jnp.concatenate([q_ref[rows, h * HD : (h + 1) * HD] for h in range(heads)], axis=0)
            m_ref[...] = jnp.full_like(m_ref, NEG_START)
            l_ref[...] = jnp.zeros_like(l_ref)
            acc_ref[...] = jnp.zeros_like(acc_ref)

            def full_block(block, _):
                at = pl.ds(base + pl.multiple_of(block * KB, KB), KB)
                step(q, stored[at, :HD], stored[at, HD:], None)
                return 0

            whole = prefix // KB
            lax.fori_loop(0, whole, full_block, 0)

            @pl.when(whole * KB < prefix)
            def _():
                at = pl.ds(base + pl.multiple_of(whole * KB, KB), KB)
                step(q, stored[at, :HD], stored[at, HD:], lane + whole * KB < prefix)

            def own_block(block, _):
                at = pl.ds(pl.multiple_of(block * KB, KB), KB)
                key_id = lane + block * KB
                step(q, k_ref[at, :], v_ref[at, :], (key_id >= start) & (key_id <= row + first))
                return 0

            def clear_block(block, _):
                at = pl.ds(pl.multiple_of(block * KB, KB), KB)
                step(q, k_ref[at, :], v_ref[at, :], None)
                return 0

            low = start // KB
            high = first // KB
            lax.fori_loop(low, jnp.minimum(low + 1, high), own_block, 0)
            lax.fori_loop(low + 1, high, clear_block, 0)
            own_block(high, 0)
            total = jnp.sum(l_ref[...], axis=1, keepdims=True)
            result = (acc_ref[...] / total).astype(o_ref.dtype)
            tok = first + lax.broadcasted_iota(jnp.int32, (TQ, HD), 0)
            own = (tok >= start) & (tok < end)
            for h in range(heads):
                at = slice(h * HD, (h + 1) * HD)
                o_ref[rows, at] = jnp.where(
                    own, result[h * TQ : (h + 1) * TQ].astype(jnp.float32), o_ref[rows, at].astype(jnp.float32)
                ).astype(o_ref.dtype)
            return 0

        lax.fori_loop(start // TQ, (end - 1) // TQ + 1, tile_body, 0)


def attend(meta, q, k, v, cache):
    rows, width = q.shape
    heads = width // HD
    return pl.pallas_call(
        attention_kernel,
        out_shape=jax.ShapeDtypeStruct((rows, width), jnp.bfloat16),
        in_specs=[
            pl.BlockSpec(memory_space=pltpu.SMEM),
            pl.BlockSpec(memory_space=pltpu.VMEM),
            pl.BlockSpec(memory_space=pltpu.VMEM),
            pl.BlockSpec(memory_space=pltpu.VMEM),
            pl.BlockSpec(memory_space=pl.ANY),
        ],
        out_specs=pl.BlockSpec(memory_space=pltpu.VMEM),
        scratch_shapes=[
            pltpu.VMEM((REQ_REP * PREF_MAX, 2 * HD), jnp.bfloat16),
            pltpu.VMEM((heads * TQ, HD), jnp.float32),
            pltpu.VMEM((heads * TQ, HD), jnp.float32),
            pltpu.VMEM((heads * TQ, HD), jnp.float32),
            pltpu.SemaphoreType.DMA((REQ_REP,)),
        ],
        cost_estimate=pl.CostEstimate(flops=2 * 10**9, bytes_accessed=3 * 2**20, transcendentals=2 * 10**6),
        name="attention",
    )(meta, q, k, v, cache)


def body(hidden, norm_gain, w_query, w_keyval, w_output, cache, lengths, prefix, out_gain):
    tp_count = lax.axis_size("tp")
    rep_count = lax.axis_size("rep")
    tp_index = lax.axis_index("tp")
    rows = hidden.shape[0]
    swapped = lax.ppermute(
        w_output,
        ("rep", "tp"),
        [(a * tp_count + b, b * tp_count + a) for a in range(rep_count) for b in range(tp_count)],
    )
    normed_in = rms_scale(hidden.astype(jnp.float32), norm_gain.astype(jnp.float32)).astype(
        jnp.bfloat16
    )
    query_raw = jnp.dot(
        normed_in,
        lax.all_gather(w_query, "rep", axis=0, tiled=True),
        preferred_element_type=jnp.float32,
    )
    fresh_part = jnp.dot(
        normed_in,
        lax.all_gather(w_keyval, "rep", axis=0, tiled=True),
        preferred_element_type=jnp.float32,
    )
    fresh_all = lax.all_gather(fresh_part.astype(jnp.bfloat16), "tp", axis=1, tiled=True)
    heads_here = w_query.shape[1] // HD
    kv_head = tp_index * heads_here // (H // KV)
    kv_count = fresh_all.shape[1] // (2 * HD)
    fresh_head = lax.dynamic_slice_in_dim(fresh_all.reshape(rows, 2 * HD, kv_count), kv_head, 1, 2)
    fresh_head = fresh_head.reshape(rows, 2 * HD)
    position, starts, ends = request_layout(lengths.reshape(-1), prefix, rows)
    queries = rotate(query_raw.reshape(rows, heads_here, HD), position).astype(jnp.bfloat16)
    queries = queries.reshape(rows, heads_here * HD)
    new_keys = rotate(fresh_head[:, :HD].astype(jnp.float32).reshape(rows, 1, HD), position)
    new_keys = new_keys.reshape(rows, HD).astype(jnp.bfloat16)
    new_vals = fresh_head[:, HD:]
    meta = jnp.concatenate([starts, ends, prefix, kv_head.reshape(1)]).astype(jnp.int32)
    attended = attend(meta, queries, new_keys, new_vals, cache)
    w_columns = lax.all_gather(swapped, "rep", axis=0, tiled=True)
    attended_all = lax.all_gather(attended, "tp", axis=1, tiled=True)
    width = hidden.shape[1] // tp_count
    proj = jnp.dot(attended_all, w_columns, preferred_element_type=jnp.float32)
    mine = lax.dynamic_slice_in_dim(hidden, tp_index * width, width, 1)
    gain = lax.dynamic_slice_in_dim(out_gain, tp_index * width, width, 0)
    resid = (mine.astype(jnp.float32) + proj).astype(jnp.bfloat16)
    wide = resid.astype(jnp.float32)
    meansq = lax.psum(jnp.sum(wide * wide, axis=-1, keepdims=True), "tp") / hidden.shape[1]
    normed = (wide * lax.rsqrt(meansq + norm_eps) * gain.astype(jnp.float32)).astype(jnp.bfloat16)
    return (resid, normed)


def solution(mesh):
    placed = (
        P("rep", None),
        P(),
        P("rep", "tp"),
        P("rep", "tp"),
        P("tp", "rep"),
        P("rep", None),
        P("rep", None),
        P("rep"),
        P(),
    )
    return jax.shard_map(
        body,
        mesh=mesh,
        in_specs=placed,
        out_specs=(P("rep", "tp"), P("rep", "tp")),
        check_vma=False,
    )
```

```python
import math

import jax
import jax.numpy as jnp
from jax import lax
from jax.experimental import pallas as pl
from jax.experimental.pallas import tpu as pltpu
from jax.sharding import PartitionSpec as P

H = 32
KV = 4
HD = 128
REQ_REP = 4
PREF_MAX = 512

norm_eps = 1e-05
rope_base = 5000000.0
TQ = 128
KB = 256
NEG_START = -1e30
NEG_MASK = -2e30
CHUNKS = 4


MESH = pl.DeviceIdType.MESH
D = 4096
BLK = 256


def place():
    rep, tp = lax.axis_index("rep"), lax.axis_index("tp")
    return rep, tp, rep // 4, rep % 4, tp // 8, (tp // 2) % 4, tp % 2


def line_order(z):
    power = 1 + 3 * z + 9 * (z * (z - 1) // 2) + 27 * (z * (z - 1) * (z - 2) // 6)
    tables = []
    for picks in ((1, 0, 1, 2), (2, 2, 3, 1), (3, 3, 0, 0)):
        tables.append(sum(pick * 4**i for i, pick in enumerate(picks)))
    return [z] + [(table // power) % 4 for table in tables]


def signal(sem, device):
    pl.semaphore_signal(sem, inc=1, device_id=device, device_id_type=MESH)


class Gather:
    def __init__(self, own, full, recv, send, half):
        self.own, self.full, self.recv, self.send, self.half = own, full, recv, send, half
        self.rep, self.tp, self.x, self.z = place()[:4]
        self.order = line_order(self.z)
        self.right = ((self.x + 1) % 4) * 4
        self.left = ((self.x + 3) % 4) * 4
        self.far = ((self.x + 2) % 4) * 4
        self.pending = []

    def copy(self, src, dst, slot, sem, rep, cond=None):
        made = pltpu.make_async_remote_copy(
            src_ref=src,
            dst_ref=dst,
            send_sem=self.send.at[slot],
            recv_sem=sem,
            device_id=(rep, self.tp),
            device_id_type=MESH,
        )
        if cond is None:
            made.start()
        else:
            pl.when(cond)(made.start)
        self.pending.append((made, cond))

    def arrived(self, index, block):
        ref = self.full.at[block]
        pltpu.make_async_copy(ref, ref, self.recv.at[index, block]).wait()

    def line(self, k):
        zo = self.order[k]
        block = self.x * 4 + zo
        dst, sem = self.full.at[block], self.recv.at[0, block]
        if k == 0:
            src = self.own
            onward, back = self.z < 3, self.z > 0
        else:
            self.arrived(0, block)
            src = dst
            onward, back = (zo < self.z) & (self.z < 3), (zo > self.z) & (self.z > 0)
        self.copy(src, dst, 6 * k, sem, self.x * 4 + lax.min(self.z + 1, 3), onward)
        self.copy(src, dst, 6 * k + 1, sem, self.x * 4 + lax.max(self.z - 1, 0), back)
        self.copy(src, dst, 6 * k + 2, sem, self.right + self.z)
        self.copy(src, dst, 6 * k + 3, sem, self.left + self.z)

    def ring(self, k, side):
        zo = self.order[k]
        block = (self.left if side == 0 else self.right) + zo
        self.arrived(0, block)
        part = pl.ds(0, self.half) if side == 0 else pl.ds(self.half, self.half)
        ref = self.full.at[block, part]
        target = (self.right if side == 0 else self.left) + self.z
        self.copy(ref, ref, 6 * k + 4 + side, self.recv.at[side, block], target)
        return block

    def opposite(self, k):
        block = self.far + self.order[k]
        for side in range(2):
            ref = self.full.at[block, pl.ds(side * self.half, self.half)]
            pltpu.make_async_copy(ref, ref, self.recv.at[side, block]).wait()
        return block

    def drain(self):
        for made, cond in self.pending:
            if cond is None:
                made.wait_send()
            else:
                pl.when(cond)(made.wait_send)


def project_kernel(
    lens_ref, pref_ref, hidden_ref, gain_ref, freq_ref, wq_ref, wkv_ref, wo_ref,
    q_ref, k_ref, v_ref, wo_out,
    hid, x3, full_q, full_s, turned, qacc, kacc, cosine, sine, mine, other,
    hid_sem, recv_q, send_q, recv_s, send_s, kv_send, kv_recv, perm_send, perm_recv, swap_sem, out_sem,
):
    rep, tp, x, z, zh, y, c = place()
    rows = hid.shape[0]
    count = hid_sem.shape[0]
    chunk = rows // count
    loads = []
    for i in range(count):
        at = pl.ds(i * chunk, chunk)
        loads.append(pltpu.make_async_copy(hidden_ref.at[at], hid.at[at], hid_sem.at[i]))
        loads[-1].start()

    zh_t = x // 2
    perm_dst = (y * 4 + zh_t * 2 + c, zh * 8 + ((x % 2) * 2 + z // 2) * 2 + z % 2)
    perm_src = (((z // 2) * 2 + y // 2) * 4 + (y % 2) * 2 + c, zh * 8 + x * 2 + z % 2)
    perm_away = (perm_dst[0] != rep) | (perm_dst[1] != tp)
    barrier = pltpu.get_barrier_semaphore()
    line_right, line_left = x * 4 + lax.min(z + 1, 3), x * 4 + lax.max(z - 1, 0)

    pl.when(z < 3)(lambda: signal(barrier, (line_right, tp)))
    pl.when(z > 0)(lambda: signal(barrier, (line_left, tp)))
    signal(barrier, (((x + 1) % 4) * 4 + z, tp))
    signal(barrier, (((x + 3) % 4) * 4 + z, tp))
    signal(barrier, (rep, tp + 1 - 2 * c))
    pl.when(perm_away)(lambda: signal(barrier, perm_src))
    for j in range(8):
        source = c * 8 + j
        pl.when(source != tp)(lambda source=source: signal(barrier, (rep, source)))
    line_peers = (lax.min(z + 1, 3) - z) + (z - lax.max(z - 1, 0))
    pl.semaphore_wait(barrier, 10 + line_peers + perm_away.astype(jnp.int32) + (c + zh) % 2)

    stream_q = Gather(wq_ref, full_q, recv_q, send_q, BLK // 2)
    stream_s = Gather(full_s.at[rep], full_s, recv_s, send_s, full_s.shape[1] // 2)
    stream_q.line(0)

    wo_dst = full_s.at[perm_dst[0], pl.ds(HD, BLK)]
    permute = pltpu.make_async_remote_copy(
        src_ref=wo_ref, dst_ref=wo_dst, send_sem=perm_send, recv_sem=perm_recv,
        device_id=perm_dst, device_id_type=MESH,
    )
    stay = pltpu.make_async_copy(wo_ref, wo_dst, perm_recv)
    pl.when(perm_away)(permute.start)
    pl.when(jnp.logical_not(perm_away))(stay.start)

    shape = (4 * 16, 4 * 16)
    out_row, in_col = lax.broadcasted_iota(jnp.int32, shape, 0), lax.broadcasted_iota(jnp.int32, shape, 1)
    pick = ((out_row % 16) * KV + out_row // 16 == in_col).astype(jnp.float32).astype(jnp.bfloat16)
    turned[...] = lax.dot_general(
        pick, wkv_ref[...], (((1,), (1,)), ((), ())), preferred_element_type=jnp.float32
    ).astype(jnp.bfloat16)

    starts, first_token = [], 0
    for request in range(REQ_REP):
        starts.append(first_token)
        first_token = first_token + lens_ref[0, request]

    def angles(i, _):
        at = pl.ds(pl.multiple_of(i * 128, 128), 128)
        token = i * 128 + lax.broadcasted_iota(jnp.int32, (128, HD), 0)
        position = jnp.zeros((128, HD), jnp.int32)
        for request in range(REQ_REP):
            shift = pref_ref[request] - starts[request]
            position = jnp.where(token >= starts[request], token + shift, position)
        angle = position.astype(jnp.float32) * freq_ref[...]
        lane = lax.broadcasted_iota(jnp.int32, (128, HD), 1)
        cosine[at, :] = jnp.cos(angle)
        wave = jnp.sin(angle)
        sine[at, :] = jnp.where(lane < HD // 2, -wave, wave)
        return 0

    def norm(i):
        loads[i].wait()

        def some(j, _):
            at = pl.ds(pl.multiple_of(i * chunk + j * 16, 16), 16)
            wide = hid[at, :].astype(jnp.float32)
            meansq = jnp.sum(wide * wide, axis=1, keepdims=True) * (1.0 / D)
            scaled = wide * lax.rsqrt(meansq + norm_eps)
            for b in range(D // BLK):
                cols = slice(b * BLK, (b + 1) * BLK)
                x3[b, at, :] = (scaled[:, cols] * gain_ref[:, cols].astype(jnp.float32)).astype(jnp.bfloat16)
            return 0

        lax.fori_loop(0, chunk // 16, some, 0)

    def piece(head, which):
        target = (head // 2) * 8 + (2 * (head % 2) + which) * 2 + zh
        from_ref = turned.at[pl.ds(head * 16, 16)]
        to_ref = full_s.at[rep, pl.ds(pl.multiple_of((tp % 8) * 16, 16), 16)]
        away = target != tp
        made = pltpu.make_async_remote_copy(
            src_ref=from_ref, dst_ref=to_ref, send_sem=kv_send.at[head * 2 + which], recv_sem=kv_recv.at[tp % 8],
            device_id=(rep, target), device_id_type=MESH,
        )
        here = pltpu.make_async_copy(from_ref, to_ref, kv_recv.at[tp % 8])
        pl.when(away)(made.start)
        pl.when(jnp.logical_not(away))(here.start)
        return made, away

    def use_q(block, own=False):
        for i in range(rows // BLK):
            at = pl.ds(i * BLK, BLK)
            weight = wq_ref[...] if own else full_q[block]
            part = jnp.dot(x3[block, at, :], weight, preferred_element_type=jnp.float32)
            qacc[at, :] = part if own else qacc[at, :] + part

    def use_s(block, own=False):
        for i in range(rows // BLK):
            at = pl.ds(i * BLK, BLK)
            part = lax.dot_general(
                x3[block, at, :], full_s[block, :HD, :], (((1,), (1,)), ((), ())),
                preferred_element_type=jnp.float32,
            )
            kacc[at, :] = part if own else kacc[at, :] + part

    norm(0)
    pieces = [piece(head, which) for head in range(KV) for which in range(2)]
    lax.fori_loop(0, rows // 128, angles, 0)
    norm(1)
    stream_q.line(1)
    norm(2)
    for j in range(8):
        ref = full_s.at[rep, pl.ds(j * 16, 16)]
        pltpu.make_async_copy(ref, ref, kv_recv.at[j]).wait()
    own_wo = full_s.at[rep, pl.ds(HD, BLK)]
    pltpu.make_async_copy(own_wo, own_wo, perm_recv).wait()
    stream_s.line(0)
    norm(3)
    stream_q.line(2)
    norm(4)
    stream_s.line(1)
    norm(5)
    stream_q.line(3)
    norm(6)
    stream_s.line(2)
    norm(7)
    stream_s.line(3)
    use_q(rep, True)
    use_s(rep, True)
    for k in range(4):
        lefts, rights = stream_q.ring(k, 0), stream_q.ring(k, 1)
        lefts_s, rights_s = stream_s.ring(k, 0), stream_s.ring(k, 1)
        if k > 0:
            own_block = x * 4 + stream_q.order[k]
            use_q(own_block)
            use_s(own_block)
        for block in (lefts, rights):
            use_q(block)
        for block in (lefts_s, rights_s):
            use_s(block)
        if k > 0:
            use_q(stream_q.opposite(k - 1))
    use_q(stream_q.opposite(3))
    for k in range(4):
        use_s(stream_s.opposite(k))
    flush = pltpu.make_async_copy(full_s.at[:, pl.ds(HD, BLK)], wo_out, out_sem)
    flush.start()

    fresh = kacc[...].astype(jnp.bfloat16).astype(jnp.float32)
    turned_key = fresh * cosine[...] + pltpu.roll(fresh, HD // 2, 1) * sine[...]
    mine[...] = jnp.where(c == 0, turned_key, fresh).astype(jnp.bfloat16)
    swap = pltpu.make_async_remote_copy(
        src_ref=mine, dst_ref=other, send_sem=swap_sem.at[0], recv_sem=swap_sem.at[1],
        device_id=(rep, tp + 1 - 2 * c), device_id_type=MESH,
    )
    for h in range(q_ref.shape[1] // HD):
        cols = slice(h * HD, (h + 1) * HD)
        u = qacc[:, cols]
        q_ref[:, cols] = (u * cosine[...] + pltpu.roll(u, HD // 2, 1) * sine[...]).astype(jnp.bfloat16)
        if h == 0:
            swap.start()
    for made, away in pieces:
        pl.when(away)(made.wait_send)
    pl.when(perm_away)(permute.wait_send)
    stream_q.drain()
    stream_s.drain()
    swap.wait()

    @pl.when(c == 0)
    def _():
        k_ref[...] = mine[...]
        v_ref[...] = other[...]

    @pl.when(c != 0)
    def _():
        k_ref[...] = other[...]
        v_ref[...] = mine[...]

    flush.wait()


def vmem():
    return pl.BlockSpec(memory_space=pltpu.VMEM)


def smem():
    return pl.BlockSpec(memory_space=pltpu.SMEM)


def anywhere():
    return pl.BlockSpec(memory_space=pl.ANY)


def project(lengths, prefix, hidden, norm_gain, freqs, w_query, w_keyval, w_output):
    rows = hidden.shape[0]
    bf16, f32, dma = jnp.bfloat16, jnp.float32, pltpu.SemaphoreType.DMA
    return pl.pallas_call(
        project_kernel,
        out_shape=(
            jax.ShapeDtypeStruct((rows, BLK), bf16),
            jax.ShapeDtypeStruct((rows, HD), bf16),
            jax.ShapeDtypeStruct((rows, HD), bf16),
            jax.ShapeDtypeStruct((16, BLK, BLK), bf16),
        ),
        in_specs=[smem(), smem(), anywhere(), vmem(), vmem(), vmem(), vmem(), vmem()],
        out_specs=(vmem(), vmem(), vmem(), anywhere()),
        scratch_shapes=[
            pltpu.VMEM((rows, D), bf16),
            pltpu.VMEM((16, rows, BLK), bf16),
            pltpu.VMEM((16, BLK, BLK), bf16),
            pltpu.VMEM((16, HD + BLK, BLK), bf16),
            pltpu.VMEM((64, BLK), bf16),
            pltpu.VMEM((rows, BLK), f32),
            pltpu.VMEM((rows, HD), f32),
            pltpu.VMEM((rows, HD), f32),
            pltpu.VMEM((rows, HD), f32),
            pltpu.VMEM((rows, HD), bf16),
            pltpu.VMEM((rows, HD), bf16),
            dma((8,)),
            dma((2, 16)),
            dma((24,)),
            dma((2, 16)),
            dma((24,)),
            dma((8,)),
            dma((8,)),
            dma,
            dma,
            dma((2,)),
            dma,
        ],
        compiler_params=pltpu.CompilerParams(collective_id=0, has_side_effects=True, vmem_limit_bytes=52 * 2**20),
        cost_estimate=pl.CostEstimate(flops=3 * 10**9, bytes_accessed=12 * 2**20, transcendentals=10**6),
        name="project",
    )(lengths, prefix, hidden, norm_gain, freqs, w_query, w_keyval, w_output)


def attention_kernel(lens_ref, pref_ref, q_ref, k_ref, v_ref, cache_ref, o_ref, stored, m_ref, l_ref, acc_ref, sems):
    kv_head = lax.axis_index("tp") // 4
    column = pl.multiple_of(kv_head * 2 * HD, 2 * HD)
    copies = []
    for request in range(REQ_REP):
        rows = pl.ds(request * PREF_MAX, PREF_MAX)
        copies.append(
            pltpu.make_async_copy(
                cache_ref.at[rows, pl.ds(column, 2 * HD)], stored.at[rows, :], sems.at[request]
            )
        )
        copies[-1].start()
    factor = HD ** (-0.5) * math.log2(math.e)
    heads = q_ref.shape[1] // HD

    def step(q, key, value, mask):
        s = lax.dot_general(q, key, (((1,), (1,)), ((), ())), preferred_element_type=jnp.float32)
        if mask is not None:
            s = jnp.where(mask, s, NEG_MASK)
        old = m_ref[...]
        new = jnp.maximum(old, jnp.max(s, axis=1, keepdims=True))
        shrink = jnp.exp2((old - new) * factor)
        m_ref[...] = new
        p = jnp.exp2((s - new[:, :1]) * factor)
        folded = p[:, :HD]
        for part in range(1, KB // HD):
            folded = folded + p[:, part * HD : (part + 1) * HD]
        l_ref[...] = l_ref[...] * shrink + folded
        acc_ref[...] = acc_ref[...] * shrink + jnp.dot(
            p.astype(jnp.bfloat16), value, preferred_element_type=jnp.float32
        )

    shape = (heads * TQ, KB)
    lane = lax.broadcasted_iota(jnp.int32, shape, 1)
    row = lax.rem(lax.broadcasted_iota(jnp.int32, shape, 0), TQ)
    end = 0
    for request in range(REQ_REP):
        start, prefix = end, pref_ref[request]
        end = start + lens_ref[0, request]
        base = request * PREF_MAX
        copies[request].wait()

        def tile_body(tile, _):
            first = pl.multiple_of(tile * TQ, TQ)
            rows = pl.ds(first, TQ)
            q = jnp.concatenate([q_ref[rows, h * HD : (h + 1) * HD] for h in range(heads)], axis=0)
            m_ref[...] = jnp.full_like(m_ref, NEG_START)
            l_ref[...] = jnp.zeros_like(l_ref)
            acc_ref[...] = jnp.zeros_like(acc_ref)

            def full_block(block, _):
                at = pl.ds(base + pl.multiple_of(block * KB, KB), KB)
                step(q, stored[at, :HD], stored[at, HD:], None)
                return 0

            whole = prefix // KB
            lax.fori_loop(0, whole, full_block, 0)

            @pl.when(whole * KB < prefix)
            def _():
                at = pl.ds(base + pl.multiple_of(whole * KB, KB), KB)
                step(q, stored[at, :HD], stored[at, HD:], lane + whole * KB < prefix)

            def own_block(block, _):
                at = pl.ds(pl.multiple_of(block * KB, KB), KB)
                key_id = lane + block * KB
                step(q, k_ref[at, :], v_ref[at, :], (key_id >= start) & (key_id <= row + first))
                return 0

            def clear_block(block, _):
                at = pl.ds(pl.multiple_of(block * KB, KB), KB)
                step(q, k_ref[at, :], v_ref[at, :], None)
                return 0

            low = start // KB
            high = first // KB
            lax.fori_loop(low, jnp.minimum(low + 1, high), own_block, 0)
            lax.fori_loop(low + 1, high, clear_block, 0)
            own_block(high, 0)
            total = jnp.sum(l_ref[...], axis=1, keepdims=True)
            result = (acc_ref[...] / total).astype(o_ref.dtype)
            tok = first + lax.broadcasted_iota(jnp.int32, (TQ, HD), 0)
            own = (tok >= start) & (tok < end)
            for h in range(heads):
                at = slice(h * HD, (h + 1) * HD)
                o_ref[rows, at] = jnp.where(
                    own, result[h * TQ : (h + 1) * TQ].astype(jnp.float32), o_ref[rows, at].astype(jnp.float32)
                ).astype(o_ref.dtype)
            return 0

        lax.fori_loop(start // TQ, (end - 1) // TQ + 1, tile_body, 0)


def attend(lengths, prefix, q, k, v, cache):
    rows, width = q.shape
    heads = width // HD
    return pl.pallas_call(
        attention_kernel,
        out_shape=jax.ShapeDtypeStruct((rows, width), jnp.bfloat16),
        in_specs=[
            smem(),
            smem(),
            vmem(),
            vmem(),
            vmem(),
            anywhere(),
        ],
        out_specs=vmem(),
        scratch_shapes=[
            pltpu.VMEM((REQ_REP * PREF_MAX, 2 * HD), jnp.bfloat16),
            pltpu.VMEM((heads * TQ, HD), jnp.float32),
            pltpu.VMEM((heads * TQ, HD), jnp.float32),
            pltpu.VMEM((heads * TQ, HD), jnp.float32),
            pltpu.SemaphoreType.DMA((REQ_REP,)),
        ],
        cost_estimate=pl.CostEstimate(flops=2 * 10**9, bytes_accessed=3 * 2**20, transcendentals=2 * 10**6),
        name="attention",
    )(lengths, prefix, q, k, v, cache)


def output_kernel(
    att_ref, hidden_ref, gain_ref, wo_ref,
    resid_ref, normed_ref,
    att, part_send, part_recv, own, hid, sums_mine, sums,
    hid_sem, ring_send, ring_recv, core_send, core_recv, part_sems, sum_send, sum_recv,
):
    rep, tp, x, z, zh, y, c = place()
    rows, width = hid.shape
    load = pltpu.make_async_copy(
        hidden_ref.at[:, pl.ds(pl.multiple_of(tp * width, width), width)], hid, hid_sem
    )
    load.start()
    barrier = pltpu.get_barrier_semaphore()
    for k in range(1, 16):
        signal(barrier, (rep, (tp + k) % 16))
    pl.semaphore_wait(barrier, 15)

    def at_y(to):
        return (rep, zh * 8 + (to % 4) * 2 + c)

    partner = (rep, tp + 1 - 2 * c)
    across = (rep, (tp + 8) % 16)
    size = rows // CHUNKS
    half = size // 2
    pending = []

    def send(src, dst, ssem, rsem, device):
        made = pltpu.make_async_remote_copy(
            src_ref=src, dst_ref=dst, send_sem=ssem, recv_sem=rsem, device_id=device, device_id_type=MESH
        )
        made.start()
        pending.append(made)

    def wait(ref, sem):
        pltpu.make_async_copy(ref, ref, sem).wait()

    def own_send(m):
        at = pl.ds(m * size, size)
        src = att_ref.at[at]
        send(src, att.at[0, 1, at], ring_send.at[0, m], ring_recv.at[0, m], at_y(y + 1))
        send(src, att.at[0, 2, at], ring_send.at[1, m], ring_recv.at[1, m], at_y(y + 3))
        send(src, att.at[1, 0, at], core_send.at[0, m], core_recv.at[0, m], partner)

    def ring_in(m):
        at = pl.ds(m * size, size)
        for side in range(2):
            ref = att.at[0, 1 + side, at]
            wait(ref, ring_recv.at[side, m])
            part = pl.ds(m * size + side * half, half)
            send(
                att.at[0, 1 + side, part], att.at[0, 3, part],
                ring_send.at[2 + side, m], ring_recv.at[2 + side, m], at_y(y + 1 + 2 * side),
            )
            send(ref, att.at[1, 1 + side, at], core_send.at[1 + side, m], core_recv.at[1 + side, m], partner)

    def far_in(m):
        for side in range(2):
            wait(att.at[0, 3, pl.ds(m * size + side * half, half)], ring_recv.at[2 + side, m])
        ref = att.at[0, 3, pl.ds(m * size, size)]
        send(ref, att.at[1, 3, pl.ds(m * size, size)], core_send.at[3, m], core_recv.at[3, m], partner)

    def compute(m):
        at = pl.ds(m * size, size)
        for d in range(4):
            wait(att.at[1, d, at], core_recv.at[d, m])
        for mine in range(2):
            target = zh if mine else 1 - zh
            total = None
            for side in range(2):
                for d, dy in enumerate((0, 3, 1, 2)):
                    core = c if side == 0 else 1 - c
                    block = ((y + dy) % 4) * 4 + target * 2 + core
                    left = att_ref[at, :] if side == 0 and d == 0 else att[side, d, at, :]
                    part = jnp.dot(left, wo_ref[block], preferred_element_type=jnp.float32)
                    total = part if total is None else total + part
            if mine:
                own[at, :] = total
            else:
                part_send[at, :] = total.astype(jnp.bfloat16)
        send(part_send.at[at], part_recv.at[at], part_sems.at[0, m], part_sems.at[1, m], across)

    own_send(0)
    own_send(1)
    for i in range(CHUNKS + 2):
        if i < CHUNKS:
            ring_in(i)
        if i + 2 < CHUNKS:
            own_send(i + 2)
        if 1 <= i <= CHUNKS:
            far_in(i - 1)
        if i >= 2:
            compute(i - 2)
    load.wait()
    for m in range(CHUNKS):
        at = pl.ds(m * size, size)
        wait(part_recv.at[at], part_sems.at[1, m])
        for i in range(size // HD):
            row = m * (size // HD) + i
            here = pl.ds(row * HD, HD)
            resid = (
                hid[here, :].astype(jnp.float32) + (own[here, :] + part_recv[here, :].astype(jnp.float32))
            ).astype(jnp.bfloat16)
            resid_ref[here, :] = resid
            wide = resid.astype(jnp.float32)
            total = jnp.sum(wide * wide, axis=1, keepdims=True)
            sums_mine[pl.ds(row, 1), :] = jnp.transpose(jnp.broadcast_to(total, (HD, HD)))[:1, :]
    for k in range(1, 16):
        send(sums_mine, sums.at[k], sum_send.at[k], sum_recv.at[k], (rep, (tp + k) % 16))
    total = sums_mine[...]
    for k in range(1, 16):
        wait(sums.at[k], sum_recv.at[k])
        total = total + sums[k]
    inverse = lax.rsqrt(total * (1.0 / D) + norm_eps)
    gain = gain_ref[:, pl.ds(pl.multiple_of(tp * width, width), width)].astype(jnp.float32)
    for row in range(rows // HD):
        here = pl.ds(row * HD, HD)
        column = jnp.transpose(jnp.broadcast_to(inverse[row : row + 1, :], (HD, HD)))
        for h in range(width // HD):
            cols = slice(h * HD, (h + 1) * HD)
            normed_ref[here, cols] = (
                resid_ref[here, cols].astype(jnp.float32) * column * gain[:, cols]
            ).astype(jnp.bfloat16)
    for made in pending:
        made.wait_send()


def finish(attended, hidden, out_gain, wo_blocks):
    rows, width = attended.shape
    bf16, f32, dma = jnp.bfloat16, jnp.float32, pltpu.SemaphoreType.DMA
    return pl.pallas_call(
        output_kernel,
        out_shape=(jax.ShapeDtypeStruct((rows, width), bf16), jax.ShapeDtypeStruct((rows, width), bf16)),
        in_specs=[vmem(), anywhere(), vmem(), vmem()],
        out_specs=(vmem(), vmem()),
        scratch_shapes=[
            pltpu.VMEM((2, 4, rows, width), bf16),
            pltpu.VMEM((rows, width), bf16),
            pltpu.VMEM((rows, width), bf16),
            pltpu.VMEM((rows, width), f32),
            pltpu.VMEM((rows, width), bf16),
            pltpu.VMEM((rows // HD, HD), f32),
            pltpu.VMEM((16, rows // HD, HD), f32),
            dma,
            dma((4, CHUNKS)),
            dma((4, CHUNKS)),
            dma((4, CHUNKS)),
            dma((4, CHUNKS)),
            dma((2, CHUNKS)),
            dma((16,)),
            dma((16,)),
        ],
        compiler_params=pltpu.CompilerParams(collective_id=1, has_side_effects=True, vmem_limit_bytes=40 * 2**20),
        cost_estimate=pl.CostEstimate(flops=2 * 10**9, bytes_accessed=6 * 2**20, transcendentals=10**4),
        name="finish",
    )(attended, hidden, out_gain, wo_blocks)


def body(hidden, norm_gain, w_query, w_keyval, w_output, cache, lengths, prefix, out_gain):
    half = HD // 2
    freqs = rope_base ** (-(jnp.arange(half, dtype=jnp.float32) * 2.0 / HD))
    freqs = jnp.concatenate([freqs, freqs]).reshape(1, HD)
    q, k, v, wo_blocks = project(
        lengths, prefix, hidden, norm_gain.reshape(1, -1), freqs, w_query, w_keyval, w_output
    )
    attended = attend(lengths, prefix, q, k, v, cache)
    return finish(attended, hidden, out_gain.reshape(1, -1), wo_blocks)


def solution(mesh):
    placed = (
        P("rep", None),
        P(),
        P("rep", "tp"),
        P("rep", "tp"),
        P("tp", "rep"),
        P("rep", None),
        P("rep", None),
        P("rep"),
        P(),
    )
    return jax.shard_map(
        body,
        mesh=mesh,
        in_specs=placed,
        out_specs=(P("rep", "tp"), P("rep", "tp")),
        check_vma=False,
    )
```

```python
import functools
import math

import jax
import jax.numpy as jnp
import numpy as np
from jax import lax
from jax.experimental import pallas as pl
from jax.experimental.pallas import tpu as pltpu
from jax.sharding import PartitionSpec as P

H = 32
KV = 4
HD = 128
REQ_REP = 4
PREF_MAX = 512

norm_eps = 1e-05
rope_base = 5000000.0
TQ = 256
NEG_MASK = -1e30
VMEM_ALL = 67043328
CHUNKS = 4


MESH = pl.DeviceIdType.MESH
D = 4096
BLK = 256


def place():
    rep, tp = lax.axis_index("rep"), lax.axis_index("tp")
    return rep, tp, rep // 4, rep % 4, tp // 8, (tp // 2) % 4, tp % 2


def line_order(z):
    power = 1 + 3 * z + 9 * (z * (z - 1) // 2) + 27 * (z * (z - 1) * (z - 2) // 6)
    tables = []
    for picks in ((1, 0, 1, 2), (2, 2, 3, 1), (3, 3, 0, 0)):
        tables.append(sum(pick * 4**i for i, pick in enumerate(picks)))
    return [z] + [(table // power) % 4 for table in tables]


def signal(sem, device):
    pl.semaphore_signal(sem, inc=1, device_id=device, device_id_type=MESH)


class Gather:
    def __init__(self, own, full, recv, send, half):
        self.own, self.full, self.recv, self.send, self.half = own, full, recv, send, half
        self.rep, self.tp, self.x, self.z = place()[:4]
        self.order = line_order(self.z)
        self.right = ((self.x + 1) % 4) * 4
        self.left = ((self.x + 3) % 4) * 4
        self.far = ((self.x + 2) % 4) * 4
        self.pending = []

    def copy(self, src, dst, slot, sem, rep, cond=None):
        made = pltpu.make_async_remote_copy(
            src_ref=src,
            dst_ref=dst,
            send_sem=self.send.at[slot],
            recv_sem=sem,
            device_id=(rep, self.tp),
            device_id_type=MESH,
        )
        if cond is None:
            made.start()
        else:
            pl.when(cond)(made.start)
        self.pending.append((made, cond))

    def arrived(self, index, block):
        ref = self.full.at[block]
        pltpu.make_async_copy(ref, ref, self.recv.at[index, block]).wait()

    def line(self, k):
        zo = self.order[k]
        block = self.x * 4 + zo
        dst, sem = self.full.at[block], self.recv.at[0, block]
        if k == 0:
            src = self.own
            onward, back = self.z < 3, self.z > 0
        else:
            self.arrived(0, block)
            src = dst
            onward, back = (zo < self.z) & (self.z < 3), (zo > self.z) & (self.z > 0)
        self.copy(src, dst, 6 * k, sem, self.x * 4 + lax.min(self.z + 1, 3), onward)
        self.copy(src, dst, 6 * k + 1, sem, self.x * 4 + lax.max(self.z - 1, 0), back)
        self.copy(src, dst, 6 * k + 2, sem, self.right + self.z)
        self.copy(src, dst, 6 * k + 3, sem, self.left + self.z)

    def ring(self, k, side):
        zo = self.order[k]
        block = (self.left if side == 0 else self.right) + zo
        self.arrived(0, block)
        part = pl.ds(0, self.half) if side == 0 else pl.ds(self.half, self.half)
        ref = self.full.at[block, part]
        target = (self.right if side == 0 else self.left) + self.z
        self.copy(ref, ref, 6 * k + 4 + side, self.recv.at[side, block], target)
        return block

    def opposite(self, k):
        block = self.far + self.order[k]
        for side in range(2):
            ref = self.full.at[block, pl.ds(side * self.half, self.half)]
            pltpu.make_async_copy(ref, ref, self.recv.at[side, block]).wait()
        return block

    def drain(self):
        for made, cond in self.pending:
            if cond is None:
                made.wait_send()
            else:
                pl.when(cond)(made.wait_send)


def project_kernel(
    lens_ref, pref_ref, hidden_ref, gain_ref, freq_ref, wq_ref, wkv_ref, wo_ref,
    q_out, k_out, v_out, wo_out,
    gain, q_ref, k_ref, v_ref, hid, x3, full_q, full_s, turned, qacc, kacc, cosine, sine, mine, other,
    hid_sem, recv_q, send_q, recv_s, send_s, kv_send, kv_recv, perm_send, perm_recv, swap_sem, out_sem, own_sem, store_sem,
):
    rep, tp, x, z, zh, y, c = place()
    rows = hid.shape[0]
    count = hid_sem.shape[0]
    chunk = rows // count
    loads = []
    for i in range(count):
        at = pl.ds(i * chunk, chunk)
        loads.append(pltpu.make_async_copy(hidden_ref.at[at], hid.at[at], hid_sem.at[i]))
        loads[-1].start()
    own_load = pltpu.make_async_copy(wq_ref, full_q.at[rep], own_sem)
    own_load.start()

    zh_t = x // 2
    perm_dst = (y * 4 + zh_t * 2 + c, zh * 8 + ((x % 2) * 2 + z // 2) * 2 + z % 2)
    perm_src = (((z // 2) * 2 + y // 2) * 4 + (y % 2) * 2 + c, zh * 8 + x * 2 + z % 2)
    perm_away = (perm_dst[0] != rep) | (perm_dst[1] != tp)
    barrier = pltpu.get_barrier_semaphore()
    line_right, line_left = x * 4 + lax.min(z + 1, 3), x * 4 + lax.max(z - 1, 0)

    pl.when(z < 3)(lambda: signal(barrier, (line_right, tp)))
    pl.when(z > 0)(lambda: signal(barrier, (line_left, tp)))
    signal(barrier, (((x + 1) % 4) * 4 + z, tp))
    signal(barrier, (((x + 3) % 4) * 4 + z, tp))
    signal(barrier, (rep, tp + 1 - 2 * c))
    pl.when(perm_away)(lambda: signal(barrier, perm_src))
    for j in range(8):
        source = c * 8 + j
        pl.when(source != tp)(lambda source=source: signal(barrier, (rep, source)))
    line_peers = (lax.min(z + 1, 3) - z) + (z - lax.max(z - 1, 0))
    pl.semaphore_wait(barrier, 10 + line_peers + perm_away.astype(jnp.int32) + (c + zh) % 2)

    stream_q = Gather(wq_ref, full_q, recv_q, send_q, BLK // 2)
    stream_s = Gather(full_s.at[rep], full_s, recv_s, send_s, full_s.shape[1] // 2)
    stream_q.line(0)

    wo_dst = full_s.at[perm_dst[0], pl.ds(HD, BLK)]
    permute = pltpu.make_async_remote_copy(
        src_ref=wo_ref, dst_ref=wo_dst, send_sem=perm_send, recv_sem=perm_recv,
        device_id=perm_dst, device_id_type=MESH,
    )
    stay = pltpu.make_async_copy(wo_ref, wo_dst, perm_recv)
    pl.when(perm_away)(permute.start)
    pl.when(jnp.logical_not(perm_away))(stay.start)

    shape = (4 * 16, 4 * 16)
    out_row, in_col = lax.broadcasted_iota(jnp.int32, shape, 0), lax.broadcasted_iota(jnp.int32, shape, 1)
    pick = ((out_row % 16) * KV + out_row // 16 == in_col).astype(jnp.float32).astype(jnp.bfloat16)
    turned[...] = lax.dot_general(
        pick, wkv_ref[...], (((1,), (0,)), ((), ())), preferred_element_type=jnp.float32
    ).astype(jnp.bfloat16)

    starts, first_token = [], 0
    for request in range(REQ_REP):
        starts.append(first_token)
        first_token = first_token + lens_ref[0, request]

    def angles(i, _):
        at = pl.ds(pl.multiple_of(i * 128, 128), 128)
        token = i * 128 + lax.broadcasted_iota(jnp.int32, (128, HD), 0)
        position = jnp.zeros((128, HD), jnp.int32)
        for request in range(REQ_REP):
            shift = pref_ref[request] - starts[request]
            position = jnp.where(token >= starts[request], token + shift, position)
        angle = position.astype(jnp.float32) * freq_ref[...]
        lane = lax.broadcasted_iota(jnp.int32, (128, HD), 1)
        cosine[at, :] = jnp.cos(angle)
        wave = jnp.sin(angle)
        sine[at, :] = jnp.where(lane < HD // 2, -wave, wave)
        return 0

    gain[...] = gain_ref[...].astype(jnp.float32).reshape(1, D)

    def norm(i):
        loads[i].wait()

        def some(j, _):
            at = pl.ds(pl.multiple_of(i * chunk + j * 16, 16), 16)
            wide = hid[at, :].astype(jnp.float32)
            meansq = jnp.sum(wide * wide, axis=1, keepdims=True) * (1.0 / D)
            scaled = wide * lax.rsqrt(meansq + norm_eps)
            for b in range(D // BLK):
                cols = slice(b * BLK, (b + 1) * BLK)
                x3[b, at, :] = (scaled[:, cols] * gain[:, cols]).astype(jnp.bfloat16)
            return 0

        lax.fori_loop(0, chunk // 16, some, 0)

    def piece(head, which):
        target = (head // 2) * 8 + (2 * (head % 2) + which) * 2 + zh
        from_ref = turned.at[pl.ds(head * 16, 16)]
        to_ref = full_s.at[rep, pl.ds(pl.multiple_of((tp % 8) * 16, 16), 16)]
        away = target != tp
        made = pltpu.make_async_remote_copy(
            src_ref=from_ref, dst_ref=to_ref, send_sem=kv_send.at[head * 2 + which], recv_sem=kv_recv.at[tp % 8],
            device_id=(rep, target), device_id_type=MESH,
        )
        here = pltpu.make_async_copy(from_ref, to_ref, kv_recv.at[tp % 8])
        pl.when(away)(made.start)
        pl.when(jnp.logical_not(away))(here.start)
        return made, away

    def use_q(block, own=False):
        for i in range(rows // BLK):
            at = pl.ds(i * BLK, BLK)
            part = jnp.dot(x3[block, at, :], full_q[block], preferred_element_type=jnp.float32)
            qacc[at, :] = part if own else qacc[at, :] + part

    def use_s(block, own=False):
        for i in range(rows // BLK):
            at = pl.ds(i * BLK, BLK)
            part = lax.dot_general(
                x3[block, at, :], full_s[block, :HD, :], (((1,), (1,)), ((), ())),
                preferred_element_type=jnp.float32,
            )
            kacc[at, :] = part if own else kacc[at, :] + part

    norm(0)
    pieces = [piece(head, which) for head in range(KV) for which in range(2)]
    lax.fori_loop(0, rows // 128, angles, 0)
    norm(1)
    stream_q.line(1)
    norm(2)
    for j in range(8):
        ref = full_s.at[rep, pl.ds(j * 16, 16)]
        pltpu.make_async_copy(ref, ref, kv_recv.at[j]).wait()
    own_wo = full_s.at[rep, pl.ds(HD, BLK)]
    pltpu.make_async_copy(own_wo, own_wo, perm_recv).wait()
    stream_s.line(0)
    norm(3)
    stream_q.line(2)
    norm(4)
    stream_s.line(1)
    norm(5)
    stream_q.line(3)
    norm(6)
    stream_s.line(2)
    norm(7)
    stream_s.line(3)
    own_load.wait()
    use_q(rep, True)
    use_s(rep, True)
    for k in range(4):
        lefts, rights = stream_q.ring(k, 0), stream_q.ring(k, 1)
        lefts_s, rights_s = stream_s.ring(k, 0), stream_s.ring(k, 1)
        if k > 0:
            own_block = x * 4 + stream_q.order[k]
            use_q(own_block)
            use_s(own_block)
        for block in (lefts, rights):
            use_q(block)
        for block in (lefts_s, rights_s):
            use_s(block)
        if k > 0:
            use_q(stream_q.opposite(k - 1))
    use_q(stream_q.opposite(3))
    for k in range(4):
        use_s(stream_s.opposite(k))
    flush = pltpu.make_async_copy(full_s.at[:, pl.ds(HD, BLK)], wo_out, out_sem)
    flush.start()

    fresh = kacc[...].astype(jnp.bfloat16).astype(jnp.float32)
    turned_key = fresh * cosine[...] + pltpu.roll(fresh, HD // 2, 1) * sine[...]
    mine[...] = jnp.where(c == 0, turned_key, fresh).astype(jnp.bfloat16)
    swap = pltpu.make_async_remote_copy(
        src_ref=mine, dst_ref=other, send_sem=swap_sem.at[0], recv_sem=swap_sem.at[1],
        device_id=(rep, tp + 1 - 2 * c), device_id_type=MESH,
    )
    for h in range(q_ref.shape[1] // HD):
        cols = slice(h * HD, (h + 1) * HD)
        u = qacc[:, cols]
        q_ref[:, cols] = (u * cosine[...] + pltpu.roll(u, HD // 2, 1) * sine[...]).astype(jnp.bfloat16)
        if h == 0:
            swap.start()
    store_q = pltpu.make_async_copy(q_ref, q_out, store_sem.at[0])
    store_q.start()
    for made, away in pieces:
        pl.when(away)(made.wait_send)
    pl.when(perm_away)(permute.wait_send)
    stream_q.drain()
    stream_s.drain()
    swap.wait()

    @pl.when(c == 0)
    def _():
        k_ref[...] = mine[...]
        v_ref[...] = other[...]

    @pl.when(c != 0)
    def _():
        k_ref[...] = other[...]
        v_ref[...] = mine[...]

    store_k = pltpu.make_async_copy(k_ref, k_out, store_sem.at[1])
    store_v = pltpu.make_async_copy(v_ref, v_out, store_sem.at[2])
    store_k.start()
    store_v.start()
    store_q.wait()
    store_k.wait()
    store_v.wait()
    flush.wait()


def vmem():
    return pl.BlockSpec(memory_space=pltpu.VMEM)


def smem():
    return pl.BlockSpec(memory_space=pltpu.SMEM)


def anywhere():
    return pl.BlockSpec(memory_space=pl.ANY)


def project(lengths, prefix, hidden, norm_gain, freqs, w_query, w_keyval, w_output):
    rows = hidden.shape[0]
    bf16, f32, dma = jnp.bfloat16, jnp.float32, pltpu.SemaphoreType.DMA
    return pl.pallas_call(
        project_kernel,
        out_shape=(
            jax.ShapeDtypeStruct((rows, BLK), bf16),
            jax.ShapeDtypeStruct((rows, HD), bf16),
            jax.ShapeDtypeStruct((rows, HD), bf16),
            jax.ShapeDtypeStruct((16, BLK, BLK), bf16),
        ),
        in_specs=[smem(), smem(), anywhere(), vmem(), vmem(), anywhere(), vmem(), anywhere()],
        out_specs=(anywhere(), anywhere(), anywhere(), anywhere()),
        scratch_shapes=[
            pltpu.VMEM((1, D), f32),
            pltpu.VMEM((rows, BLK), bf16),
            pltpu.VMEM((rows, HD), bf16),
            pltpu.VMEM((rows, HD), bf16),
            pltpu.VMEM((rows, D), bf16),
            pltpu.VMEM((16, rows, BLK), bf16),
            pltpu.VMEM((16, BLK, BLK), bf16),
            pltpu.VMEM((16, HD + BLK, BLK), bf16),
            pltpu.VMEM((64, BLK), bf16),
            pltpu.VMEM((rows, BLK), f32),
            pltpu.VMEM((rows, HD), f32),
            pltpu.VMEM((rows, HD), f32),
            pltpu.VMEM((rows, HD), f32),
            pltpu.VMEM((rows, HD), bf16),
            pltpu.VMEM((rows, HD), bf16),
            dma((8,)),
            dma((2, 16)),
            dma((24,)),
            dma((2, 16)),
            dma((24,)),
            dma((8,)),
            dma((8,)),
            dma,
            dma,
            dma((2,)),
            dma,
            dma,
            dma((3,)),
        ],
        compiler_params=pltpu.CompilerParams(collective_id=0, has_side_effects=True, vmem_limit_bytes=VMEM_ALL),
        cost_estimate=pl.CostEstimate(flops=3 * 10**9, bytes_accessed=12 * 2**20, transcendentals=10**6),
        name="project",
    )(lengths, prefix, hidden, norm_gain, freqs, w_query, w_keyval, w_output)


def attention_kernel(
    lens_ref, pref_ref, q_ref, k_ref, v_ref, cache_ref, o_ref, qs, ks, vs, stored, outs, sems, out_sem
):
    rows, width = q_ref.shape
    column = pl.multiple_of(lax.axis_index("tp") // 4 * 2 * HD, 2 * HD)
    inside = pl.ds(0, rows)
    loads = [
        pltpu.make_async_copy(q_ref, qs.at[inside], sems.at[REQ_REP]),
        pltpu.make_async_copy(k_ref, ks.at[inside], sems.at[REQ_REP + 1]),
        pltpu.make_async_copy(v_ref, vs.at[inside], sems.at[REQ_REP + 2]),
    ]

    def fetch(request):
        at = pl.ds(pl.multiple_of(request * PREF_MAX, PREF_MAX), PREF_MAX)
        return pltpu.make_async_copy(cache_ref.at[at, pl.ds(column, 2 * HD)], stored.at[at, :], sems.at[request])

    fetch(0).start()
    for load in loads:
        load.start()
    for request in range(1, REQ_REP):
        fetch(request).start()
    spare = pl.ds(rows, qs.shape[0] - rows)
    ks[spare, :] = jnp.zeros((TQ, HD), jnp.bfloat16)
    vs[spare, :] = jnp.zeros((TQ, HD), jnp.bfloat16)
    for load in loads:
        load.wait()
    factor = HD ** (-0.5) * math.log2(math.e)
    nt = (((1,), (1,)), ((), ()))
    lane = lax.broadcasted_iota(jnp.int32, (TQ, TQ), 1)
    row = lax.broadcasted_iota(jnp.int32, (TQ, TQ), 0)

    def tile(start, aligned, base, prefix, index, parts):
        rows_at = pl.ds(pl.multiple_of(aligned + index * TQ, 16), TQ)
        for h in range(width // HD):
            cols = slice(h * HD, (h + 1) * HD)
            q = qs[rows_at, cols]
            scores, values = [], []
            for part in range(parts):
                at = pl.ds(pl.multiple_of(base + part * TQ, TQ), TQ)
                score = lax.dot_general(q, stored[at, :HD], nt, preferred_element_type=jnp.float32)
                if part == parts - 1:
                    score = jnp.where(lane < prefix - part * TQ, score, NEG_MASK)
                scores.append(score)
                values.append((stored, at, slice(HD, 2 * HD)))
            for part in range(index + 1):
                at = pl.ds(pl.multiple_of(aligned + part * TQ, 16), TQ)
                score = lax.dot_general(q, ks[at, :], nt, preferred_element_type=jnp.float32)
                if part == index:
                    score = jnp.where(lane <= row, score, NEG_MASK)
                if part == 0:
                    score = jnp.where(lane >= start - aligned, score, NEG_MASK)
                scores.append(score)
                values.append((vs, at, slice(0, HD)))
            peak = scores[0]
            for score in scores[1:]:
                peak = jnp.maximum(peak, score)
            peak = jnp.max(peak, axis=1, keepdims=True)
            total, gathered = None, None
            for score, (ref, at, which) in zip(scores, values):
                e = jnp.exp2((score - peak) * factor)
                total = e if total is None else total + e
                part = jnp.dot(e.astype(jnp.bfloat16), ref[at, which], preferred_element_type=jnp.float32)
                gathered = part if gathered is None else gathered + part
            result = gathered / jnp.sum(total, axis=1, keepdims=True)
            if index == 0:
                keep = row[:, :HD] + aligned < start
                result = jnp.where(keep, outs[rows_at, cols].astype(jnp.float32), result)
            outs[rows_at, cols] = result.astype(jnp.bfloat16)

    def one(request, start):
        end, prefix = start + lens_ref[0, request], pref_ref[request]
        aligned = start // 16 * 16
        base = request * PREF_MAX
        fetch(request).wait()
        for index in range(3):
            for parts in (1, 2):
                fits = (prefix <= TQ) if parts == 1 else (prefix > TQ)
                pl.when((aligned + index * TQ < end) & fits)(
                    functools.partial(tile, start, aligned, base, prefix, index, parts)
                )
        return end

    lax.fori_loop(0, REQ_REP, one, 0)
    store = pltpu.make_async_copy(outs.at[inside], o_ref, out_sem)
    store.start()
    store.wait()


def attend(lengths, prefix, q, k, v, cache):
    rows, width = q.shape
    bf16, dma = jnp.bfloat16, pltpu.SemaphoreType.DMA
    return pl.pallas_call(
        attention_kernel,
        out_shape=jax.ShapeDtypeStruct((rows, width), bf16),
        in_specs=[smem(), smem(), anywhere(), anywhere(), anywhere(), anywhere()],
        out_specs=anywhere(),
        scratch_shapes=[
            pltpu.VMEM((rows + TQ, width), bf16),
            pltpu.VMEM((rows + TQ, HD), bf16),
            pltpu.VMEM((rows + TQ, HD), bf16),
            pltpu.VMEM((REQ_REP * PREF_MAX, 2 * HD), bf16),
            pltpu.VMEM((rows + TQ, width), bf16),
            dma((REQ_REP + 3,)),
            dma,
        ],
        compiler_params=pltpu.CompilerParams(vmem_limit_bytes=VMEM_ALL),
        cost_estimate=pl.CostEstimate(flops=2 * 10**9, bytes_accessed=3 * 2**20, transcendentals=2 * 10**6),
        name="attention",
    )(lengths, prefix, q, k, v, cache)


def output_kernel(
    att_ref, hidden_ref, gain_ref, wo_in,
    resid_ref, normed_ref,
    gain_row, wo_ref, att, part_send, part_recv, own, hid, sums_mine, sums,
    hid_sem, ring_send, ring_recv, core_send, core_recv, part_sems, sum_send, sum_recv, wo_sem, own_sem,
):
    rep, tp, x, z, zh, y, c = place()
    rows, width = hid.shape
    load = pltpu.make_async_copy(
        hidden_ref.at[:, pl.ds(pl.multiple_of(tp * width, width), width)], hid, hid_sem
    )
    load.start()
    load_wo = pltpu.make_async_copy(wo_in, wo_ref, wo_sem)
    load_wo.start()
    load_own = pltpu.make_async_copy(att_ref, att.at[0, 0], own_sem)
    load_own.start()
    gain_row[...] = gain_ref[...].astype(jnp.float32).reshape(1, D)
    barrier = pltpu.get_barrier_semaphore()
    for k in range(1, 16):
        signal(barrier, (rep, (tp + k) % 16))
    pl.semaphore_wait(barrier, 15)

    def at_y(to):
        return (rep, zh * 8 + (to % 4) * 2 + c)

    partner = (rep, tp + 1 - 2 * c)
    across = (rep, (tp + 8) % 16)
    size = rows // CHUNKS
    half = size // 2
    pending = []

    def send(src, dst, ssem, rsem, device):
        made = pltpu.make_async_remote_copy(
            src_ref=src, dst_ref=dst, send_sem=ssem, recv_sem=rsem, device_id=device, device_id_type=MESH
        )
        made.start()
        pending.append(made)

    def wait(ref, sem):
        pltpu.make_async_copy(ref, ref, sem).wait()

    def own_send(m):
        at = pl.ds(m * size, size)
        src = att_ref.at[at]
        send(src, att.at[0, 1, at], ring_send.at[0, m], ring_recv.at[0, m], at_y(y + 1))
        send(src, att.at[0, 2, at], ring_send.at[1, m], ring_recv.at[1, m], at_y(y + 3))
        send(src, att.at[1, 0, at], core_send.at[0, m], core_recv.at[0, m], partner)

    def ring_in(m):
        at = pl.ds(m * size, size)
        for side in range(2):
            ref = att.at[0, 1 + side, at]
            wait(ref, ring_recv.at[side, m])
            part = pl.ds(m * size + side * half, half)
            send(
                att.at[0, 1 + side, part], att.at[0, 3, part],
                ring_send.at[2 + side, m], ring_recv.at[2 + side, m], at_y(y + 1 + 2 * side),
            )
            send(ref, att.at[1, 1 + side, at], core_send.at[1 + side, m], core_recv.at[1 + side, m], partner)

    def far_in(m):
        for side in range(2):
            wait(att.at[0, 3, pl.ds(m * size + side * half, half)], ring_recv.at[2 + side, m])
        ref = att.at[0, 3, pl.ds(m * size, size)]
        send(ref, att.at[1, 3, pl.ds(m * size, size)], core_send.at[3, m], core_recv.at[3, m], partner)

    def compute(m):
        at = pl.ds(m * size, size)
        for d in range(4):
            wait(att.at[1, d, at], core_recv.at[d, m])
        for mine in range(2):
            target = zh if mine else 1 - zh
            total = None
            for side in range(2):
                for d, dy in enumerate((0, 3, 1, 2)):
                    core = c if side == 0 else 1 - c
                    block = ((y + dy) % 4) * 4 + target * 2 + core
                    left = att[side, d, at, :]
                    part = jnp.dot(left, wo_ref[block], preferred_element_type=jnp.float32)
                    total = part if total is None else total + part
            if mine:
                own[at, :] = total
            else:
                part_send[at, :] = total.astype(jnp.bfloat16)
        send(part_send.at[at], part_recv.at[at], part_sems.at[0, m], part_sems.at[1, m], across)

    own_send(0)
    own_send(1)
    load_wo.wait()
    load_own.wait()
    for i in range(CHUNKS + 2):
        if i < CHUNKS:
            ring_in(i)
        if i + 2 < CHUNKS:
            own_send(i + 2)
        if 1 <= i <= CHUNKS:
            far_in(i - 1)
        if i >= 2:
            compute(i - 2)
    load.wait()
    for m in range(CHUNKS):
        at = pl.ds(m * size, size)
        wait(part_recv.at[at], part_sems.at[1, m])
        for i in range(size // HD):
            row = m * (size // HD) + i
            here = pl.ds(row * HD, HD)
            resid = (
                hid[here, :].astype(jnp.float32) + (own[here, :] + part_recv[here, :].astype(jnp.float32))
            ).astype(jnp.bfloat16)
            resid_ref[here, :] = resid
            wide = resid.astype(jnp.float32)
            total = jnp.sum(wide * wide, axis=1, keepdims=True)
            sums_mine[pl.ds(row, 1), :] = jnp.transpose(jnp.broadcast_to(total, (HD, HD)))[:1, :]
    for k in range(1, 16):
        send(sums_mine, sums.at[k], sum_send.at[k], sum_recv.at[k], (rep, (tp + k) % 16))
    total = sums_mine[...]
    for k in range(1, 16):
        wait(sums.at[k], sum_recv.at[k])
        total = total + sums[k]
    inverse = lax.rsqrt(total * (1.0 / D) + norm_eps)
    gain = gain_row[:, pl.ds(pl.multiple_of(tp * width, width), width)]
    for row in range(rows // HD):
        here = pl.ds(row * HD, HD)
        column = jnp.transpose(jnp.broadcast_to(inverse[row : row + 1, :], (HD, HD)))
        for h in range(width // HD):
            cols = slice(h * HD, (h + 1) * HD)
            normed_ref[here, cols] = (
                resid_ref[here, cols].astype(jnp.float32) * column * gain[:, cols]
            ).astype(jnp.bfloat16)
    for made in pending:
        made.wait_send()


def finish(attended, hidden, out_gain, wo_blocks):
    rows, width = attended.shape
    bf16, f32, dma = jnp.bfloat16, jnp.float32, pltpu.SemaphoreType.DMA
    return pl.pallas_call(
        output_kernel,
        out_shape=(jax.ShapeDtypeStruct((rows, width), bf16), jax.ShapeDtypeStruct((rows, width), bf16)),
        in_specs=[anywhere(), anywhere(), vmem(), anywhere()],
        out_specs=(vmem(), vmem()),
        scratch_shapes=[
            pltpu.VMEM((1, D), f32),
            pltpu.VMEM((16, BLK, BLK), bf16),
            pltpu.VMEM((2, 4, rows, width), bf16),
            pltpu.VMEM((rows, width), bf16),
            pltpu.VMEM((rows, width), bf16),
            pltpu.VMEM((rows, width), f32),
            pltpu.VMEM((rows, width), bf16),
            pltpu.VMEM((rows // HD, HD), f32),
            pltpu.VMEM((16, rows // HD, HD), f32),
            dma,
            dma((4, CHUNKS)),
            dma((4, CHUNKS)),
            dma((4, CHUNKS)),
            dma((4, CHUNKS)),
            dma((2, CHUNKS)),
            dma((16,)),
            dma((16,)),
            dma,
            dma,
        ],
        compiler_params=pltpu.CompilerParams(collective_id=1, has_side_effects=True, vmem_limit_bytes=VMEM_ALL),
        cost_estimate=pl.CostEstimate(flops=2 * 10**9, bytes_accessed=6 * 2**20, transcendentals=10**4),
        name="finish",
    )(attended, hidden, out_gain, wo_blocks)


def body(hidden, norm_gain, w_query, w_keyval, w_output, cache, lengths, prefix, out_gain):
    powers = np.arange(HD) % (HD // 2) * 2.0 / HD
    freqs = jnp.asarray((rope_base**-powers).astype(np.float32).reshape(1, HD))
    q, k, v, wo_blocks = project(lengths, prefix, hidden, norm_gain, freqs, w_query, w_keyval.T, w_output)
    attended = attend(lengths, prefix, q, k, v, cache)
    return finish(attended, hidden, out_gain, wo_blocks)


def solution(mesh):
    placed = (
        P("rep", None),
        P(),
        P("rep", "tp"),
        P("rep", "tp"),
        P("tp", "rep"),
        P("rep", None),
        P("rep", None),
        P("rep"),
        P(),
    )
    return jax.shard_map(
        body,
        mesh=mesh,
        in_specs=placed,
        out_specs=(P("rep", "tp"), P("rep", "tp")),
        check_vma=False,
    )
```

```python
import functools
import math

import jax
import jax.numpy as jnp
import numpy as np
from jax import lax
from jax.experimental import pallas as pl
from jax.experimental.pallas import tpu as pltpu
from jax.sharding import PartitionSpec as P

H = 32
KV = 4
HD = 128
REQ_REP = 4
PREF_MAX = 512

norm_eps = 1e-05
rope_base = 5000000.0
TQ = 256
NEG_MASK = -1e30
VMEM_ALL = 67043328
CHUNKS = 8
WEIGHT_AT = 3
OWN_EARLY = 3


MESH = pl.DeviceIdType.MESH
D = 4096
BLK = 256


def place():
    rep, tp = lax.axis_index("rep"), lax.axis_index("tp")
    return rep, tp, rep // 4, rep % 4, tp // 8, (tp // 2) % 4, tp % 2


def line_order(z):
    power = 1 + 3 * z + 9 * (z * (z - 1) // 2) + 27 * (z * (z - 1) * (z - 2) // 6)
    tables = []
    for picks in ((1, 0, 1, 2), (2, 2, 3, 1), (3, 3, 0, 0)):
        tables.append(sum(pick * 4**i for i, pick in enumerate(picks)))
    return [z] + [(table // power) % 4 for table in tables]


def signal(sem, device):
    pl.semaphore_signal(sem, inc=1, device_id=device, device_id_type=MESH)


class Gather:
    def __init__(self, own, full, recv, send, half, ring=True):
        self.own, self.full, self.recv, self.send, self.half = own, full, recv, send, half
        self.in_ring = ring
        self.rep, self.tp, self.x, self.z = place()[:4]
        self.order = line_order(self.z)
        self.right = ((self.x + 1) % 4) * 4
        self.left = ((self.x + 3) % 4) * 4
        self.far = ((self.x + 2) % 4) * 4
        self.pending = []

    def copy(self, src, dst, slot, sem, rep, cond=None):
        made = pltpu.make_async_remote_copy(
            src_ref=src,
            dst_ref=dst,
            send_sem=self.send.at[slot],
            recv_sem=sem,
            device_id=(rep, self.tp),
            device_id_type=MESH,
        )
        if cond is None:
            made.start()
        else:
            pl.when(cond)(made.start)
        self.pending.append((made, cond))

    def arrived(self, index, block):
        ref = self.full.at[block]
        pltpu.make_async_copy(ref, ref, self.recv.at[index, block]).wait()

    def line(self, k):
        zo = self.order[k]
        block = self.x * 4 + zo if self.in_ring else zo
        dst, sem = self.full.at[block], self.recv.at[0, block]
        if k == 0:
            src = self.own
            onward, back = self.z < 3, self.z > 0
        else:
            self.arrived(0, block)
            src = dst
            onward, back = (zo < self.z) & (self.z < 3), (zo > self.z) & (self.z > 0)
        self.copy(src, dst, 6 * k, sem, self.x * 4 + lax.min(self.z + 1, 3), onward)
        self.copy(src, dst, 6 * k + 1, sem, self.x * 4 + lax.max(self.z - 1, 0), back)
        if not self.in_ring:
            return
        self.copy(src, dst, 6 * k + 2, sem, self.right + self.z)
        self.copy(src, dst, 6 * k + 3, sem, self.left + self.z)

    def ring(self, k, side):
        zo = self.order[k]
        block = (self.left if side == 0 else self.right) + zo
        self.arrived(0, block)
        part = pl.ds(0, self.half) if side == 0 else pl.ds(self.half, self.half)
        ref = self.full.at[block, part]
        target = (self.right if side == 0 else self.left) + self.z
        self.copy(ref, ref, 6 * k + 4 + side, self.recv.at[side, block], target)
        return block

    def opposite(self, k):
        block = self.far + self.order[k]
        for side in range(2):
            ref = self.full.at[block, pl.ds(side * self.half, self.half)]
            pltpu.make_async_copy(ref, ref, self.recv.at[side, block]).wait()
        return block

    def drain(self):
        for made, cond in self.pending:
            if cond is None:
                made.wait_send()
            else:
                pl.when(cond)(made.wait_send)


def project_kernel(
    lens_ref, pref_ref, hidden_ref, gain_ref, freq_ref, wq_ref, wkv_ref, wo_ref,
    q_out, k_out, v_out, wo_out,
    gain, q_ref, k_ref, v_ref, hid, x3, full_q, full_s, full_w, turned, qacc, kacc, cosine, sine, mine, other,
    hid_sem, recv_q, send_q, recv_s, send_s, recv_w, send_w, kv_send, kv_recv, perm_send, perm_recv, swap_sem, out_sem, own_sem, store_sem,
):
    rep, tp, x, z, zh, y, c = place()
    rows = hid.shape[0]
    count = hid_sem.shape[0]
    chunk = rows // count
    loads = []
    for i in range(count):
        at = pl.ds(i * chunk, chunk)
        loads.append(pltpu.make_async_copy(hidden_ref.at[at], hid.at[at], hid_sem.at[i]))
        loads[-1].start()
    own_load = pltpu.make_async_copy(wq_ref, full_q.at[rep], own_sem)
    own_load.start()

    zh_t = x // 2
    perm_dst = (y * 4 + zh_t * 2 + c, zh * 8 + ((x % 2) * 2 + z // 2) * 2 + z % 2)
    perm_src = (((z // 2) * 2 + y // 2) * 4 + (y % 2) * 2 + c, zh * 8 + x * 2 + z % 2)
    perm_away = (perm_dst[0] != rep) | (perm_dst[1] != tp)
    barrier = pltpu.get_barrier_semaphore()
    line_right, line_left = x * 4 + lax.min(z + 1, 3), x * 4 + lax.max(z - 1, 0)

    pl.when(z < 3)(lambda: signal(barrier, (line_right, tp)))
    pl.when(z > 0)(lambda: signal(barrier, (line_left, tp)))
    signal(barrier, (((x + 1) % 4) * 4 + z, tp))
    signal(barrier, (((x + 3) % 4) * 4 + z, tp))
    signal(barrier, (rep, tp + 1 - 2 * c))
    pl.when(perm_away)(lambda: signal(barrier, perm_src))
    for j in range(8):
        source = c * 8 + j
        pl.when(source != tp)(lambda source=source: signal(barrier, (rep, source)))
    shape = (4 * 16, 4 * 16)
    out_row, in_col = lax.broadcasted_iota(jnp.int32, shape, 0), lax.broadcasted_iota(jnp.int32, shape, 1)
    pick = ((out_row % 16) * KV + out_row // 16 == in_col).astype(jnp.float32).astype(jnp.bfloat16)
    turned[...] = lax.dot_general(
        pick, wkv_ref[...], (((1,), (0,)), ((), ())), preferred_element_type=jnp.float32
    ).astype(jnp.bfloat16)

    starts, first_token = [], 0
    for request in range(REQ_REP):
        starts.append(first_token)
        first_token = first_token + lens_ref[0, request]

    def angles(i, _):
        at = pl.ds(pl.multiple_of(i * 128, 128), 128)
        token = i * 128 + lax.broadcasted_iota(jnp.int32, (128, HD), 0)
        position = jnp.zeros((128, HD), jnp.int32)
        for request in range(REQ_REP):
            shift = pref_ref[request] - starts[request]
            position = jnp.where(token >= starts[request], token + shift, position)
        angle = position.astype(jnp.float32) * freq_ref[...]
        lane = lax.broadcasted_iota(jnp.int32, (128, HD), 1)
        cosine[at, :] = jnp.cos(angle)
        wave = jnp.sin(angle)
        sine[at, :] = jnp.where(lane < HD // 2, -wave, wave)
        return 0

    lax.fori_loop(0, rows // 128, angles, 0)
    gain[...] = gain_ref[...].astype(jnp.float32).reshape(1, D)

    line_peers = (lax.min(z + 1, 3) - z) + (z - lax.max(z - 1, 0))
    pl.semaphore_wait(barrier, 10 + line_peers + perm_away.astype(jnp.int32) + (c + zh) % 2)

    stream_q = Gather(wq_ref, full_q, recv_q, send_q, BLK // 2)
    stream_s = Gather(full_s.at[rep], full_s, recv_s, send_s, full_s.shape[1] // 2)
    stream_w = Gather(full_w.at[z], full_w, recv_w, send_w, 0, False)
    stream_q.line(0)

    def piece(head, which):
        target = (head // 2) * 8 + (2 * (head % 2) + which) * 2 + zh
        from_ref = turned.at[pl.ds(head * 16, 16)]
        to_ref = full_s.at[rep, pl.ds(pl.multiple_of((tp % 8) * 16, 16), 16)]
        away = target != tp
        made = pltpu.make_async_remote_copy(
            src_ref=from_ref, dst_ref=to_ref, send_sem=kv_send.at[head * 2 + which], recv_sem=kv_recv.at[tp % 8],
            device_id=(rep, target), device_id_type=MESH,
        )
        here = pltpu.make_async_copy(from_ref, to_ref, kv_recv.at[tp % 8])
        pl.when(away)(made.start)
        pl.when(jnp.logical_not(away))(here.start)
        return made, away

    pieces = [piece(head, which) for head in range(KV) for which in range(2)]

    wo_dst = full_w.at[perm_dst[0] % 4]
    permute = pltpu.make_async_remote_copy(
        src_ref=wo_ref, dst_ref=wo_dst, send_sem=perm_send, recv_sem=perm_recv,
        device_id=perm_dst, device_id_type=MESH,
    )
    stay = pltpu.make_async_copy(wo_ref, wo_dst, perm_recv)
    pl.when(perm_away)(permute.start)
    pl.when(jnp.logical_not(perm_away))(stay.start)

    def norm(i):
        loads[i].wait()

        def some(j, _):
            at = pl.ds(pl.multiple_of(i * chunk + j * 16, 16), 16)
            wide = hid[at, :].astype(jnp.float32)
            meansq = jnp.sum(wide * wide, axis=1, keepdims=True) * (1.0 / D)
            scaled = wide * lax.rsqrt(meansq + norm_eps)
            for b in range(D // BLK):
                cols = slice(b * BLK, (b + 1) * BLK)
                x3[b, at, :] = (scaled[:, cols] * gain[:, cols]).astype(jnp.bfloat16)
            return 0

        lax.fori_loop(0, chunk // 16, some, 0)

    def use_q(block, own=False):
        for i in range(rows // BLK):
            at = pl.ds(i * BLK, BLK)
            part = jnp.dot(x3[block, at, :], full_q[block], preferred_element_type=jnp.float32)
            qacc[at, :] = part if own else qacc[at, :] + part

    def use_s(block, own=False):
        for i in range(rows // BLK):
            at = pl.ds(i * BLK, BLK)
            part = lax.dot_general(
                x3[block, at, :], full_s[block, :HD, :], (((1,), (1,)), ((), ())),
                preferred_element_type=jnp.float32,
            )
            kacc[at, :] = part if own else kacc[at, :] + part

    norm(0)
    norm(1)
    stream_q.line(1)
    for j in range(8):
        ref = full_s.at[rep, pl.ds(j * 16, 16)]
        pltpu.make_async_copy(ref, ref, kv_recv.at[j]).wait()
    stream_s.line(0)
    norm(2)
    norm(3)
    stream_s.line(1)
    norm(4)
    stream_q.line(2)
    norm(5)
    stream_s.line(2)
    norm(6)
    stream_q.line(3)
    norm(7)
    stream_s.line(3)
    own_load.wait()
    use_q(rep, True)
    use_s(rep, True)
    for k in range(4):
        lefts, rights = stream_q.ring(k, 0), stream_q.ring(k, 1)
        lefts_s, rights_s = stream_s.ring(k, 0), stream_s.ring(k, 1)
        if k == 0:
            own_wo = full_w.at[z]
            pltpu.make_async_copy(own_wo, own_wo, perm_recv).wait()
        stream_w.line(k)
        if k > 0:
            own_block = x * 4 + stream_q.order[k]
            use_q(own_block)
            use_s(own_block)
        for block in (lefts, rights):
            use_q(block)
        for block in (lefts_s, rights_s):
            use_s(block)
        if k > 0:
            use_q(stream_q.opposite(k - 1))
            use_s(stream_s.opposite(k - 1))
    flush = pltpu.make_async_copy(full_w, wo_out, out_sem)
    flush.start()
    use_s(stream_s.opposite(3))

    fresh = kacc[...].astype(jnp.bfloat16).astype(jnp.float32)
    turned_key = fresh * cosine[...] + pltpu.roll(fresh, HD // 2, 1) * sine[...]
    mine[...] = jnp.where(c == 0, turned_key, fresh).astype(jnp.bfloat16)
    swap = pltpu.make_async_remote_copy(
        src_ref=mine, dst_ref=other, send_sem=swap_sem.at[0], recv_sem=swap_sem.at[1],
        device_id=(rep, tp + 1 - 2 * c), device_id_type=MESH,
    )
    use_q(stream_q.opposite(3))
    swap.start()
    for h in range(q_ref.shape[1] // HD):
        cols = slice(h * HD, (h + 1) * HD)
        u = qacc[:, cols]
        q_ref[:, cols] = (u * cosine[...] + pltpu.roll(u, HD // 2, 1) * sine[...]).astype(jnp.bfloat16)
    store_q = pltpu.make_async_copy(q_ref, q_out, store_sem.at[0])
    store_q.start()
    for made, away in pieces:
        pl.when(away)(made.wait_send)
    pl.when(perm_away)(permute.wait_send)
    stream_q.drain()
    stream_s.drain()
    stream_w.drain()
    swap.wait()

    @pl.when(c == 0)
    def _():
        k_ref[...] = mine[...]
        v_ref[...] = other[...]

    @pl.when(c != 0)
    def _():
        k_ref[...] = other[...]
        v_ref[...] = mine[...]

    store_k = pltpu.make_async_copy(k_ref, k_out, store_sem.at[1])
    store_v = pltpu.make_async_copy(v_ref, v_out, store_sem.at[2])
    store_k.start()
    store_v.start()
    store_q.wait()
    store_k.wait()
    store_v.wait()
    flush.wait()


def vmem():
    return pl.BlockSpec(memory_space=pltpu.VMEM)


def smem():
    return pl.BlockSpec(memory_space=pltpu.SMEM)


def anywhere():
    return pl.BlockSpec(memory_space=pl.ANY)


def project(lengths, prefix, hidden, norm_gain, freqs, w_query, w_keyval, w_output):
    rows = hidden.shape[0]
    bf16, f32, dma = jnp.bfloat16, jnp.float32, pltpu.SemaphoreType.DMA
    return pl.pallas_call(
        project_kernel,
        out_shape=(
            jax.ShapeDtypeStruct((rows, BLK), bf16),
            jax.ShapeDtypeStruct((rows, HD), bf16),
            jax.ShapeDtypeStruct((rows, HD), bf16),
            jax.ShapeDtypeStruct((4, BLK, BLK), bf16),
        ),
        in_specs=[smem(), smem(), anywhere(), vmem(), vmem(), anywhere(), vmem(), anywhere()],
        out_specs=(anywhere(), anywhere(), anywhere(), anywhere()),
        scratch_shapes=[
            pltpu.VMEM((1, D), f32),
            pltpu.VMEM((rows, BLK), bf16),
            pltpu.VMEM((rows, HD), bf16),
            pltpu.VMEM((rows, HD), bf16),
            pltpu.VMEM((rows, D), bf16),
            pltpu.VMEM((16, rows, BLK), bf16),
            pltpu.VMEM((16, BLK, BLK), bf16),
            pltpu.VMEM((16, HD, BLK), bf16),
            pltpu.VMEM((4, BLK, BLK), bf16),
            pltpu.VMEM((64, BLK), bf16),
            pltpu.VMEM((rows, BLK), f32),
            pltpu.VMEM((rows, HD), f32),
            pltpu.VMEM((rows, HD), f32),
            pltpu.VMEM((rows, HD), f32),
            pltpu.VMEM((rows, HD), bf16),
            pltpu.VMEM((rows, HD), bf16),
            dma((8,)),
            dma((2, 16)),
            dma((24,)),
            dma((2, 16)),
            dma((24,)),
            dma((1, 4)),
            dma((24,)),
            dma((8,)),
            dma((8,)),
            dma,
            dma,
            dma((2,)),
            dma,
            dma,
            dma((3,)),
        ],
        compiler_params=pltpu.CompilerParams(collective_id=0, has_side_effects=True, vmem_limit_bytes=VMEM_ALL),
        cost_estimate=pl.CostEstimate(flops=3 * 10**9, bytes_accessed=12 * 2**20, transcendentals=10**6),
        name="project",
    )(lengths, prefix, hidden, norm_gain, freqs, w_query, w_keyval, w_output)


def attention_kernel(
    lens_ref, pref_ref, q_ref, k_ref, v_ref, cache_ref, o_ref, qs, ks, vs, stored, outs, sems, out_sem
):
    rows, width = q_ref.shape
    column = pl.multiple_of(lax.axis_index("tp") // 4 * 2 * HD, 2 * HD)
    inside = pl.ds(0, rows)
    loads = [
        pltpu.make_async_copy(q_ref, qs.at[inside], sems.at[REQ_REP]),
        pltpu.make_async_copy(k_ref, ks.at[inside], sems.at[REQ_REP + 1]),
        pltpu.make_async_copy(v_ref, vs.at[inside], sems.at[REQ_REP + 2]),
    ]

    def fetch(request):
        at = pl.ds(pl.multiple_of(request * PREF_MAX, PREF_MAX), PREF_MAX)
        return pltpu.make_async_copy(cache_ref.at[at, pl.ds(column, 2 * HD)], stored.at[at, :], sems.at[request])

    fetch(0).start()
    for load in loads:
        load.start()
    for request in range(1, REQ_REP):
        fetch(request).start()
    spare = pl.ds(rows, qs.shape[0] - rows)
    ks[spare, :] = jnp.zeros((TQ, HD), jnp.bfloat16)
    vs[spare, :] = jnp.zeros((TQ, HD), jnp.bfloat16)
    for load in loads:
        load.wait()
    factor = HD ** (-0.5) * math.log2(math.e)
    nt = (((1,), (1,)), ((), ()))
    lane = lax.broadcasted_iota(jnp.int32, (TQ, TQ), 1)
    row = lax.broadcasted_iota(jnp.int32, (TQ, TQ), 0)

    def tile(start, aligned, base, prefix, index, parts):
        rows_at = pl.ds(pl.multiple_of(aligned + index * TQ, 16), TQ)
        for h in range(width // HD):
            cols = slice(h * HD, (h + 1) * HD)
            q = qs[rows_at, cols]
            scores, values = [], []
            for part in range(parts):
                at = pl.ds(pl.multiple_of(base + part * TQ, TQ), TQ)
                score = lax.dot_general(q, stored[at, :HD], nt, preferred_element_type=jnp.float32)
                if part == parts - 1:
                    score = jnp.where(lane < prefix - part * TQ, score, NEG_MASK)
                scores.append(score)
                values.append((stored, at, slice(HD, 2 * HD)))
            for part in range(index + 1):
                at = pl.ds(pl.multiple_of(aligned + part * TQ, 16), TQ)
                score = lax.dot_general(q, ks[at, :], nt, preferred_element_type=jnp.float32)
                if part == index:
                    score = jnp.where(lane <= row, score, NEG_MASK)
                if part == 0:
                    score = jnp.where(lane >= start - aligned, score, NEG_MASK)
                scores.append(score)
                values.append((vs, at, slice(0, HD)))
            peak = scores[0]
            for score in scores[1:]:
                peak = jnp.maximum(peak, score)
            peak = jnp.max(peak, axis=1, keepdims=True)
            total, gathered = None, None
            for score, (ref, at, which) in zip(scores, values):
                e = jnp.exp2((score - peak) * factor)
                total = e if total is None else total + e
                part = jnp.dot(e.astype(jnp.bfloat16), ref[at, which], preferred_element_type=jnp.float32)
                gathered = part if gathered is None else gathered + part
            result = gathered / jnp.sum(total, axis=1, keepdims=True)
            if index == 0:
                keep = row[:, :HD] + aligned < start
                result = jnp.where(keep, outs[rows_at, cols].astype(jnp.float32), result)
            outs[rows_at, cols] = result.astype(jnp.bfloat16)

    def one(request, start):
        end, prefix = start + lens_ref[0, request], pref_ref[request]
        aligned = start // 16 * 16
        base = request * PREF_MAX
        fetch(request).wait()
        for index in range(3):
            for parts in (1, 2):
                fits = (prefix <= TQ) if parts == 1 else (prefix > TQ)
                pl.when((aligned + index * TQ < end) & fits)(
                    functools.partial(tile, start, aligned, base, prefix, index, parts)
                )
        return end

    lax.fori_loop(0, REQ_REP, one, 0)
    store = pltpu.make_async_copy(outs.at[inside], o_ref, out_sem)
    store.start()
    store.wait()


def attend(lengths, prefix, q, k, v, cache):
    rows, width = q.shape
    bf16, dma = jnp.bfloat16, pltpu.SemaphoreType.DMA
    return pl.pallas_call(
        attention_kernel,
        out_shape=jax.ShapeDtypeStruct((rows, width), bf16),
        in_specs=[smem(), smem(), anywhere(), anywhere(), anywhere(), anywhere()],
        out_specs=anywhere(),
        scratch_shapes=[
            pltpu.VMEM((rows + TQ, width), bf16),
            pltpu.VMEM((rows + TQ, HD), bf16),
            pltpu.VMEM((rows + TQ, HD), bf16),
            pltpu.VMEM((REQ_REP * PREF_MAX, 2 * HD), bf16),
            pltpu.VMEM((rows + TQ, width), bf16),
            dma((REQ_REP + 3,)),
            dma,
        ],
        compiler_params=pltpu.CompilerParams(vmem_limit_bytes=VMEM_ALL),
        cost_estimate=pl.CostEstimate(flops=2 * 10**9, bytes_accessed=3 * 2**20, transcendentals=2 * 10**6),
        name="attention",
    )(lengths, prefix, q, k, v, cache)


def output_kernel(
    att_ref, hidden_ref, wo_here,
    resid_out, inverse_ref,
    resid_ref, wo_ref, att, part_send, part_recv, own, hid, sums_mine, sums,
    hid_sem, ring_send, ring_recv, core_send, core_recv, part_sems, sum_send, sum_recv, wo_sem, own_sem, wo_send, wo_recv, store_sem,
):
    rep, tp, x, z, zh, y, c = place()
    rows, width = hid.shape
    load = pltpu.make_async_copy(
        hidden_ref.at[:, pl.ds(pl.multiple_of(tp * width, width), width)], hid, hid_sem
    )
    load.start()
    load_wo = pltpu.make_async_copy(wo_here, wo_ref.at[pl.ds(x * 4, 4)], wo_sem)
    load_wo.start()
    load_own = pltpu.make_async_copy(att_ref, att.at[0, 0], own_sem)
    load_own.start()
    barrier = pltpu.get_barrier_semaphore()
    for k in range(1, 16):
        signal(barrier, (rep, (tp + k) % 16))
    for dx in (1, 3):
        signal(barrier, ((x + dx) % 4 * 4 + z, tp))
    pl.semaphore_wait(barrier, 17)

    def at_y(to):
        return (rep, zh * 8 + (to % 4) * 2 + c)

    partner = (rep, tp + 1 - 2 * c)
    across = (rep, (tp + 8) % 16)
    size = rows // CHUNKS
    half = size // 2
    pending = []

    def send(src, dst, ssem, rsem, device):
        made = pltpu.make_async_remote_copy(
            src_ref=src, dst_ref=dst, send_sem=ssem, recv_sem=rsem, device_id=device, device_id_type=MESH
        )
        made.start()
        pending.append(made)

    def wait(ref, sem):
        pltpu.make_async_copy(ref, ref, sem).wait()

    def own_send(m):
        at = pl.ds(m * size, size)
        src = att_ref.at[at]
        send(src, att.at[0, 1, at], ring_send.at[0, m], ring_recv.at[0, m], at_y(y + 1))
        send(src, att.at[0, 2, at], ring_send.at[1, m], ring_recv.at[1, m], at_y(y + 3))
        send(src, att.at[1, 0, at], core_send.at[0, m], core_recv.at[0, m], partner)

    def ring_in(m):
        at = pl.ds(m * size, size)
        for side in range(2):
            ref = att.at[0, 1 + side, at]
            wait(ref, ring_recv.at[side, m])
            part = pl.ds(m * size + side * half, half)
            send(
                att.at[0, 1 + side, part], att.at[0, 3, part],
                ring_send.at[2 + side, m], ring_recv.at[2 + side, m], at_y(y + 1 + 2 * side),
            )
            send(ref, att.at[1, 1 + side, at], core_send.at[1 + side, m], core_recv.at[1 + side, m], partner)

    def far_in(m):
        for side in range(2):
            wait(att.at[0, 3, pl.ds(m * size + side * half, half)], ring_recv.at[2 + side, m])
        ref = att.at[0, 3, pl.ds(m * size, size)]
        send(ref, att.at[1, 3, pl.ds(m * size, size)], core_send.at[3, m], core_recv.at[3, m], partner)

    def columns(which):
        return (1 - zh if which == 0 else zh) * 2

    def beside(dx):
        return ((x + dx) % 4 * 4 + z, tp)

    def weight_out(which):
        for side, dx in enumerate((1, 3)):
            send(
                wo_here.at[pl.ds(columns(which), 2)], wo_ref.at[pl.ds(x * 4 + columns(which), 2)],
                wo_send.at[which, side], wo_recv.at[which, side], beside(dx),
            )

    def weight_relay(which):
        for side, dx in enumerate((3, 1)):
            at = pl.ds((x + dx) % 4 * 4 + columns(which), 2)
            wait(wo_ref.at[at], wo_recv.at[which, side])
            some = wo_ref.at[at, pl.ds(side * (BLK // 2), BLK // 2)]
            send(some, some, wo_send.at[which, 2 + side], wo_recv.at[which, 2 + side], beside(4 - dx))

    def weight_in(which):
        for side in range(2):
            some = pl.ds(side * (BLK // 2), BLK // 2)
            wait(wo_ref.at[pl.ds((x + 2) % 4 * 4 + columns(which), 2), some], wo_recv.at[which, 2 + side])

    def contract(at, target):
        total = None
        for side in range(2):
            for d, dy in enumerate((0, 3, 1, 2)):
                core = c if side == 0 else 1 - c
                block = ((y + dy) % 4) * 4 + target * 2 + core
                part = jnp.dot(att[side, d, at, :], wo_ref[block], preferred_element_type=jnp.float32)
                total = part if total is None else total + part
        return total

    def away(m):
        at = pl.ds(m * size, size)
        for d in range(4):
            wait(att.at[1, d, at], core_recv.at[d, m])
        part_send[at, :] = contract(at, 1 - zh).astype(jnp.bfloat16)
        send(part_send.at[at], part_recv.at[at], part_sems.at[0, m], part_sems.at[1, m], across)

    def mine(m):
        at = pl.ds(m * BLK, BLK)
        own[at, :] = contract(at, zh)

    own_send(0)
    weight_out(0)
    own_send(1)
    own_send(2)
    load_wo.wait()
    load_own.wait()
    ready = 0
    for i in range(CHUNKS + 2):
        if i < CHUNKS:
            ring_in(i)
        if i + 3 < CHUNKS:
            own_send(i + 3)
        if 1 <= i <= CHUNKS:
            far_in(i - 1)
        if i == 1:
            weight_relay(0)
            weight_out(1)
        if i == WEIGHT_AT:
            weight_in(0)
        if i == CHUNKS - 2:
            weight_relay(1)
        if i >= WEIGHT_AT:
            for _ in range(2):
                if ready <= i - 2:
                    away(ready)
                    ready += 1
        if i == CHUNKS:
            weight_in(1)
            for m in range(OWN_EARLY):
                mine(m)
    for m in range(OWN_EARLY, rows // BLK):
        mine(m)
    load.wait()
    for m in range(CHUNKS):
        at = pl.ds(m * size, size)
        wait(part_recv.at[at], part_sems.at[1, m])
        for i in range(size // HD):
            row = m * (size // HD) + i
            here = pl.ds(row * HD, HD)
            resid = (
                hid[here, :].astype(jnp.float32) + (own[here, :] + part_recv[here, :].astype(jnp.float32))
            ).astype(jnp.bfloat16)
            resid_ref[here, :] = resid
            wide = resid.astype(jnp.float32)
            total = jnp.sum(wide * wide, axis=1, keepdims=True)
            sums_mine[pl.ds(row, 1), :] = jnp.transpose(jnp.broadcast_to(total, (HD, HD)))[:1, :]
    store = pltpu.make_async_copy(resid_ref, resid_out, store_sem)
    for k in range(1, 16):
        send(sums_mine, sums.at[k], sum_send.at[k], sum_recv.at[k], (rep, (tp + k) % 16))
    store.start()
    total = sums_mine[...]
    for k in range(1, 16):
        wait(sums.at[k], sum_recv.at[k])
        total = total + sums[k]
    inverse_ref[...] = lax.rsqrt(total * (1.0 / D) + norm_eps)
    store.wait()
    for made in pending:
        made.wait_send()


def finish(attended, hidden, wo_here):
    rows, width = attended.shape
    bf16, f32, dma = jnp.bfloat16, jnp.float32, pltpu.SemaphoreType.DMA
    return pl.pallas_call(
        output_kernel,
        out_shape=(jax.ShapeDtypeStruct((rows, width), bf16), jax.ShapeDtypeStruct((rows // HD, HD), f32)),
        in_specs=[anywhere(), anywhere(), anywhere()],
        out_specs=(anywhere(), vmem()),
        scratch_shapes=[
            pltpu.VMEM((rows, width), bf16),
            pltpu.VMEM((16, BLK, BLK), bf16),
            pltpu.VMEM((2, 4, rows, width), bf16),
            pltpu.VMEM((rows, width), bf16),
            pltpu.VMEM((rows, width), bf16),
            pltpu.VMEM((rows, width), f32),
            pltpu.VMEM((rows, width), bf16),
            pltpu.VMEM((rows // HD, HD), f32),
            pltpu.VMEM((16, rows // HD, HD), f32),
            dma,
            dma((4, CHUNKS)),
            dma((4, CHUNKS)),
            dma((4, CHUNKS)),
            dma((4, CHUNKS)),
            dma((2, CHUNKS)),
            dma((16,)),
            dma((16,)),
            dma,
            dma,
            dma((2, 4)),
            dma((2, 4)),
            dma,
        ],
        compiler_params=pltpu.CompilerParams(collective_id=1, has_side_effects=True, vmem_limit_bytes=VMEM_ALL),
        cost_estimate=pl.CostEstimate(flops=2 * 10**9, bytes_accessed=6 * 2**20, transcendentals=10**4),
        name="finish",
    )(attended, hidden, wo_here)


def scale_kernel(resid_in, inverse_ref, gain_ref, resid_out, normed_out, gain_row, resid, normed, in_sem, out_sem, norm_sem):
    rows, width = resid.shape
    count = in_sem.shape[0]
    size = rows // count
    loads, stores = [], []
    for i in range(count):
        at = pl.ds(i * size, size)
        loads.append(pltpu.make_async_copy(resid_in.at[at], resid.at[at], in_sem.at[i]))
        loads[-1].start()
    gain_row[...] = gain_ref[...].astype(jnp.float32).reshape(1, D)
    gain = gain_row[:, pl.ds(pl.multiple_of(lax.axis_index("tp") * width, width), width)]
    for i in range(count):
        at = pl.ds(i * size, size)
        loads[i].wait()
        stores.append(pltpu.make_async_copy(resid.at[at], resid_out.at[at], out_sem.at[i]))
        stores[-1].start()
        for row in range(i * size // HD, (i + 1) * size // HD):
            here = pl.ds(row * HD, HD)
            column = jnp.transpose(jnp.broadcast_to(inverse_ref[row : row + 1, :], (HD, HD)))
            for h in range(width // HD):
                cols = slice(h * HD, (h + 1) * HD)
                normed[here, cols] = (
                    resid[here, cols].astype(jnp.float32) * column * gain[:, cols]
                ).astype(jnp.bfloat16)
        stores.append(pltpu.make_async_copy(normed.at[at], normed_out.at[at], norm_sem.at[i]))
        stores[-1].start()
    for store in stores:
        store.wait()


def scale(resid, inverse, out_gain):
    rows, width = resid.shape
    bf16, dma = jnp.bfloat16, pltpu.SemaphoreType.DMA
    return pl.pallas_call(
        scale_kernel,
        out_shape=(jax.ShapeDtypeStruct((rows, width), bf16), jax.ShapeDtypeStruct((rows, width), bf16)),
        in_specs=[anywhere(), vmem(), vmem()],
        out_specs=(anywhere(), anywhere()),
        scratch_shapes=[
            pltpu.VMEM((1, D), jnp.float32),
            pltpu.VMEM((rows, width), bf16),
            pltpu.VMEM((rows, width), bf16),
            dma((4,)),
            dma((4,)),
            dma((4,)),
        ],
        compiler_params=pltpu.CompilerParams(vmem_limit_bytes=VMEM_ALL),
        cost_estimate=pl.CostEstimate(flops=10**6, bytes_accessed=3 * 2**19, transcendentals=0),
        name="scale",
    )(resid, inverse, out_gain)


def body(hidden, norm_gain, w_query, w_keyval, w_output, cache, lengths, prefix, out_gain):
    powers = np.arange(HD) % (HD // 2) * 2.0 / HD
    freqs = jnp.asarray((rope_base**-powers).astype(np.float32).reshape(1, HD))
    q, k, v, wo_here = project(lengths, prefix, hidden, norm_gain, freqs, w_query, w_keyval.T, w_output)
    attended = attend(lengths, prefix, q, k, v, cache)
    resid, inverse = finish(attended, hidden, wo_here)
    return scale(resid, inverse, out_gain)


def solution(mesh):
    placed = (
        P("rep", None),
        P(),
        P("rep", "tp"),
        P("rep", "tp"),
        P("tp", "rep"),
        P("rep", None),
        P("rep", None),
        P("rep"),
        P(),
    )
    return jax.shard_map(
        body,
        mesh=mesh,
        in_specs=placed,
        out_specs=(P("rep", "tp"), P("rep", "tp")),
        check_vma=False,
    )
```

```python
import functools
import math

import jax
import jax.numpy as jnp
import numpy as np
from jax import lax
from jax.experimental import pallas as pl
from jax.experimental.pallas import tpu as pltpu
from jax.sharding import PartitionSpec as P

H = 32
KV = 4
HD = 128
REQ_REP = 4
PREF_MAX = 512

norm_eps = 1e-05
rope_base = 5000000.0
TQ = 256
NEG_MASK = -1e30
VMEM_ALL = 67043328
CHUNKS = 8
WEIGHT_AT = 3
OWN_EARLY = 3


MESH = pl.DeviceIdType.MESH
D = 4096
BLK = 256


def place():
    rep, tp = lax.axis_index("rep"), lax.axis_index("tp")
    return rep, tp, rep // 4, rep % 4, tp // 8, (tp // 2) % 4, tp % 2


def line_order(z):
    power = 1 + 3 * z + 9 * (z * (z - 1) // 2) + 27 * (z * (z - 1) * (z - 2) // 6)
    tables = []
    for picks in ((1, 0, 1, 2), (2, 2, 3, 1), (3, 3, 0, 0)):
        tables.append(sum(pick * 4**i for i, pick in enumerate(picks)))
    return [z] + [(table // power) % 4 for table in tables]


def signal(sem, device):
    pl.semaphore_signal(sem, inc=1, device_id=device, device_id_type=MESH)


class Gather:
    def __init__(self, own, full, recv, send, half, ring=True):
        self.own, self.full, self.recv, self.send, self.half = own, full, recv, send, half
        self.in_ring = ring
        self.rep, self.tp, self.x, self.z = place()[:4]
        self.order = line_order(self.z)
        self.right = ((self.x + 1) % 4) * 4
        self.left = ((self.x + 3) % 4) * 4
        self.far = ((self.x + 2) % 4) * 4
        self.pending = []

    def copy(self, src, dst, slot, sem, rep, cond=None):
        made = pltpu.make_async_remote_copy(
            src_ref=src,
            dst_ref=dst,
            send_sem=self.send.at[slot],
            recv_sem=sem,
            device_id=(rep, self.tp),
            device_id_type=MESH,
        )
        if cond is None:
            made.start()
        else:
            pl.when(cond)(made.start)
        self.pending.append((made, cond))

    def arrived(self, index, block):
        ref = self.full.at[block]
        pltpu.make_async_copy(ref, ref, self.recv.at[index, block]).wait()

    def line(self, k):
        zo = self.order[k]
        block = self.x * 4 + zo if self.in_ring else zo
        dst, sem = self.full.at[block], self.recv.at[0, block]
        if k == 0:
            src = self.own
            onward, back = self.z < 3, self.z > 0
        else:
            self.arrived(0, block)
            src = dst
            onward, back = (zo < self.z) & (self.z < 3), (zo > self.z) & (self.z > 0)
        self.copy(src, dst, 6 * k, sem, self.x * 4 + lax.min(self.z + 1, 3), onward)
        self.copy(src, dst, 6 * k + 1, sem, self.x * 4 + lax.max(self.z - 1, 0), back)
        if not self.in_ring:
            return
        self.copy(src, dst, 6 * k + 2, sem, self.right + self.z)
        self.copy(src, dst, 6 * k + 3, sem, self.left + self.z)

    def ring(self, k, side):
        zo = self.order[k]
        block = (self.left if side == 0 else self.right) + zo
        self.arrived(0, block)
        part = pl.ds(0, self.half) if side == 0 else pl.ds(self.half, self.half)
        ref = self.full.at[block, part]
        target = (self.right if side == 0 else self.left) + self.z
        self.copy(ref, ref, 6 * k + 4 + side, self.recv.at[side, block], target)
        return block

    def opposite(self, k):
        block = self.far + self.order[k]
        for side in range(2):
            ref = self.full.at[block, pl.ds(side * self.half, self.half)]
            pltpu.make_async_copy(ref, ref, self.recv.at[side, block]).wait()
        return block

    def drain(self):
        for made, cond in self.pending:
            if cond is None:
                made.wait_send()
            else:
                pl.when(cond)(made.wait_send)


def project_kernel(
    lens_ref, pref_ref, hidden_ref, gain_ref, freq_ref, wq_ref, wkv_ref, wo_ref,
    q_out, k_out, v_out, wo_out,
    gain, q_ref, k_ref, v_ref, hid, x3, full_q, full_s, full_w, turned, qacc, kacc, cosine, sine, mine, other,
    hid_sem, recv_q, send_q, recv_r, send_r, recv_s, send_s, recv_w, send_w, kv_send, kv_recv, perm_send, perm_recv, swap_sem, out_sem, own_sem, store_sem,
):
    rep, tp, x, z, zh, y, c = place()
    rows = hid.shape[0]
    count = hid_sem.shape[0]
    chunk = rows // count
    loads = []
    for i in range(count):
        at = pl.ds(i * chunk, chunk)
        loads.append(pltpu.make_async_copy(hidden_ref.at[at], hid.at[at], hid_sem.at[i]))
        loads[-1].start()
    own_load = pltpu.make_async_copy(wq_ref, full_q.at[rep], own_sem)
    own_load.start()

    zh_t = x // 2
    perm_dst = (y * 4 + zh_t * 2 + c, zh * 8 + ((x % 2) * 2 + z // 2) * 2 + z % 2)
    perm_src = (((z // 2) * 2 + y // 2) * 4 + (y % 2) * 2 + c, zh * 8 + x * 2 + z % 2)
    perm_away = (perm_dst[0] != rep) | (perm_dst[1] != tp)
    barrier = pltpu.get_barrier_semaphore()
    line_right, line_left = x * 4 + lax.min(z + 1, 3), x * 4 + lax.max(z - 1, 0)

    pl.when(z < 3)(lambda: signal(barrier, (line_right, tp)))
    pl.when(z > 0)(lambda: signal(barrier, (line_left, tp)))
    signal(barrier, (((x + 1) % 4) * 4 + z, tp))
    signal(barrier, (((x + 3) % 4) * 4 + z, tp))
    signal(barrier, (rep, tp + 1 - 2 * c))
    pl.when(perm_away)(lambda: signal(barrier, perm_src))
    for j in range(8):
        source = c * 8 + j
        pl.when(source != tp)(lambda source=source: signal(barrier, (rep, source)))
    shape = (4 * 16, 4 * 16)
    out_row, in_col = lax.broadcasted_iota(jnp.int32, shape, 0), lax.broadcasted_iota(jnp.int32, shape, 1)
    pick = ((out_row % 16) * KV + out_row // 16 == in_col).astype(jnp.float32).astype(jnp.bfloat16)
    turned[...] = lax.dot_general(
        pick, wkv_ref[...], (((1,), (0,)), ((), ())), preferred_element_type=jnp.float32
    ).astype(jnp.bfloat16)

    starts, first_token = [], 0
    for request in range(REQ_REP):
        starts.append(first_token)
        first_token = first_token + lens_ref[0, request]

    def angles(i, _):
        at = pl.ds(pl.multiple_of(i * 128, 128), 128)
        token = i * 128 + lax.broadcasted_iota(jnp.int32, (128, HD), 0)
        position = jnp.zeros((128, HD), jnp.int32)
        for request in range(REQ_REP):
            shift = pref_ref[request] - starts[request]
            position = jnp.where(token >= starts[request], token + shift, position)
        angle = position.astype(jnp.float32) * freq_ref[...]
        lane = lax.broadcasted_iota(jnp.int32, (128, HD), 1)
        cosine[at, :] = jnp.cos(angle)
        wave = jnp.sin(angle)
        sine[at, :] = jnp.where(lane < HD // 2, -wave, wave)
        return 0

    lax.fori_loop(0, rows // 128, angles, 0)
    gain[...] = gain_ref[...].astype(jnp.float32).reshape(1, D)

    line_peers = (lax.min(z + 1, 3) - z) + (z - lax.max(z - 1, 0))
    pl.semaphore_wait(barrier, 10 + line_peers + perm_away.astype(jnp.int32) + (c + zh) % 2)

    low, high = pl.ds(0, BLK // 2), pl.ds(BLK // 2, BLK // 2)
    stream_q = Gather(wq_ref.at[low], full_q.at[:, low], recv_q, send_q, BLK // 4)
    stream_r = Gather(wq_ref.at[high], full_q.at[:, high], recv_r, send_r, BLK // 4)
    stream_s = Gather(full_s.at[rep], full_s, recv_s, send_s, full_s.shape[1] // 2)
    stream_w = Gather(full_w.at[z], full_w, recv_w, send_w, 0, False)
    stream_q.line(0)
    stream_r.line(0)

    def piece(head, which):
        target = (head // 2) * 8 + (2 * (head % 2) + which) * 2 + zh
        from_ref = turned.at[pl.ds(head * 16, 16)]
        to_ref = full_s.at[rep, pl.ds(pl.multiple_of((tp % 8) * 16, 16), 16)]
        away = target != tp
        made = pltpu.make_async_remote_copy(
            src_ref=from_ref, dst_ref=to_ref, send_sem=kv_send.at[head * 2 + which], recv_sem=kv_recv.at[tp % 8],
            device_id=(rep, target), device_id_type=MESH,
        )
        here = pltpu.make_async_copy(from_ref, to_ref, kv_recv.at[tp % 8])
        pl.when(away)(made.start)
        pl.when(jnp.logical_not(away))(here.start)
        return made, away

    pieces = [piece(head, which) for head in range(KV) for which in range(2)]

    wo_dst = full_w.at[perm_dst[0] % 4]
    permute = pltpu.make_async_remote_copy(
        src_ref=wo_ref, dst_ref=wo_dst, send_sem=perm_send, recv_sem=perm_recv,
        device_id=perm_dst, device_id_type=MESH,
    )
    stay = pltpu.make_async_copy(wo_ref, wo_dst, perm_recv)
    pl.when(perm_away)(permute.start)
    pl.when(jnp.logical_not(perm_away))(stay.start)

    def norm(i):
        loads[i].wait()

        def some(j, _):
            at = pl.ds(pl.multiple_of(i * chunk + j * 16, 16), 16)
            wide = hid[at, :].astype(jnp.float32)
            meansq = jnp.sum(wide * wide, axis=1, keepdims=True) * (1.0 / D)
            scaled = wide * lax.rsqrt(meansq + norm_eps)
            for b in range(D // BLK):
                cols = slice(b * BLK, (b + 1) * BLK)
                x3[b, at, :] = (scaled[:, cols] * gain[:, cols]).astype(jnp.bfloat16)
            return 0

        lax.fori_loop(0, chunk // 16, some, 0)

    def use_q(block, own=False):
        for i in range(rows // BLK):
            at = pl.ds(i * BLK, BLK)
            part = jnp.dot(x3[block, at, :], full_q[block], preferred_element_type=jnp.float32)
            qacc[at, :] = part if own else qacc[at, :] + part

    def use_s(block, own=False):
        for i in range(rows // BLK):
            at = pl.ds(i * BLK, BLK)
            part = lax.dot_general(
                x3[block, at, :], full_s[block, :HD, :], (((1,), (1,)), ((), ())),
                preferred_element_type=jnp.float32,
            )
            kacc[at, :] = part if own else kacc[at, :] + part

    norm(0)
    norm(1)
    stream_q.line(1)
    stream_r.line(1)
    for j in range(8):
        ref = full_s.at[rep, pl.ds(j * 16, 16)]
        pltpu.make_async_copy(ref, ref, kv_recv.at[j]).wait()
    stream_s.line(0)
    norm(2)
    norm(3)
    stream_s.line(1)
    norm(4)
    stream_s.line(2)
    stream_q.line(2)
    stream_r.line(2)
    norm(5)
    norm(6)
    stream_s.line(3)
    stream_q.line(3)
    stream_r.line(3)
    norm(7)
    own_load.wait()
    use_q(rep, True)
    use_s(rep, True)
    for k in range(4):
        lefts_s, rights_s = stream_s.ring(k, 0), stream_s.ring(k, 1)
        lefts, rights = stream_q.ring(k, 0), stream_q.ring(k, 1)
        stream_r.ring(k, 0)
        stream_r.ring(k, 1)
        if k > 0:
            own_block = x * 4 + stream_q.order[k]
            use_q(own_block)
            use_s(own_block)
        for block in (lefts, rights):
            use_q(block)
        for block in (lefts_s, rights_s):
            use_s(block)
        if k > 0:
            stream_r.opposite(k - 1)
            use_q(stream_q.opposite(k - 1))
            use_s(stream_s.opposite(k - 1))
        if k == 0:
            own_wo = full_w.at[z]
            pltpu.make_async_copy(own_wo, own_wo, perm_recv).wait()
        stream_w.line(k)
    flush = pltpu.make_async_copy(full_w, wo_out, out_sem)
    flush.start()
    use_s(stream_s.opposite(3))

    fresh = kacc[...].astype(jnp.bfloat16).astype(jnp.float32)
    turned_key = fresh * cosine[...] + pltpu.roll(fresh, HD // 2, 1) * sine[...]
    mine[...] = jnp.where(c == 0, turned_key, fresh).astype(jnp.bfloat16)
    swap = pltpu.make_async_remote_copy(
        src_ref=mine, dst_ref=other, send_sem=swap_sem.at[0], recv_sem=swap_sem.at[1],
        device_id=(rep, tp + 1 - 2 * c), device_id_type=MESH,
    )
    stream_r.opposite(3)
    use_q(stream_q.opposite(3))
    swap.start()
    for h in range(q_ref.shape[1] // HD):
        cols = slice(h * HD, (h + 1) * HD)
        u = qacc[:, cols]
        q_ref[:, cols] = (u * cosine[...] + pltpu.roll(u, HD // 2, 1) * sine[...]).astype(jnp.bfloat16)
    store_q = pltpu.make_async_copy(q_ref, q_out, store_sem.at[0])
    store_q.start()
    for made, away in pieces:
        pl.when(away)(made.wait_send)
    pl.when(perm_away)(permute.wait_send)
    stream_q.drain()
    stream_r.drain()
    stream_s.drain()
    stream_w.drain()
    swap.wait()

    @pl.when(c == 0)
    def _():
        k_ref[...] = mine[...]
        v_ref[...] = other[...]

    @pl.when(c != 0)
    def _():
        k_ref[...] = other[...]
        v_ref[...] = mine[...]

    store_k = pltpu.make_async_copy(k_ref, k_out, store_sem.at[1])
    store_v = pltpu.make_async_copy(v_ref, v_out, store_sem.at[2])
    store_k.start()
    store_v.start()
    store_q.wait()
    store_k.wait()
    store_v.wait()
    flush.wait()


def vmem():
    return pl.BlockSpec(memory_space=pltpu.VMEM)


def smem():
    return pl.BlockSpec(memory_space=pltpu.SMEM)


def anywhere():
    return pl.BlockSpec(memory_space=pl.ANY)


def project(lengths, prefix, hidden, norm_gain, freqs, w_query, w_keyval, w_output):
    rows = hidden.shape[0]
    bf16, f32, dma = jnp.bfloat16, jnp.float32, pltpu.SemaphoreType.DMA
    return pl.pallas_call(
        project_kernel,
        out_shape=(
            jax.ShapeDtypeStruct((rows, BLK), bf16),
            jax.ShapeDtypeStruct((rows, HD), bf16),
            jax.ShapeDtypeStruct((rows, HD), bf16),
            jax.ShapeDtypeStruct((4, BLK, BLK), bf16),
        ),
        in_specs=[smem(), smem(), anywhere(), vmem(), vmem(), anywhere(), vmem(), anywhere()],
        out_specs=(anywhere(), anywhere(), anywhere(), anywhere()),
        scratch_shapes=[
            pltpu.VMEM((1, D), f32),
            pltpu.VMEM((rows, BLK), bf16),
            pltpu.VMEM((rows, HD), bf16),
            pltpu.VMEM((rows, HD), bf16),
            pltpu.VMEM((rows, D), bf16),
            pltpu.VMEM((16, rows, BLK), bf16),
            pltpu.VMEM((16, BLK, BLK), bf16),
            pltpu.VMEM((16, HD, BLK), bf16),
            pltpu.VMEM((4, BLK, BLK), bf16),
            pltpu.VMEM((64, BLK), bf16),
            pltpu.VMEM((rows, BLK), f32),
            pltpu.VMEM((rows, HD), f32),
            pltpu.VMEM((rows, HD), f32),
            pltpu.VMEM((rows, HD), f32),
            pltpu.VMEM((rows, HD), bf16),
            pltpu.VMEM((rows, HD), bf16),
            dma((8,)),
            dma((2, 16)),
            dma((24,)),
            dma((2, 16)),
            dma((24,)),
            dma((2, 16)),
            dma((24,)),
            dma((1, 4)),
            dma((24,)),
            dma((8,)),
            dma((8,)),
            dma,
            dma,
            dma((2,)),
            dma,
            dma,
            dma((3,)),
        ],
        compiler_params=pltpu.CompilerParams(collective_id=0, has_side_effects=True, vmem_limit_bytes=VMEM_ALL),
        cost_estimate=pl.CostEstimate(flops=3 * 10**9, bytes_accessed=12 * 2**20, transcendentals=10**6),
        name="project",
    )(lengths, prefix, hidden, norm_gain, freqs, w_query, w_keyval, w_output)


def attention_kernel(
    lens_ref, pref_ref, q_ref, k_ref, v_ref, cache_ref, o_ref, qs, ks, vs, stored, outs, sems, out_sem
):
    rows, width = q_ref.shape
    column = pl.multiple_of(lax.axis_index("tp") // 4 * 2 * HD, 2 * HD)
    inside = pl.ds(0, rows)
    loads = [
        pltpu.make_async_copy(q_ref, qs.at[inside], sems.at[REQ_REP]),
        pltpu.make_async_copy(k_ref, ks.at[inside], sems.at[REQ_REP + 1]),
        pltpu.make_async_copy(v_ref, vs.at[inside], sems.at[REQ_REP + 2]),
    ]

    def fetch(request):
        at = pl.ds(pl.multiple_of(request * PREF_MAX, PREF_MAX), PREF_MAX)
        return pltpu.make_async_copy(cache_ref.at[at, pl.ds(column, 2 * HD)], stored.at[at, :], sems.at[request])

    fetch(0).start()
    for load in loads:
        load.start()
    for request in range(1, REQ_REP):
        fetch(request).start()
    spare = pl.ds(rows, qs.shape[0] - rows)
    ks[spare, :] = jnp.zeros((TQ, HD), jnp.bfloat16)
    vs[spare, :] = jnp.zeros((TQ, HD), jnp.bfloat16)
    for load in loads:
        load.wait()
    factor = HD ** (-0.5) * math.log2(math.e)
    nt = (((1,), (1,)), ((), ()))
    lane = lax.broadcasted_iota(jnp.int32, (TQ, TQ), 1)
    row = lax.broadcasted_iota(jnp.int32, (TQ, TQ), 0)

    def tile(start, aligned, base, prefix, index, parts):
        rows_at = pl.ds(pl.multiple_of(aligned + index * TQ, 16), TQ)
        for h in range(width // HD):
            cols = slice(h * HD, (h + 1) * HD)
            q = qs[rows_at, cols]
            scores, values = [], []
            for part in range(parts):
                at = pl.ds(pl.multiple_of(base + part * TQ, TQ), TQ)
                score = lax.dot_general(q, stored[at, :HD], nt, preferred_element_type=jnp.float32)
                if part == parts - 1:
                    score = jnp.where(lane < prefix - part * TQ, score, NEG_MASK)
                scores.append(score)
                values.append((stored, at, slice(HD, 2 * HD)))
            for part in range(index + 1):
                at = pl.ds(pl.multiple_of(aligned + part * TQ, 16), TQ)
                score = lax.dot_general(q, ks[at, :], nt, preferred_element_type=jnp.float32)
                if part == index:
                    score = jnp.where(lane <= row, score, NEG_MASK)
                if part == 0:
                    score = jnp.where(lane >= start - aligned, score, NEG_MASK)
                scores.append(score)
                values.append((vs, at, slice(0, HD)))
            peak = scores[0]
            for score in scores[1:]:
                peak = jnp.maximum(peak, score)
            peak = jnp.max(peak, axis=1, keepdims=True)
            total, gathered = None, None
            for score, (ref, at, which) in zip(scores, values):
                e = jnp.exp2((score - peak) * factor)
                total = e if total is None else total + e
                part = jnp.dot(e.astype(jnp.bfloat16), ref[at, which], preferred_element_type=jnp.float32)
                gathered = part if gathered is None else gathered + part
            result = gathered / jnp.sum(total, axis=1, keepdims=True)
            if index == 0:
                keep = row[:, :HD] + aligned < start
                result = jnp.where(keep, outs[rows_at, cols].astype(jnp.float32), result)
            outs[rows_at, cols] = result.astype(jnp.bfloat16)

    def one(request, start):
        end, prefix = start + lens_ref[0, request], pref_ref[request]
        aligned = start // 16 * 16
        base = request * PREF_MAX
        fetch(request).wait()
        for index in range(3):
            for parts in (1, 2):
                fits = (prefix <= TQ) if parts == 1 else (prefix > TQ)
                pl.when((aligned + index * TQ < end) & fits)(
                    functools.partial(tile, start, aligned, base, prefix, index, parts)
                )
        return end

    lax.fori_loop(0, REQ_REP, one, 0)
    store = pltpu.make_async_copy(outs.at[inside], o_ref, out_sem)
    store.start()
    store.wait()


def attend(lengths, prefix, q, k, v, cache):
    rows, width = q.shape
    bf16, dma = jnp.bfloat16, pltpu.SemaphoreType.DMA
    return pl.pallas_call(
        attention_kernel,
        out_shape=jax.ShapeDtypeStruct((rows, width), bf16),
        in_specs=[smem(), smem(), anywhere(), anywhere(), anywhere(), anywhere()],
        out_specs=anywhere(),
        scratch_shapes=[
            pltpu.VMEM((rows + TQ, width), bf16),
            pltpu.VMEM((rows + TQ, HD), bf16),
            pltpu.VMEM((rows + TQ, HD), bf16),
            pltpu.VMEM((REQ_REP * PREF_MAX, 2 * HD), bf16),
            pltpu.VMEM((rows + TQ, width), bf16),
            dma((REQ_REP + 3,)),
            dma,
        ],
        compiler_params=pltpu.CompilerParams(vmem_limit_bytes=VMEM_ALL),
        cost_estimate=pl.CostEstimate(flops=2 * 10**9, bytes_accessed=3 * 2**20, transcendentals=2 * 10**6),
        name="attention",
    )(lengths, prefix, q, k, v, cache)


def output_kernel(
    att_ref, hidden_ref, wo_here,
    resid_out, inverse_ref,
    resid_ref, wo_ref, att, part_send, part_recv, own, hid, sums_mine, sums,
    hid_sem, ring_send, ring_recv, core_send, core_recv, part_sems, sum_send, sum_recv, wo_sem, own_sem, wo_send, wo_recv, store_sem,
):
    rep, tp, x, z, zh, y, c = place()
    rows, width = hid.shape
    load = pltpu.make_async_copy(
        hidden_ref.at[:, pl.ds(pl.multiple_of(tp * width, width), width)], hid, hid_sem
    )
    load.start()
    load_wo = pltpu.make_async_copy(wo_here, wo_ref.at[pl.ds(x * 4, 4)], wo_sem)
    load_wo.start()
    load_own = pltpu.make_async_copy(att_ref, att.at[0, 0], own_sem)
    load_own.start()
    barrier = pltpu.get_barrier_semaphore()
    for k in range(1, 16):
        signal(barrier, (rep, (tp + k) % 16))
    for dx in (1, 3):
        signal(barrier, ((x + dx) % 4 * 4 + z, tp))
    pl.semaphore_wait(barrier, 17)

    def at_y(to):
        return (rep, zh * 8 + (to % 4) * 2 + c)

    partner = (rep, tp + 1 - 2 * c)
    across = (rep, (tp + 8) % 16)
    size = rows // CHUNKS
    half = size // 2
    pending = []

    def send(src, dst, ssem, rsem, device):
        made = pltpu.make_async_remote_copy(
            src_ref=src, dst_ref=dst, send_sem=ssem, recv_sem=rsem, device_id=device, device_id_type=MESH
        )
        made.start()
        pending.append(made)

    def wait(ref, sem):
        pltpu.make_async_copy(ref, ref, sem).wait()

    def own_send(m):
        at = pl.ds(m * size, size)
        src = att_ref.at[at]
        send(src, att.at[0, 1, at], ring_send.at[0, m], ring_recv.at[0, m], at_y(y + 1))
        send(src, att.at[0, 2, at], ring_send.at[1, m], ring_recv.at[1, m], at_y(y + 3))
        send(src, att.at[1, 0, at], core_send.at[0, m], core_recv.at[0, m], partner)

    def ring_in(m):
        at = pl.ds(m * size, size)
        for side in range(2):
            ref = att.at[0, 1 + side, at]
            wait(ref, ring_recv.at[side, m])
            part = pl.ds(m * size + side * half, half)
            send(
                att.at[0, 1 + side, part], att.at[0, 3, part],
                ring_send.at[2 + side, m], ring_recv.at[2 + side, m], at_y(y + 1 + 2 * side),
            )
            send(ref, att.at[1, 1 + side, at], core_send.at[1 + side, m], core_recv.at[1 + side, m], partner)

    def far_in(m):
        for side in range(2):
            wait(att.at[0, 3, pl.ds(m * size + side * half, half)], ring_recv.at[2 + side, m])
        ref = att.at[0, 3, pl.ds(m * size, size)]
        send(ref, att.at[1, 3, pl.ds(m * size, size)], core_send.at[3, m], core_recv.at[3, m], partner)

    def columns(which):
        return (1 - zh if which == 0 else zh) * 2

    def beside(dx):
        return ((x + dx) % 4 * 4 + z, tp)

    def weight_out(which):
        for side, dx in enumerate((1, 3)):
            send(
                wo_here.at[pl.ds(columns(which), 2)], wo_ref.at[pl.ds(x * 4 + columns(which), 2)],
                wo_send.at[which, side], wo_recv.at[which, side], beside(dx),
            )

    def weight_relay(which):
        for side, dx in enumerate((3, 1)):
            at = pl.ds((x + dx) % 4 * 4 + columns(which), 2)
            wait(wo_ref.at[at], wo_recv.at[which, side])
            some = wo_ref.at[at, pl.ds(side * (BLK // 2), BLK // 2)]
            send(some, some, wo_send.at[which, 2 + side], wo_recv.at[which, 2 + side], beside(4 - dx))

    def weight_in(which):
        for side in range(2):
            some = pl.ds(side * (BLK // 2), BLK // 2)
            wait(wo_ref.at[pl.ds((x + 2) % 4 * 4 + columns(which), 2), some], wo_recv.at[which, 2 + side])

    def contract(at, target):
        total = None
        for side in range(2):
            for d, dy in enumerate((0, 3, 1, 2)):
                core = c if side == 0 else 1 - c
                block = ((y + dy) % 4) * 4 + target * 2 + core
                part = jnp.dot(att[side, d, at, :], wo_ref[block], preferred_element_type=jnp.float32)
                total = part if total is None else total + part
        return total

    def away(m):
        at = pl.ds(m * size, size)
        for d in range(4):
            wait(att.at[1, d, at], core_recv.at[d, m])
        part_send[at, :] = contract(at, 1 - zh).astype(jnp.bfloat16)
        send(part_send.at[at], part_recv.at[at], part_sems.at[0, m], part_sems.at[1, m], across)

    def mine(m):
        at = pl.ds(m * BLK, BLK)
        own[at, :] = contract(at, zh)

    own_send(0)
    weight_out(0)
    own_send(1)
    own_send(2)
    load_wo.wait()
    load_own.wait()
    ready = 0
    for i in range(CHUNKS + 2):
        if i < CHUNKS:
            ring_in(i)
        if i + 3 < CHUNKS:
            own_send(i + 3)
        if 1 <= i <= CHUNKS:
            far_in(i - 1)
        if i == 1:
            weight_relay(0)
        if i == WEIGHT_AT:
            weight_in(0)
            weight_out(1)
        if i == CHUNKS - 1:
            weight_relay(1)
        if i >= WEIGHT_AT:
            for _ in range(2):
                if ready <= i - 2:
                    away(ready)
                    ready += 1
        if i == CHUNKS:
            weight_in(1)
            for m in range(OWN_EARLY):
                mine(m)
    for m in range(OWN_EARLY, rows // BLK):
        mine(m)
    load.wait()
    for m in range(CHUNKS):
        at = pl.ds(m * size, size)
        wait(part_recv.at[at], part_sems.at[1, m])
        for i in range(size // HD):
            row = m * (size // HD) + i
            here = pl.ds(row * HD, HD)
            resid = (
                hid[here, :].astype(jnp.float32) + (own[here, :] + part_recv[here, :].astype(jnp.float32))
            ).astype(jnp.bfloat16)
            resid_ref[here, :] = resid
            wide = resid.astype(jnp.float32)
            total = jnp.sum(wide * wide, axis=1, keepdims=True)
            sums_mine[pl.ds(row, 1), :] = jnp.transpose(jnp.broadcast_to(total, (HD, HD)))[:1, :]
    store = pltpu.make_async_copy(resid_ref, resid_out, store_sem)
    for k in range(1, 16):
        send(sums_mine, sums.at[k], sum_send.at[k], sum_recv.at[k], (rep, (tp + k) % 16))
    store.start()
    total = sums_mine[...]
    for k in range(1, 16):
        wait(sums.at[k], sum_recv.at[k])
        total = total + sums[k]
    inverse_ref[...] = lax.rsqrt(total * (1.0 / D) + norm_eps)
    store.wait()
    for made in pending:
        made.wait_send()


def finish(attended, hidden, wo_here):
    rows, width = attended.shape
    bf16, f32, dma = jnp.bfloat16, jnp.float32, pltpu.SemaphoreType.DMA
    return pl.pallas_call(
        output_kernel,
        out_shape=(jax.ShapeDtypeStruct((rows, width), bf16), jax.ShapeDtypeStruct((rows // HD, HD), f32)),
        in_specs=[anywhere(), anywhere(), anywhere()],
        out_specs=(anywhere(), vmem()),
        scratch_shapes=[
            pltpu.VMEM((rows, width), bf16),
            pltpu.VMEM((16, BLK, BLK), bf16),
            pltpu.VMEM((2, 4, rows, width), bf16),
            pltpu.VMEM((rows, width), bf16),
            pltpu.VMEM((rows, width), bf16),
            pltpu.VMEM((rows, width), f32),
            pltpu.VMEM((rows, width), bf16),
            pltpu.VMEM((rows // HD, HD), f32),
            pltpu.VMEM((16, rows // HD, HD), f32),
            dma,
            dma((4, CHUNKS)),
            dma((4, CHUNKS)),
            dma((4, CHUNKS)),
            dma((4, CHUNKS)),
            dma((2, CHUNKS)),
            dma((16,)),
            dma((16,)),
            dma,
            dma,
            dma((2, 4)),
            dma((2, 4)),
            dma,
        ],
        compiler_params=pltpu.CompilerParams(collective_id=1, has_side_effects=True, vmem_limit_bytes=VMEM_ALL),
        cost_estimate=pl.CostEstimate(flops=2 * 10**9, bytes_accessed=6 * 2**20, transcendentals=10**4),
        name="finish",
    )(attended, hidden, wo_here)


def scale_kernel(resid_in, inverse_ref, gain_ref, resid_out, normed_out, gain_row, resid, normed, in_sem, out_sem, norm_sem):
    rows, width = resid.shape
    count = in_sem.shape[0]
    size = rows // count
    loads, stores = [], []
    for i in range(count):
        at = pl.ds(i * size, size)
        loads.append(pltpu.make_async_copy(resid_in.at[at], resid.at[at], in_sem.at[i]))
        loads[-1].start()
    gain_row[...] = gain_ref[...].astype(jnp.float32).reshape(1, D)
    gain = gain_row[:, pl.ds(pl.multiple_of(lax.axis_index("tp") * width, width), width)]
    for i in range(count):
        at = pl.ds(i * size, size)
        loads[i].wait()
        stores.append(pltpu.make_async_copy(resid.at[at], resid_out.at[at], out_sem.at[i]))
        stores[-1].start()
        for row in range(i * size // HD, (i + 1) * size // HD):
            here = pl.ds(row * HD, HD)
            column = jnp.transpose(jnp.broadcast_to(inverse_ref[row : row + 1, :], (HD, HD)))
            for h in range(width // HD):
                cols = slice(h * HD, (h + 1) * HD)
                normed[here, cols] = (
                    resid[here, cols].astype(jnp.float32) * column * gain[:, cols]
                ).astype(jnp.bfloat16)
        stores.append(pltpu.make_async_copy(normed.at[at], normed_out.at[at], norm_sem.at[i]))
        stores[-1].start()
    for store in stores:
        store.wait()


def scale(resid, inverse, out_gain):
    rows, width = resid.shape
    bf16, dma = jnp.bfloat16, pltpu.SemaphoreType.DMA
    return pl.pallas_call(
        scale_kernel,
        out_shape=(jax.ShapeDtypeStruct((rows, width), bf16), jax.ShapeDtypeStruct((rows, width), bf16)),
        in_specs=[anywhere(), vmem(), vmem()],
        out_specs=(anywhere(), anywhere()),
        scratch_shapes=[
            pltpu.VMEM((1, D), jnp.float32),
            pltpu.VMEM((rows, width), bf16),
            pltpu.VMEM((rows, width), bf16),
            dma((4,)),
            dma((4,)),
            dma((4,)),
        ],
        compiler_params=pltpu.CompilerParams(vmem_limit_bytes=VMEM_ALL),
        cost_estimate=pl.CostEstimate(flops=10**6, bytes_accessed=3 * 2**19, transcendentals=0),
        name="scale",
    )(resid, inverse, out_gain)


def body(hidden, norm_gain, w_query, w_keyval, w_output, cache, lengths, prefix, out_gain):
    powers = np.arange(HD) % (HD // 2) * 2.0 / HD
    freqs = jnp.asarray((rope_base**-powers).astype(np.float32).reshape(1, HD))
    q, k, v, wo_here = project(lengths, prefix, hidden, norm_gain, freqs, w_query, w_keyval.T, w_output)
    attended = attend(lengths, prefix, q, k, v, cache)
    resid, inverse = finish(attended, hidden, wo_here)
    return scale(resid, inverse, out_gain)


def solution(mesh):
    placed = (
        P("rep", None),
        P(),
        P("rep", "tp"),
        P("rep", "tp"),
        P("tp", "rep"),
        P("rep", None),
        P("rep", None),
        P("rep"),
        P(),
    )
    return jax.shard_map(
        body,
        mesh=mesh,
        in_specs=placed,
        out_specs=(P("rep", "tp"), P("rep", "tp")),
        check_vma=False,
    )
```

```python
import functools
import math

import jax
import jax.numpy as jnp
import numpy as np
from jax import lax
from jax.experimental import pallas as pl
from jax.experimental.pallas import tpu as pltpu
from jax.sharding import PartitionSpec as P

H = 32
KV = 4
HD = 128
REQ_REP = 4
PREF_MAX = 512

norm_eps = 1e-05
rope_base = 5000000.0
TQ = 256
NEG_MASK = -1e30
VMEM_ALL = 67043328
CHUNKS = 8
WEIGHT_AT = 3
OWN_EARLY = 3


MESH = pl.DeviceIdType.MESH
D = 4096
BLK = 256


def place():
    rep, tp = lax.axis_index("rep"), lax.axis_index("tp")
    return rep, tp, rep // 4, rep % 4, tp // 8, (tp // 2) % 4, tp % 2


def line_order(z):
    power = 1 + 3 * z + 9 * (z * (z - 1) // 2) + 27 * (z * (z - 1) * (z - 2) // 6)
    tables = []
    for picks in ((1, 0, 1, 2), (2, 2, 3, 1), (3, 3, 0, 0)):
        tables.append(sum(pick * 4**i for i, pick in enumerate(picks)))
    return [z] + [(table // power) % 4 for table in tables]


def signal(sem, device):
    pl.semaphore_signal(sem, inc=1, device_id=device, device_id_type=MESH)


class Gather:
    def __init__(self, own, full, recv, send, half, ring=True):
        self.own, self.full, self.recv, self.send, self.half = own, full, recv, send, half
        self.in_ring = ring
        self.rep, self.tp, self.x, self.z = place()[:4]
        self.order = line_order(self.z)
        self.right = ((self.x + 1) % 4) * 4
        self.left = ((self.x + 3) % 4) * 4
        self.far = ((self.x + 2) % 4) * 4
        self.pending = []

    def copy(self, src, dst, slot, sem, rep, cond=None):
        made = pltpu.make_async_remote_copy(
            src_ref=src,
            dst_ref=dst,
            send_sem=self.send.at[slot],
            recv_sem=sem,
            device_id=(rep, self.tp),
            device_id_type=MESH,
        )
        if cond is None:
            made.start()
        else:
            pl.when(cond)(made.start)
        self.pending.append((made, cond))

    def arrived(self, index, block):
        ref = self.full.at[block]
        pltpu.make_async_copy(ref, ref, self.recv.at[index, block]).wait()

    def line(self, k):
        zo = self.order[k]
        block = self.x * 4 + zo if self.in_ring else zo
        dst, sem = self.full.at[block], self.recv.at[0, block]
        if k == 0:
            src = self.own
            onward, back = self.z < 3, self.z > 0
        else:
            self.arrived(0, block)
            src = dst
            onward, back = (zo < self.z) & (self.z < 3), (zo > self.z) & (self.z > 0)
        self.copy(src, dst, 6 * k, sem, self.x * 4 + lax.min(self.z + 1, 3), onward)
        self.copy(src, dst, 6 * k + 1, sem, self.x * 4 + lax.max(self.z - 1, 0), back)
        if not self.in_ring:
            return
        self.copy(src, dst, 6 * k + 2, sem, self.right + self.z)
        self.copy(src, dst, 6 * k + 3, sem, self.left + self.z)

    def ring(self, k, side):
        zo = self.order[k]
        block = (self.left if side == 0 else self.right) + zo
        self.arrived(0, block)
        part = pl.ds(0, self.half) if side == 0 else pl.ds(self.half, self.half)
        ref = self.full.at[block, part]
        target = (self.right if side == 0 else self.left) + self.z
        self.copy(ref, ref, 6 * k + 4 + side, self.recv.at[side, block], target)
        return block

    def opposite(self, k):
        block = self.far + self.order[k]
        for side in range(2):
            ref = self.full.at[block, pl.ds(side * self.half, self.half)]
            pltpu.make_async_copy(ref, ref, self.recv.at[side, block]).wait()
        return block

    def drain(self):
        for made, cond in self.pending:
            if cond is None:
                made.wait_send()
            else:
                pl.when(cond)(made.wait_send)


def project_kernel(
    lens_ref, pref_ref, hidden_ref, gain_ref, freq_ref, wq_ref, wkv_ref, wo_ref,
    q_out, k_out, v_out, wo_out,
    gain, q_ref, k_ref, v_ref, hid, x3, full_q, full_s, full_w, turned, qacc, kacc, cosine, sine, mine, other,
    hid_sem, recv_q, send_q, recv_r, send_r, recv_s, send_s, recv_w, send_w, kv_send, kv_recv, perm_send, perm_recv, swap_sem, out_sem, own_sem, store_sem,
):
    rep, tp, x, z, zh, y, c = place()
    rows = hid.shape[0]
    count = hid_sem.shape[0]
    chunk = rows // count
    loads = []
    for i in range(count):
        at = pl.ds(i * chunk, chunk)
        loads.append(pltpu.make_async_copy(hidden_ref.at[at], hid.at[at], hid_sem.at[i]))
        loads[-1].start()
    own_load = pltpu.make_async_copy(wq_ref, full_q.at[rep], own_sem)
    own_load.start()

    zh_t = x // 2
    perm_dst = (y * 4 + zh_t * 2 + c, zh * 8 + ((x % 2) * 2 + z // 2) * 2 + z % 2)
    perm_src = (((z // 2) * 2 + y // 2) * 4 + (y % 2) * 2 + c, zh * 8 + x * 2 + z % 2)
    perm_away = (perm_dst[0] != rep) | (perm_dst[1] != tp)
    barrier = pltpu.get_barrier_semaphore()
    line_right, line_left = x * 4 + lax.min(z + 1, 3), x * 4 + lax.max(z - 1, 0)

    pl.when(z < 3)(lambda: signal(barrier, (line_right, tp)))
    pl.when(z > 0)(lambda: signal(barrier, (line_left, tp)))
    signal(barrier, (((x + 1) % 4) * 4 + z, tp))
    signal(barrier, (((x + 3) % 4) * 4 + z, tp))
    signal(barrier, (rep, tp + 1 - 2 * c))
    pl.when(perm_away)(lambda: signal(barrier, perm_src))
    for j in range(8):
        source = c * 8 + j
        pl.when(source != tp)(lambda source=source: signal(barrier, (rep, source)))
    shape = (4 * 16, 4 * 16)
    out_row, in_col = lax.broadcasted_iota(jnp.int32, shape, 0), lax.broadcasted_iota(jnp.int32, shape, 1)
    pick = ((out_row % 16) * KV + out_row // 16 == in_col).astype(jnp.float32).astype(jnp.bfloat16)
    turned[...] = lax.dot_general(
        pick, wkv_ref[...], (((1,), (0,)), ((), ())), preferred_element_type=jnp.float32
    ).astype(jnp.bfloat16)

    starts, first_token = [], 0
    for request in range(REQ_REP):
        starts.append(first_token)
        first_token = first_token + lens_ref[0, request]

    def angles(i, _):
        at = pl.ds(pl.multiple_of(i * 128, 128), 128)
        token = i * 128 + lax.broadcasted_iota(jnp.int32, (128, HD), 0)
        position = jnp.zeros((128, HD), jnp.int32)
        for request in range(REQ_REP):
            shift = pref_ref[request] - starts[request]
            position = jnp.where(token >= starts[request], token + shift, position)
        angle = position.astype(jnp.float32) * freq_ref[...]
        lane = lax.broadcasted_iota(jnp.int32, (128, HD), 1)
        cosine[at, :] = jnp.cos(angle)
        wave = jnp.sin(angle)
        sine[at, :] = jnp.where(lane < HD // 2, -wave, wave)
        return 0

    gain[...] = gain_ref[...].astype(jnp.float32).reshape(1, D)

    line_peers = (lax.min(z + 1, 3) - z) + (z - lax.max(z - 1, 0))
    pl.semaphore_wait(barrier, 10 + line_peers + perm_away.astype(jnp.int32) + (c + zh) % 2)

    low, high = pl.ds(0, BLK // 2), pl.ds(BLK // 2, BLK // 2)
    stream_q = Gather(wq_ref.at[low], full_q.at[:, low], recv_q, send_q, BLK // 4)
    stream_r = Gather(wq_ref.at[high], full_q.at[:, high], recv_r, send_r, BLK // 4)
    stream_s = Gather(full_s.at[rep], full_s, recv_s, send_s, full_s.shape[1] // 2)
    stream_w = Gather(full_w.at[z], full_w, recv_w, send_w, 0, False)
    stream_q.line(0)
    stream_r.line(0)

    def piece(head, which):
        target = (head // 2) * 8 + (2 * (head % 2) + which) * 2 + zh
        from_ref = turned.at[pl.ds(head * 16, 16)]
        to_ref = full_s.at[rep, pl.ds(pl.multiple_of((tp % 8) * 16, 16), 16)]
        away = target != tp
        made = pltpu.make_async_remote_copy(
            src_ref=from_ref, dst_ref=to_ref, send_sem=kv_send.at[head * 2 + which], recv_sem=kv_recv.at[tp % 8],
            device_id=(rep, target), device_id_type=MESH,
        )
        here = pltpu.make_async_copy(from_ref, to_ref, kv_recv.at[tp % 8])
        pl.when(away)(made.start)
        pl.when(jnp.logical_not(away))(here.start)
        return made, away

    pieces = [piece(head, which) for head in range(KV) for which in range(2)]

    wo_dst = full_w.at[perm_dst[0] % 4]
    permute = pltpu.make_async_remote_copy(
        src_ref=wo_ref, dst_ref=wo_dst, send_sem=perm_send, recv_sem=perm_recv,
        device_id=perm_dst, device_id_type=MESH,
    )
    stay = pltpu.make_async_copy(wo_ref, wo_dst, perm_recv)
    pl.when(perm_away)(permute.start)
    pl.when(jnp.logical_not(perm_away))(stay.start)

    def norm(i):
        loads[i].wait()

        def some(j, _):
            at = pl.ds(pl.multiple_of(i * chunk + j * 16, 16), 16)
            wide = hid[at, :].astype(jnp.float32)
            meansq = jnp.sum(wide * wide, axis=1, keepdims=True) * (1.0 / D)
            scaled = wide * lax.rsqrt(meansq + norm_eps)
            for b in range(D // BLK):
                cols = slice(b * BLK, (b + 1) * BLK)
                x3[b, at, :] = (scaled[:, cols] * gain[:, cols]).astype(jnp.bfloat16)
            return 0

        lax.fori_loop(0, chunk // 16, some, 0)

    def use_q(block, own=False):
        for i in range(rows // BLK):
            at = pl.ds(i * BLK, BLK)
            part = jnp.dot(x3[block, at, :], full_q[block], preferred_element_type=jnp.float32)
            qacc[at, :] = part if own else qacc[at, :] + part

    def use_s(block, own=False):
        for i in range(rows // BLK):
            at = pl.ds(i * BLK, BLK)
            part = lax.dot_general(
                x3[block, at, :], full_s[block, :HD, :], (((1,), (1,)), ((), ())),
                preferred_element_type=jnp.float32,
            )
            kacc[at, :] = part if own else kacc[at, :] + part

    norm(0)
    lax.fori_loop(0, rows // 128, angles, 0)
    norm(1)
    stream_q.line(1)
    stream_r.line(1)
    for j in range(8):
        ref = full_s.at[rep, pl.ds(j * 16, 16)]
        pltpu.make_async_copy(ref, ref, kv_recv.at[j]).wait()
    stream_s.line(0)
    norm(2)
    norm(3)
    stream_s.line(1)
    norm(4)
    stream_s.line(2)
    stream_q.line(2)
    stream_r.line(2)
    norm(5)
    norm(6)
    stream_s.line(3)
    stream_q.line(3)
    stream_r.line(3)
    norm(7)
    own_load.wait()
    use_q(rep, True)
    use_s(rep, True)
    for k in range(4):
        lefts_s, rights_s = stream_s.ring(k, 0), stream_s.ring(k, 1)
        lefts, rights = stream_q.ring(k, 0), stream_q.ring(k, 1)
        stream_r.ring(k, 0)
        stream_r.ring(k, 1)
        if k > 0:
            own_block = x * 4 + stream_q.order[k]
            use_q(own_block)
            use_s(own_block)
        for block in (lefts, rights):
            use_q(block)
        for block in (lefts_s, rights_s):
            use_s(block)
        if k > 0:
            stream_r.opposite(k - 1)
            use_q(stream_q.opposite(k - 1))
            use_s(stream_s.opposite(k - 1))
        if k == 0:
            own_wo = full_w.at[z]
            pltpu.make_async_copy(own_wo, own_wo, perm_recv).wait()
        stream_w.line(k)
    flush = pltpu.make_async_copy(full_w, wo_out, out_sem)
    flush.start()
    use_s(stream_s.opposite(3))

    fresh = kacc[...].astype(jnp.bfloat16).astype(jnp.float32)
    turned_key = fresh * cosine[...] + pltpu.roll(fresh, HD // 2, 1) * sine[...]
    mine[...] = jnp.where(c == 0, turned_key, fresh).astype(jnp.bfloat16)
    swap = pltpu.make_async_remote_copy(
        src_ref=mine, dst_ref=other, send_sem=swap_sem.at[0], recv_sem=swap_sem.at[1],
        device_id=(rep, tp + 1 - 2 * c), device_id_type=MESH,
    )
    stream_r.opposite(3)
    use_q(stream_q.opposite(3))
    swap.start()
    for h in range(q_ref.shape[1] // HD):
        cols = slice(h * HD, (h + 1) * HD)
        u = qacc[:, cols]
        q_ref[:, cols] = (u * cosine[...] + pltpu.roll(u, HD // 2, 1) * sine[...]).astype(jnp.bfloat16)
    store_q = pltpu.make_async_copy(q_ref, q_out, store_sem.at[0])
    store_q.start()
    for made, away in pieces:
        pl.when(away)(made.wait_send)
    pl.when(perm_away)(permute.wait_send)
    stream_q.drain()
    stream_r.drain()
    stream_s.drain()
    stream_w.drain()
    swap.wait()

    @pl.when(c == 0)
    def _():
        k_ref[...] = mine[...]
        v_ref[...] = other[...]

    @pl.when(c != 0)
    def _():
        k_ref[...] = other[...]
        v_ref[...] = mine[...]

    store_k = pltpu.make_async_copy(k_ref, k_out, store_sem.at[1])
    store_v = pltpu.make_async_copy(v_ref, v_out, store_sem.at[2])
    store_k.start()
    store_v.start()
    store_q.wait()
    store_k.wait()
    store_v.wait()
    flush.wait()


def vmem():
    return pl.BlockSpec(memory_space=pltpu.VMEM)


def smem():
    return pl.BlockSpec(memory_space=pltpu.SMEM)


def anywhere():
    return pl.BlockSpec(memory_space=pl.ANY)


def project(lengths, prefix, hidden, norm_gain, freqs, w_query, w_keyval, w_output):
    rows = hidden.shape[0]
    bf16, f32, dma = jnp.bfloat16, jnp.float32, pltpu.SemaphoreType.DMA
    return pl.pallas_call(
        project_kernel,
        out_shape=(
            jax.ShapeDtypeStruct((rows, BLK), bf16),
            jax.ShapeDtypeStruct((rows, HD), bf16),
            jax.ShapeDtypeStruct((rows, HD), bf16),
            jax.ShapeDtypeStruct((4, BLK, BLK), bf16),
        ),
        in_specs=[smem(), smem(), anywhere(), vmem(), vmem(), anywhere(), vmem(), anywhere()],
        out_specs=(anywhere(), anywhere(), anywhere(), anywhere()),
        scratch_shapes=[
            pltpu.VMEM((1, D), f32),
            pltpu.VMEM((rows, BLK), bf16),
            pltpu.VMEM((rows, HD), bf16),
            pltpu.VMEM((rows, HD), bf16),
            pltpu.VMEM((rows, D), bf16),
            pltpu.VMEM((16, rows, BLK), bf16),
            pltpu.VMEM((16, BLK, BLK), bf16),
            pltpu.VMEM((16, HD, BLK), bf16),
            pltpu.VMEM((4, BLK, BLK), bf16),
            pltpu.VMEM((64, BLK), bf16),
            pltpu.VMEM((rows, BLK), f32),
            pltpu.VMEM((rows, HD), f32),
            pltpu.VMEM((rows, HD), f32),
            pltpu.VMEM((rows, HD), f32),
            pltpu.VMEM((rows, HD), bf16),
            pltpu.VMEM((rows, HD), bf16),
            dma((8,)),
            dma((2, 16)),
            dma((24,)),
            dma((2, 16)),
            dma((24,)),
            dma((2, 16)),
            dma((24,)),
            dma((1, 4)),
            dma((24,)),
            dma((8,)),
            dma((8,)),
            dma,
            dma,
            dma((2,)),
            dma,
            dma,
            dma((3,)),
        ],
        compiler_params=pltpu.CompilerParams(collective_id=0, has_side_effects=True, vmem_limit_bytes=VMEM_ALL),
        cost_estimate=pl.CostEstimate(flops=3 * 10**9, bytes_accessed=12 * 2**20, transcendentals=10**6),
        name="project",
    )(lengths, prefix, hidden, norm_gain, freqs, w_query, w_keyval, w_output)


def attention_kernel(
    lens_ref, pref_ref, q_ref, k_ref, v_ref, cache_ref, o_ref, qs, ks, vs, stored, outs, sems, out_sem
):
    rows, width = q_ref.shape
    column = pl.multiple_of(lax.axis_index("tp") // 4 * 2 * HD, 2 * HD)
    inside = pl.ds(0, rows)
    loads = [
        pltpu.make_async_copy(q_ref, qs.at[inside], sems.at[REQ_REP]),
        pltpu.make_async_copy(k_ref, ks.at[inside], sems.at[REQ_REP + 1]),
        pltpu.make_async_copy(v_ref, vs.at[inside], sems.at[REQ_REP + 2]),
    ]

    def fetch(request):
        at = pl.ds(pl.multiple_of(request * PREF_MAX, PREF_MAX), PREF_MAX)
        return pltpu.make_async_copy(cache_ref.at[at, pl.ds(column, 2 * HD)], stored.at[at, :], sems.at[request])

    fetch(0).start()
    for load in loads:
        load.start()
    for request in range(1, REQ_REP):
        fetch(request).start()
    spare = pl.ds(rows, qs.shape[0] - rows)
    ks[spare, :] = jnp.zeros((TQ, HD), jnp.bfloat16)
    vs[spare, :] = jnp.zeros((TQ, HD), jnp.bfloat16)
    for load in loads:
        load.wait()
    factor = HD ** (-0.5) * math.log2(math.e)
    nt = (((1,), (1,)), ((), ()))
    lane = lax.broadcasted_iota(jnp.int32, (TQ, TQ), 1)
    row = lax.broadcasted_iota(jnp.int32, (TQ, TQ), 0)

    def tile(start, aligned, base, prefix, index, parts):
        rows_at = pl.ds(pl.multiple_of(aligned + index * TQ, 16), TQ)
        for h in range(width // HD):
            cols = slice(h * HD, (h + 1) * HD)
            q = qs[rows_at, cols]
            scores, values = [], []
            for part in range(parts):
                at = pl.ds(pl.multiple_of(base + part * TQ, TQ), TQ)
                score = lax.dot_general(q, stored[at, :HD], nt, preferred_element_type=jnp.float32)
                if part == parts - 1:
                    score = jnp.where(lane < prefix - part * TQ, score, NEG_MASK)
                scores.append(score)
                values.append((stored, at, slice(HD, 2 * HD)))
            for part in range(index + 1):
                at = pl.ds(pl.multiple_of(aligned + part * TQ, 16), TQ)
                score = lax.dot_general(q, ks[at, :], nt, preferred_element_type=jnp.float32)
                if part == index:
                    score = jnp.where(lane <= row, score, NEG_MASK)
                if part == 0:
                    score = jnp.where(lane >= start - aligned, score, NEG_MASK)
                scores.append(score)
                values.append((vs, at, slice(0, HD)))
            peak = scores[0]
            for score in scores[1:]:
                peak = jnp.maximum(peak, score)
            peak = jnp.max(peak, axis=1, keepdims=True)
            total, gathered = None, None
            for score, (ref, at, which) in zip(scores, values):
                e = jnp.exp2((score - peak) * factor)
                total = e if total is None else total + e
                part = jnp.dot(e.astype(jnp.bfloat16), ref[at, which], preferred_element_type=jnp.float32)
                gathered = part if gathered is None else gathered + part
            result = gathered / jnp.sum(total, axis=1, keepdims=True)
            if index == 0:
                keep = row[:, :HD] + aligned < start
                result = jnp.where(keep, outs[rows_at, cols].astype(jnp.float32), result)
            outs[rows_at, cols] = result.astype(jnp.bfloat16)

    def one(request, start):
        end, prefix = start + lens_ref[0, request], pref_ref[request]
        aligned = start // 16 * 16
        base = request * PREF_MAX
        fetch(request).wait()
        for index in range(3):
            for parts in (1, 2):
                fits = (prefix <= TQ) if parts == 1 else (prefix > TQ)
                pl.when((aligned + index * TQ < end) & fits)(
                    functools.partial(tile, start, aligned, base, prefix, index, parts)
                )
        return end

    lax.fori_loop(0, REQ_REP, one, 0)
    store = pltpu.make_async_copy(outs.at[inside], o_ref, out_sem)
    store.start()
    store.wait()


def attend(lengths, prefix, q, k, v, cache):
    rows, width = q.shape
    bf16, dma = jnp.bfloat16, pltpu.SemaphoreType.DMA
    return pl.pallas_call(
        attention_kernel,
        out_shape=jax.ShapeDtypeStruct((rows, width), bf16),
        in_specs=[smem(), smem(), anywhere(), anywhere(), anywhere(), anywhere()],
        out_specs=anywhere(),
        scratch_shapes=[
            pltpu.VMEM((rows + TQ, width), bf16),
            pltpu.VMEM((rows + TQ, HD), bf16),
            pltpu.VMEM((rows + TQ, HD), bf16),
            pltpu.VMEM((REQ_REP * PREF_MAX, 2 * HD), bf16),
            pltpu.VMEM((rows + TQ, width), bf16),
            dma((REQ_REP + 3,)),
            dma,
        ],
        compiler_params=pltpu.CompilerParams(vmem_limit_bytes=VMEM_ALL),
        cost_estimate=pl.CostEstimate(flops=2 * 10**9, bytes_accessed=3 * 2**20, transcendentals=2 * 10**6),
        name="attention",
    )(lengths, prefix, q, k, v, cache)


def output_kernel(
    att_ref, hidden_ref, wo_here,
    resid_out, inverse_ref,
    resid_ref, wo_ref, att, part_send, part_recv, own, hid, sums_mine, sums,
    hid_sem, ring_send, ring_recv, core_send, core_recv, part_sems, sum_send, sum_recv, wo_sem, own_sem, wo_send, wo_recv, store_sem,
):
    rep, tp, x, z, zh, y, c = place()
    rows, width = hid.shape
    load = pltpu.make_async_copy(
        hidden_ref.at[:, pl.ds(pl.multiple_of(tp * width, width), width)], hid, hid_sem
    )
    load.start()
    load_wo = pltpu.make_async_copy(wo_here, wo_ref.at[pl.ds(x * 4, 4)], wo_sem)
    load_wo.start()
    load_own = pltpu.make_async_copy(att_ref, att.at[0, 0], own_sem)
    load_own.start()
    barrier = pltpu.get_barrier_semaphore()
    for k in range(1, 16):
        signal(barrier, (rep, (tp + k) % 16))
    for dx in (1, 3):
        signal(barrier, ((x + dx) % 4 * 4 + z, tp))
    pl.semaphore_wait(barrier, 17)

    def at_y(to):
        return (rep, zh * 8 + (to % 4) * 2 + c)

    partner = (rep, tp + 1 - 2 * c)
    across = (rep, (tp + 8) % 16)
    size = rows // CHUNKS
    half = size // 2
    pending = []

    def send(src, dst, ssem, rsem, device):
        made = pltpu.make_async_remote_copy(
            src_ref=src, dst_ref=dst, send_sem=ssem, recv_sem=rsem, device_id=device, device_id_type=MESH
        )
        made.start()
        pending.append(made)

    def wait(ref, sem):
        pltpu.make_async_copy(ref, ref, sem).wait()

    def own_send(m):
        at = pl.ds(m * size, size)
        src = att_ref.at[at]
        send(src, att.at[0, 1, at], ring_send.at[0, m], ring_recv.at[0, m], at_y(y + 1))
        send(src, att.at[0, 2, at], ring_send.at[1, m], ring_recv.at[1, m], at_y(y + 3))
        send(src, att.at[1, 0, at], core_send.at[0, m], core_recv.at[0, m], partner)

    def ring_in(m):
        at = pl.ds(m * size, size)
        for side in range(2):
            ref = att.at[0, 1 + side, at]
            wait(ref, ring_recv.at[side, m])
            part = pl.ds(m * size + side * half, half)
            send(
                att.at[0, 1 + side, part], att.at[0, 3, part],
                ring_send.at[2 + side, m], ring_recv.at[2 + side, m], at_y(y + 1 + 2 * side),
            )
            send(ref, att.at[1, 1 + side, at], core_send.at[1 + side, m], core_recv.at[1 + side, m], partner)

    def far_in(m):
        for side in range(2):
            wait(att.at[0, 3, pl.ds(m * size + side * half, half)], ring_recv.at[2 + side, m])
        ref = att.at[0, 3, pl.ds(m * size, size)]
        send(ref, att.at[1, 3, pl.ds(m * size, size)], core_send.at[3, m], core_recv.at[3, m], partner)

    def columns(which):
        return (1 - zh if which == 0 else zh) * 2

    def beside(dx):
        return ((x + dx) % 4 * 4 + z, tp)

    def weight_out(which):
        for side, dx in enumerate((1, 3)):
            send(
                wo_here.at[pl.ds(columns(which), 2)], wo_ref.at[pl.ds(x * 4 + columns(which), 2)],
                wo_send.at[which, side], wo_recv.at[which, side], beside(dx),
            )

    def weight_relay(which):
        for side, dx in enumerate((3, 1)):
            at = pl.ds((x + dx) % 4 * 4 + columns(which), 2)
            wait(wo_ref.at[at], wo_recv.at[which, side])
            some = wo_ref.at[at, pl.ds(side * (BLK // 2), BLK // 2)]
            send(some, some, wo_send.at[which, 2 + side], wo_recv.at[which, 2 + side], beside(4 - dx))

    def weight_in(which):
        for side in range(2):
            some = pl.ds(side * (BLK // 2), BLK // 2)
            wait(wo_ref.at[pl.ds((x + 2) % 4 * 4 + columns(which), 2), some], wo_recv.at[which, 2 + side])

    def contract(at, target):
        total = None
        for side in range(2):
            for d, dy in enumerate((0, 3, 1, 2)):
                core = c if side == 0 else 1 - c
                block = ((y + dy) % 4) * 4 + target * 2 + core
                part = jnp.dot(att[side, d, at, :], wo_ref[block], preferred_element_type=jnp.float32)
                total = part if total is None else total + part
        return total

    def away(m):
        at = pl.ds(m * size, size)
        for d in range(4):
            wait(att.at[1, d, at], core_recv.at[d, m])
        part_send[at, :] = contract(at, 1 - zh).astype(jnp.bfloat16)
        send(part_send.at[at], part_recv.at[at], part_sems.at[0, m], part_sems.at[1, m], across)

    def mine(m):
        at = pl.ds(m * BLK, BLK)
        own[at, :] = contract(at, zh)

    own_send(0)
    weight_out(0)
    own_send(1)
    own_send(2)
    load_wo.wait()
    load_own.wait()
    ready = 0
    for i in range(CHUNKS + 2):
        if i < CHUNKS:
            ring_in(i)
        if i + 3 < CHUNKS:
            own_send(i + 3)
        if 1 <= i <= CHUNKS:
            far_in(i - 1)
        if i == 1:
            weight_relay(0)
        if i == WEIGHT_AT:
            weight_in(0)
            weight_out(1)
        if i == CHUNKS - 1:
            weight_relay(1)
        if i >= WEIGHT_AT:
            for _ in range(2):
                if ready <= i - 2:
                    away(ready)
                    ready += 1
        if i == CHUNKS:
            weight_in(1)
            for m in range(OWN_EARLY):
                mine(m)
    for m in range(OWN_EARLY, rows // BLK):
        mine(m)
    load.wait()
    for m in range(CHUNKS):
        at = pl.ds(m * size, size)
        wait(part_recv.at[at], part_sems.at[1, m])
        for i in range(size // HD):
            row = m * (size // HD) + i
            here = pl.ds(row * HD, HD)
            resid = (
                hid[here, :].astype(jnp.float32) + (own[here, :] + part_recv[here, :].astype(jnp.float32))
            ).astype(jnp.bfloat16)
            resid_ref[here, :] = resid
            wide = resid.astype(jnp.float32)
            total = jnp.sum(wide * wide, axis=1, keepdims=True)
            sums_mine[pl.ds(row, 1), :] = jnp.transpose(jnp.broadcast_to(total, (HD, HD)))[:1, :]
    store = pltpu.make_async_copy(resid_ref, resid_out, store_sem)
    for k in range(1, 16):
        send(sums_mine, sums.at[k], sum_send.at[k], sum_recv.at[k], (rep, (tp + k) % 16))
    store.start()
    total = sums_mine[...]
    for k in range(1, 16):
        wait(sums.at[k], sum_recv.at[k])
        total = total + sums[k]
    inverse_ref[...] = lax.rsqrt(total * (1.0 / D) + norm_eps)
    store.wait()
    for made in pending:
        made.wait_send()


def finish(attended, hidden, wo_here):
    rows, width = attended.shape
    bf16, f32, dma = jnp.bfloat16, jnp.float32, pltpu.SemaphoreType.DMA
    return pl.pallas_call(
        output_kernel,
        out_shape=(jax.ShapeDtypeStruct((rows, width), bf16), jax.ShapeDtypeStruct((rows // HD, HD), f32)),
        in_specs=[anywhere(), anywhere(), anywhere()],
        out_specs=(anywhere(), vmem()),
        scratch_shapes=[
            pltpu.VMEM((rows, width), bf16),
            pltpu.VMEM((16, BLK, BLK), bf16),
            pltpu.VMEM((2, 4, rows, width), bf16),
            pltpu.VMEM((rows, width), bf16),
            pltpu.VMEM((rows, width), bf16),
            pltpu.VMEM((rows, width), f32),
            pltpu.VMEM((rows, width), bf16),
            pltpu.VMEM((rows // HD, HD), f32),
            pltpu.VMEM((16, rows // HD, HD), f32),
            dma,
            dma((4, CHUNKS)),
            dma((4, CHUNKS)),
            dma((4, CHUNKS)),
            dma((4, CHUNKS)),
            dma((2, CHUNKS)),
            dma((16,)),
            dma((16,)),
            dma,
            dma,
            dma((2, 4)),
            dma((2, 4)),
            dma,
        ],
        compiler_params=pltpu.CompilerParams(collective_id=1, has_side_effects=True, vmem_limit_bytes=VMEM_ALL),
        cost_estimate=pl.CostEstimate(flops=2 * 10**9, bytes_accessed=6 * 2**20, transcendentals=10**4),
        name="finish",
    )(attended, hidden, wo_here)


def scale_kernel(resid_in, inverse_ref, gain_ref, resid_out, normed_out, gain_row, resid, normed, in_sem, out_sem, norm_sem):
    rows, width = resid.shape
    count = in_sem.shape[0]
    size = rows // count
    loads, stores = [], []
    for i in range(count):
        at = pl.ds(i * size, size)
        loads.append(pltpu.make_async_copy(resid_in.at[at], resid.at[at], in_sem.at[i]))
        loads[-1].start()
    gain_row[...] = gain_ref[...].astype(jnp.float32).reshape(1, D)
    gain = gain_row[:, pl.ds(pl.multiple_of(lax.axis_index("tp") * width, width), width)]
    for i in range(count):
        at = pl.ds(i * size, size)
        loads[i].wait()
        stores.append(pltpu.make_async_copy(resid.at[at], resid_out.at[at], out_sem.at[i]))
        stores[-1].start()
        for row in range(i * size // HD, (i + 1) * size // HD):
            here = pl.ds(row * HD, HD)
            column = jnp.transpose(jnp.broadcast_to(inverse_ref[row : row + 1, :], (HD, HD)))
            for h in range(width // HD):
                cols = slice(h * HD, (h + 1) * HD)
                normed[here, cols] = (
                    resid[here, cols].astype(jnp.float32) * column * gain[:, cols]
                ).astype(jnp.bfloat16)
        stores.append(pltpu.make_async_copy(normed.at[at], normed_out.at[at], norm_sem.at[i]))
        stores[-1].start()
    for store in stores:
        store.wait()


def scale(resid, inverse, out_gain):
    rows, width = resid.shape
    bf16, dma = jnp.bfloat16, pltpu.SemaphoreType.DMA
    return pl.pallas_call(
        scale_kernel,
        out_shape=(jax.ShapeDtypeStruct((rows, width), bf16), jax.ShapeDtypeStruct((rows, width), bf16)),
        in_specs=[anywhere(), vmem(), vmem()],
        out_specs=(anywhere(), anywhere()),
        scratch_shapes=[
            pltpu.VMEM((1, D), jnp.float32),
            pltpu.VMEM((rows, width), bf16),
            pltpu.VMEM((rows, width), bf16),
            dma((4,)),
            dma((4,)),
            dma((4,)),
        ],
        compiler_params=pltpu.CompilerParams(vmem_limit_bytes=VMEM_ALL),
        cost_estimate=pl.CostEstimate(flops=10**6, bytes_accessed=3 * 2**19, transcendentals=0),
        name="scale",
    )(resid, inverse, out_gain)


def body(hidden, norm_gain, w_query, w_keyval, w_output, cache, lengths, prefix, out_gain):
    powers = np.arange(HD) % (HD // 2) * 2.0 / HD
    freqs = jnp.asarray((rope_base**-powers).astype(np.float32).reshape(1, HD))
    q, k, v, wo_here = project(lengths, prefix, hidden, norm_gain, freqs, w_query, w_keyval.T, w_output)
    attended = attend(lengths, prefix, q, k, v, cache)
    resid, inverse = finish(attended, hidden, wo_here)
    return scale(resid, inverse, out_gain)


def solution(mesh):
    placed = (
        P("rep", None),
        P(),
        P("rep", "tp"),
        P("rep", "tp"),
        P("tp", "rep"),
        P("rep", None),
        P("rep", None),
        P("rep"),
        P(),
    )
    return jax.shard_map(
        body,
        mesh=mesh,
        in_specs=placed,
        out_specs=(P("rep", "tp"), P("rep", "tp")),
        check_vma=False,
    )
```

```python
import functools
import math

import jax
import jax.numpy as jnp
import numpy as np
from jax import lax
from jax.experimental import pallas as pl
from jax.experimental.pallas import tpu as pltpu
from jax.sharding import PartitionSpec as P

H = 32
KV = 4
HD = 128
REQ_REP = 4
PREF_MAX = 512

norm_eps = 1e-05
rope_base = 5000000.0
TQ = 256
NEG_MASK = -1e30
VMEM_ALL = 67043328
CHUNKS = 8
WEIGHT_AT = 3
OWN_EARLY = 3


MESH = pl.DeviceIdType.MESH
D = 4096
BLK = 256


def place():
    rep, tp = lax.axis_index("rep"), lax.axis_index("tp")
    return rep, tp, rep // 4, rep % 4, tp // 8, (tp // 2) % 4, tp % 2


def line_order(z):
    power = 1 + 3 * z + 9 * (z * (z - 1) // 2) + 27 * (z * (z - 1) * (z - 2) // 6)
    tables = []
    for picks in ((1, 0, 1, 2), (2, 2, 3, 1), (3, 3, 0, 0)):
        tables.append(sum(pick * 4**i for i, pick in enumerate(picks)))
    return [z] + [(table // power) % 4 for table in tables]


def signal(sem, device):
    pl.semaphore_signal(sem, inc=1, device_id=device, device_id_type=MESH)


class Gather:
    def __init__(self, own, full, recv, send, half, ring=True):
        self.own, self.full, self.recv, self.send, self.half = own, full, recv, send, half
        self.in_ring = ring
        self.rep, self.tp, self.x, self.z = place()[:4]
        self.order = line_order(self.z)
        self.right = ((self.x + 1) % 4) * 4
        self.left = ((self.x + 3) % 4) * 4
        self.far = ((self.x + 2) % 4) * 4
        self.pending = []

    def copy(self, src, dst, slot, sem, rep, cond=None):
        made = pltpu.make_async_remote_copy(
            src_ref=src,
            dst_ref=dst,
            send_sem=self.send.at[slot],
            recv_sem=sem,
            device_id=(rep, self.tp),
            device_id_type=MESH,
        )
        if cond is None:
            made.start()
        else:
            pl.when(cond)(made.start)
        self.pending.append((made, cond))

    def arrived(self, index, block):
        ref = self.full.at[block]
        pltpu.make_async_copy(ref, ref, self.recv.at[index, block]).wait()

    def line(self, k):
        zo = self.order[k]
        block = self.x * 4 + zo if self.in_ring else zo
        dst, sem = self.full.at[block], self.recv.at[0, block]
        if k == 0:
            src = self.own
            onward, back = self.z < 3, self.z > 0
        else:
            self.arrived(0, block)
            src = dst
            onward, back = (zo < self.z) & (self.z < 3), (zo > self.z) & (self.z > 0)
        self.copy(src, dst, 6 * k, sem, self.x * 4 + lax.min(self.z + 1, 3), onward)
        self.copy(src, dst, 6 * k + 1, sem, self.x * 4 + lax.max(self.z - 1, 0), back)
        if not self.in_ring:
            return
        self.copy(src, dst, 6 * k + 2, sem, self.right + self.z)
        self.copy(src, dst, 6 * k + 3, sem, self.left + self.z)

    def ring(self, k, side):
        zo = self.order[k]
        block = (self.left if side == 0 else self.right) + zo
        self.arrived(0, block)
        part = pl.ds(0, self.half) if side == 0 else pl.ds(self.half, self.half)
        ref = self.full.at[block, part]
        target = (self.right if side == 0 else self.left) + self.z
        self.copy(ref, ref, 6 * k + 4 + side, self.recv.at[side, block], target)
        return block

    def opposite(self, k):
        block = self.far + self.order[k]
        for side in range(2):
            ref = self.full.at[block, pl.ds(side * self.half, self.half)]
            pltpu.make_async_copy(ref, ref, self.recv.at[side, block]).wait()
        return block

    def drain(self):
        for made, cond in self.pending:
            if cond is None:
                made.wait_send()
            else:
                pl.when(cond)(made.wait_send)


def project_kernel(
    lens_ref, pref_ref, hidden_ref, gain_ref, freq_ref, wq_ref, wkv_ref, wo_ref,
    q_out, k_out, v_out, wo_out,
    gain, q_ref, k_ref, v_ref, hid, x3, full_q, full_s, full_w, turned, qacc, kacc, cosine, sine, mine, other,
    hid_sem, recv_q, send_q, recv_r, send_r, recv_s, send_s, recv_w, send_w, kv_send, kv_recv, perm_send, perm_recv, swap_sem, out_sem, own_sem, store_sem,
):
    rep, tp, x, z, zh, y, c = place()
    rows = hid.shape[0]
    count = hid_sem.shape[0]
    chunk = rows // count
    loads = []
    for i in range(count):
        at = pl.ds(i * chunk, chunk)
        loads.append(pltpu.make_async_copy(hidden_ref.at[at], hid.at[at], hid_sem.at[i]))
        loads[-1].start()
    own_load = pltpu.make_async_copy(wq_ref, full_q.at[rep], own_sem)
    own_load.start()

    zh_t = x // 2
    perm_dst = (y * 4 + zh_t * 2 + c, zh * 8 + ((x % 2) * 2 + z // 2) * 2 + z % 2)
    perm_src = (((z // 2) * 2 + y // 2) * 4 + (y % 2) * 2 + c, zh * 8 + x * 2 + z % 2)
    perm_away = (perm_dst[0] != rep) | (perm_dst[1] != tp)
    barrier = pltpu.get_barrier_semaphore()
    line_right, line_left = x * 4 + lax.min(z + 1, 3), x * 4 + lax.max(z - 1, 0)

    pl.when(z < 3)(lambda: signal(barrier, (line_right, tp)))
    pl.when(z > 0)(lambda: signal(barrier, (line_left, tp)))
    signal(barrier, (((x + 1) % 4) * 4 + z, tp))
    signal(barrier, (((x + 3) % 4) * 4 + z, tp))
    signal(barrier, (rep, tp + 1 - 2 * c))
    pl.when(perm_away)(lambda: signal(barrier, perm_src))
    for j in range(8):
        source = c * 8 + j
        pl.when(source != tp)(lambda source=source: signal(barrier, (rep, source)))
    shape = (4 * 16, 4 * 16)
    out_row, in_col = lax.broadcasted_iota(jnp.int32, shape, 0), lax.broadcasted_iota(jnp.int32, shape, 1)
    pick = ((out_row % 16) * KV + out_row // 16 == in_col).astype(jnp.float32).astype(jnp.bfloat16)
    turned[...] = lax.dot_general(
        pick, wkv_ref[...], (((1,), (0,)), ((), ())), preferred_element_type=jnp.float32
    ).astype(jnp.bfloat16)

    starts, first_token = [], 0
    for request in range(REQ_REP):
        starts.append(first_token)
        first_token = first_token + lens_ref[0, request]

    def angles(i, _):
        at = pl.ds(pl.multiple_of(i * 128, 128), 128)
        token = i * 128 + lax.broadcasted_iota(jnp.int32, (128, HD), 0)
        position = jnp.zeros((128, HD), jnp.int32)
        for request in range(REQ_REP):
            shift = pref_ref[request] - starts[request]
            position = jnp.where(token >= starts[request], token + shift, position)
        angle = position.astype(jnp.float32) * freq_ref[...]
        lane = lax.broadcasted_iota(jnp.int32, (128, HD), 1)
        cosine[at, :] = jnp.cos(angle)
        wave = jnp.sin(angle)
        sine[at, :] = jnp.where(lane < HD // 2, -wave, wave)
        return 0

    lax.fori_loop(0, rows // 128, angles, 0)
    gain[...] = gain_ref[...].astype(jnp.float32).reshape(1, D)

    line_peers = (lax.min(z + 1, 3) - z) + (z - lax.max(z - 1, 0))
    pl.semaphore_wait(barrier, 10 + line_peers + perm_away.astype(jnp.int32) + (c + zh) % 2)

    low, high = pl.ds(0, BLK // 2), pl.ds(BLK // 2, BLK // 2)
    stream_q = Gather(wq_ref.at[low], full_q.at[:, low], recv_q, send_q, BLK // 4)
    stream_r = Gather(wq_ref.at[high], full_q.at[:, high], recv_r, send_r, BLK // 4)
    stream_s = Gather(full_s.at[rep], full_s, recv_s, send_s, full_s.shape[1] // 2)
    stream_w = Gather(full_w.at[z], full_w, recv_w, send_w, 0, False)
    stream_q.line(0)
    stream_r.line(0)

    def piece(head, which):
        target = (head // 2) * 8 + (2 * (head % 2) + which) * 2 + zh
        from_ref = turned.at[pl.ds(head * 16, 16)]
        to_ref = full_s.at[rep, pl.ds(pl.multiple_of((tp % 8) * 16, 16), 16)]
        away = target != tp
        made = pltpu.make_async_remote_copy(
            src_ref=from_ref, dst_ref=to_ref, send_sem=kv_send.at[head * 2 + which], recv_sem=kv_recv.at[tp % 8],
            device_id=(rep, target), device_id_type=MESH,
        )
        here = pltpu.make_async_copy(from_ref, to_ref, kv_recv.at[tp % 8])
        pl.when(away)(made.start)
        pl.when(jnp.logical_not(away))(here.start)
        return made, away

    pieces = [piece(head, which) for head in range(KV) for which in range(2)]

    wo_dst = full_w.at[perm_dst[0] % 4]
    permute = pltpu.make_async_remote_copy(
        src_ref=wo_ref, dst_ref=wo_dst, send_sem=perm_send, recv_sem=perm_recv,
        device_id=perm_dst, device_id_type=MESH,
    )
    stay = pltpu.make_async_copy(wo_ref, wo_dst, perm_recv)
    pl.when(perm_away)(permute.start)
    pl.when(jnp.logical_not(perm_away))(stay.start)

    def norm(i):
        loads[i].wait()

        def some(j, _):
            at = pl.ds(pl.multiple_of(i * chunk + j * 16, 16), 16)
            wide = hid[at, :].astype(jnp.float32)
            meansq = jnp.sum(wide * wide, axis=1, keepdims=True) * (1.0 / D)
            scaled = wide * lax.rsqrt(meansq + norm_eps)
            for b in range(D // BLK):
                cols = slice(b * BLK, (b + 1) * BLK)
                x3[b, at, :] = (scaled[:, cols] * gain[:, cols]).astype(jnp.bfloat16)
            return 0

        lax.fori_loop(0, chunk // 16, some, 0)

    def use_q(block, own=False):
        for i in range(rows // BLK):
            at = pl.ds(i * BLK, BLK)
            part = jnp.dot(x3[block, at, :], full_q[block], preferred_element_type=jnp.float32)
            qacc[at, :] = part if own else qacc[at, :] + part

    def use_s(block, own=False):
        for i in range(rows // BLK):
            at = pl.ds(i * BLK, BLK)
            part = lax.dot_general(
                x3[block, at, :], full_s[block, :HD, :], (((1,), (1,)), ((), ())),
                preferred_element_type=jnp.float32,
            )
            kacc[at, :] = part if own else kacc[at, :] + part

    norm(0)
    norm(1)
    stream_q.line(1)
    stream_r.line(1)
    for j in range(8):
        ref = full_s.at[rep, pl.ds(j * 16, 16)]
        pltpu.make_async_copy(ref, ref, kv_recv.at[j]).wait()
    stream_s.line(0)
    norm(2)
    norm(3)
    stream_s.line(1)
    norm(4)
    stream_s.line(2)
    stream_q.line(2)
    stream_r.line(2)
    norm(5)
    norm(6)
    stream_s.line(3)
    stream_q.line(3)
    stream_r.line(3)
    norm(7)
    own_load.wait()
    use_q(rep, True)
    use_s(rep, True)
    for k in range(4):
        lefts_s, rights_s = stream_s.ring(k, 0), stream_s.ring(k, 1)
        lefts, rights = stream_q.ring(k, 0), stream_q.ring(k, 1)
        stream_r.ring(k, 0)
        stream_r.ring(k, 1)
        if k > 0:
            own_block = x * 4 + stream_q.order[k]
            use_q(own_block)
            use_s(own_block)
        for block in (lefts, rights):
            use_q(block)
        for block in (lefts_s, rights_s):
            use_s(block)
        if k > 0:
            stream_r.opposite(k - 1)
            use_q(stream_q.opposite(k - 1))
            use_s(stream_s.opposite(k - 1))
        if k == 0:
            own_wo = full_w.at[z]
            pltpu.make_async_copy(own_wo, own_wo, perm_recv).wait()
        stream_w.line(k)
    flush = pltpu.make_async_copy(full_w, wo_out, out_sem)
    flush.start()
    use_s(stream_s.opposite(3))

    fresh = kacc[...].astype(jnp.bfloat16).astype(jnp.float32)
    turned_key = fresh * cosine[...] + pltpu.roll(fresh, HD // 2, 1) * sine[...]
    mine[...] = jnp.where(c == 0, turned_key, fresh).astype(jnp.bfloat16)
    swap = pltpu.make_async_remote_copy(
        src_ref=mine, dst_ref=other, send_sem=swap_sem.at[0], recv_sem=swap_sem.at[1],
        device_id=(rep, tp + 1 - 2 * c), device_id_type=MESH,
    )
    stream_r.opposite(3)
    use_q(stream_q.opposite(3))
    swap.start()
    for h in range(q_ref.shape[1] // HD):
        cols = slice(h * HD, (h + 1) * HD)
        u = qacc[:, cols]
        q_ref[:, cols] = (u * cosine[...] + pltpu.roll(u, HD // 2, 1) * sine[...]).astype(jnp.bfloat16)
    store_q = pltpu.make_async_copy(q_ref, q_out, store_sem.at[0])
    store_q.start()
    for made, away in pieces:
        pl.when(away)(made.wait_send)
    pl.when(perm_away)(permute.wait_send)
    stream_q.drain()
    stream_r.drain()
    stream_s.drain()
    stream_w.drain()
    swap.wait()

    @pl.when(c == 0)
    def _():
        k_ref[...] = mine[...]
        v_ref[...] = other[...]

    @pl.when(c != 0)
    def _():
        k_ref[...] = other[...]
        v_ref[...] = mine[...]

    store_k = pltpu.make_async_copy(k_ref, k_out, store_sem.at[1])
    store_v = pltpu.make_async_copy(v_ref, v_out, store_sem.at[2])
    store_k.start()
    store_v.start()
    store_q.wait()
    store_k.wait()
    store_v.wait()
    flush.wait()


def vmem():
    return pl.BlockSpec(memory_space=pltpu.VMEM)


def smem():
    return pl.BlockSpec(memory_space=pltpu.SMEM)


def anywhere():
    return pl.BlockSpec(memory_space=pl.ANY)


def project(lengths, prefix, hidden, norm_gain, freqs, w_query, w_keyval, w_output):
    rows = hidden.shape[0]
    bf16, f32, dma = jnp.bfloat16, jnp.float32, pltpu.SemaphoreType.DMA
    return pl.pallas_call(
        project_kernel,
        out_shape=(
            jax.ShapeDtypeStruct((rows, BLK), bf16),
            jax.ShapeDtypeStruct((rows, HD), bf16),
            jax.ShapeDtypeStruct((rows, HD), bf16),
            jax.ShapeDtypeStruct((4, BLK, BLK), bf16),
        ),
        in_specs=[smem(), smem(), anywhere(), vmem(), vmem(), anywhere(), vmem(), anywhere()],
        out_specs=(anywhere(), anywhere(), anywhere(), anywhere()),
        scratch_shapes=[
            pltpu.VMEM((1, D), f32),
            pltpu.VMEM((rows, BLK), bf16),
            pltpu.VMEM((rows, HD), bf16),
            pltpu.VMEM((rows, HD), bf16),
            pltpu.VMEM((rows, D), bf16),
            pltpu.VMEM((16, rows, BLK), bf16),
            pltpu.VMEM((16, BLK, BLK), bf16),
            pltpu.VMEM((16, HD, BLK), bf16),
            pltpu.VMEM((4, BLK, BLK), bf16),
            pltpu.VMEM((64, BLK), bf16),
            pltpu.VMEM((rows, BLK), f32),
            pltpu.VMEM((rows, HD), f32),
            pltpu.VMEM((rows, HD), f32),
            pltpu.VMEM((rows, HD), f32),
            pltpu.VMEM((rows, HD), bf16),
            pltpu.VMEM((rows, HD), bf16),
            dma((8,)),
            dma((2, 16)),
            dma((24,)),
            dma((2, 16)),
            dma((24,)),
            dma((2, 16)),
            dma((24,)),
            dma((1, 4)),
            dma((24,)),
            dma((8,)),
            dma((8,)),
            dma,
            dma,
            dma((2,)),
            dma,
            dma,
            dma((3,)),
        ],
        compiler_params=pltpu.CompilerParams(collective_id=0, has_side_effects=True, vmem_limit_bytes=VMEM_ALL),
        cost_estimate=pl.CostEstimate(flops=3 * 10**9, bytes_accessed=12 * 2**20, transcendentals=10**6),
        name="project",
    )(lengths, prefix, hidden, norm_gain, freqs, w_query, w_keyval, w_output)


def attention_kernel(
    lens_ref, pref_ref, q_ref, k_ref, v_ref, cache_ref, o_ref, qs, ks, vs, stored, outs, sems, out_sem
):
    rows, width = q_ref.shape
    column = pl.multiple_of(lax.axis_index("tp") // 4 * 2 * HD, 2 * HD)
    inside = pl.ds(0, rows)
    loads = [
        pltpu.make_async_copy(q_ref, qs.at[inside], sems.at[REQ_REP]),
        pltpu.make_async_copy(k_ref, ks.at[inside], sems.at[REQ_REP + 1]),
        pltpu.make_async_copy(v_ref, vs.at[inside], sems.at[REQ_REP + 2]),
    ]

    def fetch(request):
        at = pl.ds(pl.multiple_of(request * PREF_MAX, PREF_MAX), PREF_MAX)
        return pltpu.make_async_copy(cache_ref.at[at, pl.ds(column, 2 * HD)], stored.at[at, :], sems.at[request])

    fetch(0).start()
    for load in loads:
        load.start()
    for request in range(1, REQ_REP):
        fetch(request).start()
    spare = pl.ds(rows, qs.shape[0] - rows)
    ks[spare, :] = jnp.zeros((TQ, HD), jnp.bfloat16)
    vs[spare, :] = jnp.zeros((TQ, HD), jnp.bfloat16)
    for load in loads:
        load.wait()
    factor = HD ** (-0.5) * math.log2(math.e)
    nt = (((1,), (1,)), ((), ()))
    lane = lax.broadcasted_iota(jnp.int32, (TQ, TQ), 1)
    row = lax.broadcasted_iota(jnp.int32, (TQ, TQ), 0)

    def tile(start, aligned, base, prefix, index, parts):
        rows_at = pl.ds(pl.multiple_of(aligned + index * TQ, 16), TQ)
        for h in range(width // HD):
            cols = slice(h * HD, (h + 1) * HD)
            q = qs[rows_at, cols]
            scores, values = [], []
            for part in range(parts):
                at = pl.ds(pl.multiple_of(base + part * TQ, TQ), TQ)
                score = lax.dot_general(q, stored[at, :HD], nt, preferred_element_type=jnp.float32)
                if part == parts - 1:
                    score = jnp.where(lane < prefix - part * TQ, score, NEG_MASK)
                scores.append(score)
                values.append((stored, at, slice(HD, 2 * HD)))
            for part in range(index + 1):
                at = pl.ds(pl.multiple_of(aligned + part * TQ, 16), TQ)
                score = lax.dot_general(q, ks[at, :], nt, preferred_element_type=jnp.float32)
                if part == index:
                    score = jnp.where(lane <= row, score, NEG_MASK)
                if part == 0:
                    score = jnp.where(lane >= start - aligned, score, NEG_MASK)
                scores.append(score)
                values.append((vs, at, slice(0, HD)))
            peak = scores[0]
            for score in scores[1:]:
                peak = jnp.maximum(peak, score)
            peak = jnp.max(peak, axis=1, keepdims=True)
            total, gathered = None, None
            for score, (ref, at, which) in zip(scores, values):
                e = jnp.exp2((score - peak) * factor)
                total = e if total is None else total + e
                part = jnp.dot(e.astype(jnp.bfloat16), ref[at, which], preferred_element_type=jnp.float32)
                gathered = part if gathered is None else gathered + part
            result = gathered / jnp.sum(total, axis=1, keepdims=True)
            if index == 0:
                keep = row[:, :HD] + aligned < start
                result = jnp.where(keep, outs[rows_at, cols].astype(jnp.float32), result)
            outs[rows_at, cols] = result.astype(jnp.bfloat16)

    def one(request, start):
        end, prefix = start + lens_ref[0, request], pref_ref[request]
        aligned = start // 16 * 16
        base = request * PREF_MAX
        fetch(request).wait()
        for index in range(3):
            for parts in (1, 2):
                fits = (prefix <= TQ) if parts == 1 else (prefix > TQ)
                pl.when((aligned + index * TQ < end) & fits)(
                    functools.partial(tile, start, aligned, base, prefix, index, parts)
                )
        return end

    lax.fori_loop(0, REQ_REP, one, 0)
    store = pltpu.make_async_copy(outs.at[inside], o_ref, out_sem)
    store.start()
    store.wait()


def attend(lengths, prefix, q, k, v, cache):
    rows, width = q.shape
    bf16, dma = jnp.bfloat16, pltpu.SemaphoreType.DMA
    return pl.pallas_call(
        attention_kernel,
        out_shape=jax.ShapeDtypeStruct((rows, width), bf16),
        in_specs=[smem(), smem(), anywhere(), anywhere(), anywhere(), anywhere()],
        out_specs=anywhere(),
        scratch_shapes=[
            pltpu.VMEM((rows + TQ, width), bf16),
            pltpu.VMEM((rows + TQ, HD), bf16),
            pltpu.VMEM((rows + TQ, HD), bf16),
            pltpu.VMEM((REQ_REP * PREF_MAX, 2 * HD), bf16),
            pltpu.VMEM((rows + TQ, width), bf16),
            dma((REQ_REP + 3,)),
            dma,
        ],
        compiler_params=pltpu.CompilerParams(vmem_limit_bytes=VMEM_ALL),
        cost_estimate=pl.CostEstimate(flops=2 * 10**9, bytes_accessed=3 * 2**20, transcendentals=2 * 10**6),
        name="attention",
    )(lengths, prefix, q, k, v, cache)


def output_kernel(
    att_ref, hidden_ref, wo_here,
    resid_out, inverse_ref,
    resid_ref, wo_ref, att, part_send, part_recv, own, hid, sums_mine, sums,
    hid_sem, ring_send, ring_recv, core_send, core_recv, part_sems, sum_send, sum_recv, wo_sem, own_sem, wo_send, wo_recv, store_sem,
):
    rep, tp, x, z, zh, y, c = place()
    rows, width = hid.shape
    barrier = pltpu.get_barrier_semaphore()
    for k in sorted(range(1, 16), key=lambda k: abs(k - 8)):
        signal(barrier, (rep, (tp + k) % 16))
    for dx in (1, 3):
        signal(barrier, ((x + dx) % 4 * 4 + z, tp))
    load = pltpu.make_async_copy(
        hidden_ref.at[:, pl.ds(pl.multiple_of(tp * width, width), width)], hid, hid_sem
    )
    load.start()
    load_wo = pltpu.make_async_copy(wo_here, wo_ref.at[pl.ds(x * 4, 4)], wo_sem)
    load_wo.start()
    load_own = pltpu.make_async_copy(att_ref, att.at[0, 0], own_sem)
    load_own.start()
    pl.semaphore_wait(barrier, 17)

    def at_y(to):
        return (rep, zh * 8 + (to % 4) * 2 + c)

    partner = (rep, tp + 1 - 2 * c)
    across = (rep, (tp + 8) % 16)
    size = rows // CHUNKS
    half = size // 2
    pending = []

    def send(src, dst, ssem, rsem, device):
        made = pltpu.make_async_remote_copy(
            src_ref=src, dst_ref=dst, send_sem=ssem, recv_sem=rsem, device_id=device, device_id_type=MESH
        )
        made.start()
        pending.append(made)

    def wait(ref, sem):
        pltpu.make_async_copy(ref, ref, sem).wait()

    def own_send(m):
        at = pl.ds(m * size, size)
        src = att_ref.at[at]
        send(src, att.at[0, 1, at], ring_send.at[0, m], ring_recv.at[0, m], at_y(y + 1))
        send(src, att.at[0, 2, at], ring_send.at[1, m], ring_recv.at[1, m], at_y(y + 3))
        send(src, att.at[1, 0, at], core_send.at[0, m], core_recv.at[0, m], partner)

    def ring_in(m):
        at = pl.ds(m * size, size)
        for side in range(2):
            ref = att.at[0, 1 + side, at]
            wait(ref, ring_recv.at[side, m])
            part = pl.ds(m * size + side * half, half)
            send(
                att.at[0, 1 + side, part], att.at[0, 3, part],
                ring_send.at[2 + side, m], ring_recv.at[2 + side, m], at_y(y + 1 + 2 * side),
            )
            send(ref, att.at[1, 1 + side, at], core_send.at[1 + side, m], core_recv.at[1 + side, m], partner)

    def far_in(m):
        for side in range(2):
            wait(att.at[0, 3, pl.ds(m * size + side * half, half)], ring_recv.at[2 + side, m])
        ref = att.at[0, 3, pl.ds(m * size, size)]
        send(ref, att.at[1, 3, pl.ds(m * size, size)], core_send.at[3, m], core_recv.at[3, m], partner)

    def columns(which):
        return (1 - zh if which == 0 else zh) * 2

    def beside(dx):
        return ((x + dx) % 4 * 4 + z, tp)

    def weight_out(which):
        for side, dx in enumerate((1, 3)):
            send(
                wo_here.at[pl.ds(columns(which), 2)], wo_ref.at[pl.ds(x * 4 + columns(which), 2)],
                wo_send.at[which, side], wo_recv.at[which, side], beside(dx),
            )

    def weight_relay(which):
        for side, dx in enumerate((3, 1)):
            at = pl.ds((x + dx) % 4 * 4 + columns(which), 2)
            wait(wo_ref.at[at], wo_recv.at[which, side])
            some = wo_ref.at[at, pl.ds(side * (BLK // 2), BLK // 2)]
            send(some, some, wo_send.at[which, 2 + side], wo_recv.at[which, 2 + side], beside(4 - dx))

    def weight_in(which):
        for side in range(2):
            some = pl.ds(side * (BLK // 2), BLK // 2)
            wait(wo_ref.at[pl.ds((x + 2) % 4 * 4 + columns(which), 2), some], wo_recv.at[which, 2 + side])

    def contract(at, target):
        total = None
        for side in range(2):
            for d, dy in enumerate((0, 3, 1, 2)):
                core = c if side == 0 else 1 - c
                block = ((y + dy) % 4) * 4 + target * 2 + core
                part = jnp.dot(att[side, d, at, :], wo_ref[block], preferred_element_type=jnp.float32)
                total = part if total is None else total + part
        return total

    def away(m):
        at = pl.ds(m * size, size)
        for d in range(4):
            wait(att.at[1, d, at], core_recv.at[d, m])
        part_send[at, :] = contract(at, 1 - zh).astype(jnp.bfloat16)
        send(part_send.at[at], part_recv.at[at], part_sems.at[0, m], part_sems.at[1, m], across)

    def mine(m):
        at = pl.ds(m * BLK, BLK)
        own[at, :] = contract(at, zh)

    own_send(0)
    weight_out(0)
    own_send(1)
    own_send(2)
    load_wo.wait()
    load_own.wait()
    ready = 0
    for i in range(CHUNKS + 2):
        if i < CHUNKS:
            ring_in(i)
        if i + 3 < CHUNKS:
            own_send(i + 3)
        if 1 <= i <= CHUNKS:
            far_in(i - 1)
        if i == 1:
            weight_relay(0)
        if i == WEIGHT_AT:
            weight_in(0)
            weight_out(1)
        if i == CHUNKS - 1:
            weight_relay(1)
        if i >= WEIGHT_AT:
            for _ in range(2):
                if ready <= i - 2:
                    away(ready)
                    ready += 1
        if i == CHUNKS:
            weight_in(1)
            for m in range(OWN_EARLY):
                mine(m)
    for m in range(OWN_EARLY, rows // BLK):
        mine(m)
    load.wait()
    for m in range(CHUNKS):
        at = pl.ds(m * size, size)
        wait(part_recv.at[at], part_sems.at[1, m])
        for i in range(size // HD):
            row = m * (size // HD) + i
            here = pl.ds(row * HD, HD)
            resid = (
                hid[here, :].astype(jnp.float32) + (own[here, :] + part_recv[here, :].astype(jnp.float32))
            ).astype(jnp.bfloat16)
            resid_ref[here, :] = resid
            wide = resid.astype(jnp.float32)
            total = jnp.sum(wide * wide, axis=1, keepdims=True)
            sums_mine[pl.ds(row, 1), :] = jnp.transpose(jnp.broadcast_to(total, (HD, HD)))[:1, :]
    store = pltpu.make_async_copy(resid_ref, resid_out, store_sem)
    for k in sorted(range(1, 16), key=lambda k: abs(k - 8)):
        send(sums_mine, sums.at[k], sum_send.at[k], sum_recv.at[k], (rep, (tp + k) % 16))
    store.start()
    total = sums_mine[...]
    for k in range(1, 16):
        wait(sums.at[k], sum_recv.at[k])
        total = total + sums[k]
    inverse_ref[...] = lax.rsqrt(total * (1.0 / D) + norm_eps)
    store.wait()
    for made in pending:
        made.wait_send()


def finish(attended, hidden, wo_here):
    rows, width = attended.shape
    bf16, f32, dma = jnp.bfloat16, jnp.float32, pltpu.SemaphoreType.DMA
    return pl.pallas_call(
        output_kernel,
        out_shape=(jax.ShapeDtypeStruct((rows, width), bf16), jax.ShapeDtypeStruct((rows // HD, HD), f32)),
        in_specs=[anywhere(), anywhere(), anywhere()],
        out_specs=(anywhere(), vmem()),
        scratch_shapes=[
            pltpu.VMEM((rows, width), bf16),
            pltpu.VMEM((16, BLK, BLK), bf16),
            pltpu.VMEM((2, 4, rows, width), bf16),
            pltpu.VMEM((rows, width), bf16),
            pltpu.VMEM((rows, width), bf16),
            pltpu.VMEM((rows, width), f32),
            pltpu.VMEM((rows, width), bf16),
            pltpu.VMEM((rows // HD, HD), f32),
            pltpu.VMEM((16, rows // HD, HD), f32),
            dma,
            dma((4, CHUNKS)),
            dma((4, CHUNKS)),
            dma((4, CHUNKS)),
            dma((4, CHUNKS)),
            dma((2, CHUNKS)),
            dma((16,)),
            dma((16,)),
            dma,
            dma,
            dma((2, 4)),
            dma((2, 4)),
            dma,
        ],
        compiler_params=pltpu.CompilerParams(collective_id=1, has_side_effects=True, vmem_limit_bytes=VMEM_ALL),
        cost_estimate=pl.CostEstimate(flops=2 * 10**9, bytes_accessed=6 * 2**20, transcendentals=10**4),
        name="finish",
    )(attended, hidden, wo_here)


def scale_kernel(resid_in, inverse_ref, gain_ref, resid_out, normed_out, gain_row, resid, normed, in_sem, out_sem, norm_sem):
    rows, width = resid.shape
    count = in_sem.shape[0]
    size = rows // count
    loads, stores = [], []
    for i in range(count):
        at = pl.ds(i * size, size)
        loads.append(pltpu.make_async_copy(resid_in.at[at], resid.at[at], in_sem.at[i]))
        loads[-1].start()
    gain_row[...] = gain_ref[...].astype(jnp.float32).reshape(1, D)
    gain = gain_row[:, pl.ds(pl.multiple_of(lax.axis_index("tp") * width, width), width)]
    for i in range(count):
        at = pl.ds(i * size, size)
        loads[i].wait()
        stores.append(pltpu.make_async_copy(resid.at[at], resid_out.at[at], out_sem.at[i]))
        stores[-1].start()
        for row in range(i * size // HD, (i + 1) * size // HD):
            here = pl.ds(row * HD, HD)
            column = jnp.transpose(jnp.broadcast_to(inverse_ref[row : row + 1, :], (HD, HD)))
            for h in range(width // HD):
                cols = slice(h * HD, (h + 1) * HD)
                normed[here, cols] = (
                    resid[here, cols].astype(jnp.float32) * column * gain[:, cols]
                ).astype(jnp.bfloat16)
        stores.append(pltpu.make_async_copy(normed.at[at], normed_out.at[at], norm_sem.at[i]))
        stores[-1].start()
    for store in stores:
        store.wait()


def scale(resid, inverse, out_gain):
    rows, width = resid.shape
    bf16, dma = jnp.bfloat16, pltpu.SemaphoreType.DMA
    return pl.pallas_call(
        scale_kernel,
        out_shape=(jax.ShapeDtypeStruct((rows, width), bf16), jax.ShapeDtypeStruct((rows, width), bf16)),
        in_specs=[anywhere(), vmem(), vmem()],
        out_specs=(anywhere(), anywhere()),
        scratch_shapes=[
            pltpu.VMEM((1, D), jnp.float32),
            pltpu.VMEM((rows, width), bf16),
            pltpu.VMEM((rows, width), bf16),
            dma((4,)),
            dma((4,)),
            dma((4,)),
        ],
        compiler_params=pltpu.CompilerParams(vmem_limit_bytes=VMEM_ALL),
        cost_estimate=pl.CostEstimate(flops=10**6, bytes_accessed=3 * 2**19, transcendentals=0),
        name="scale",
    )(resid, inverse, out_gain)


def body(hidden, norm_gain, w_query, w_keyval, w_output, cache, lengths, prefix, out_gain):
    powers = np.arange(HD) % (HD // 2) * 2.0 / HD
    freqs = jnp.asarray((rope_base**-powers).astype(np.float32).reshape(1, HD))
    q, k, v, wo_here = project(lengths, prefix, hidden, norm_gain, freqs, w_query, w_keyval.T, w_output)
    attended = attend(lengths, prefix, q, k, v, cache)
    resid, inverse = finish(attended, hidden, wo_here)
    return scale(resid, inverse, out_gain)


def solution(mesh):
    placed = (
        P("rep", None),
        P(),
        P("rep", "tp"),
        P("rep", "tp"),
        P("tp", "rep"),
        P("rep", None),
        P("rep", None),
        P("rep"),
        P(),
    )
    return jax.shard_map(
        body,
        mesh=mesh,
        in_specs=placed,
        out_specs=(P("rep", "tp"), P("rep", "tp")),
        check_vma=False,
    )
```

```python
import functools
import math

import jax
import jax.numpy as jnp
import numpy as np
from jax import lax
from jax.experimental import pallas as pl
from jax.experimental.pallas import tpu as pltpu
from jax.sharding import PartitionSpec as P

H = 32
KV = 4
HD = 128
REQ_REP = 4
PREF_MAX = 512

norm_eps = 1e-05
rope_base = 5000000.0
TQ = 256
NEG_MASK = -1e30
VMEM_ALL = 67043328
CHUNKS = 8
WEIGHT_AT = 3
OWN_EARLY = 3


MESH = pl.DeviceIdType.MESH
D = 4096
BLK = 256


def place():
    rep, tp = lax.axis_index("rep"), lax.axis_index("tp")
    return rep, tp, rep // 4, rep % 4, tp // 8, (tp // 2) % 4, tp % 2


def line_order(z):
    power = 1 + 3 * z + 9 * (z * (z - 1) // 2) + 27 * (z * (z - 1) * (z - 2) // 6)
    tables = []
    for picks in ((1, 0, 1, 2), (2, 2, 3, 1), (3, 3, 0, 0)):
        tables.append(sum(pick * 4**i for i, pick in enumerate(picks)))
    return [z] + [(table // power) % 4 for table in tables]


def signal(sem, device):
    pl.semaphore_signal(sem, inc=1, device_id=device, device_id_type=MESH)


class Gather:
    def __init__(self, own, full, recv, send, half, ring=True):
        self.own, self.full, self.recv, self.send, self.half = own, full, recv, send, half
        self.in_ring = ring
        self.rep, self.tp, self.x, self.z = place()[:4]
        self.order = line_order(self.z)
        self.right = ((self.x + 1) % 4) * 4
        self.left = ((self.x + 3) % 4) * 4
        self.far = ((self.x + 2) % 4) * 4
        self.pending = []

    def copy(self, src, dst, slot, sem, rep, cond=None):
        made = pltpu.make_async_remote_copy(
            src_ref=src,
            dst_ref=dst,
            send_sem=self.send.at[slot],
            recv_sem=sem,
            device_id=(rep, self.tp),
            device_id_type=MESH,
        )
        if cond is None:
            made.start()
        else:
            pl.when(cond)(made.start)
        self.pending.append((made, cond))

    def arrived(self, index, block):
        ref = self.full.at[block]
        pltpu.make_async_copy(ref, ref, self.recv.at[index, block]).wait()

    def line(self, k):
        zo = self.order[k]
        block = self.x * 4 + zo if self.in_ring else zo
        dst, sem = self.full.at[block], self.recv.at[0, block]
        if k == 0:
            src = self.own
            onward, back = self.z < 3, self.z > 0
        else:
            self.arrived(0, block)
            src = dst
            onward, back = (zo < self.z) & (self.z < 3), (zo > self.z) & (self.z > 0)
        self.copy(src, dst, 6 * k, sem, self.x * 4 + lax.min(self.z + 1, 3), onward)
        self.copy(src, dst, 6 * k + 1, sem, self.x * 4 + lax.max(self.z - 1, 0), back)
        if not self.in_ring:
            return
        self.copy(src, dst, 6 * k + 2, sem, self.right + self.z)
        self.copy(src, dst, 6 * k + 3, sem, self.left + self.z)

    def ring(self, k, side):
        zo = self.order[k]
        block = (self.left if side == 0 else self.right) + zo
        self.arrived(0, block)
        part = pl.ds(0, self.half) if side == 0 else pl.ds(self.half, self.half)
        ref = self.full.at[block, part]
        target = (self.right if side == 0 else self.left) + self.z
        self.copy(ref, ref, 6 * k + 4 + side, self.recv.at[side, block], target)
        return block

    def opposite(self, k):
        block = self.far + self.order[k]
        for side in range(2):
            ref = self.full.at[block, pl.ds(side * self.half, self.half)]
            pltpu.make_async_copy(ref, ref, self.recv.at[side, block]).wait()
        return block

    def drain(self):
        for made, cond in self.pending:
            if cond is None:
                made.wait_send()
            else:
                pl.when(cond)(made.wait_send)


def project_kernel(
    lens_ref, pref_ref, hidden_ref, gain_ref, freq_ref, wq_ref, wkv_ref, wo_ref,
    q_out, k_out, v_out, wo_out,
    gain, q_ref, k_ref, v_ref, hid, x3, full_q, full_s, full_w, turned, qacc, kacc, cosine, sine, mine, other,
    hid_sem, recv_q, send_q, recv_r, send_r, recv_s, send_s, recv_w, send_w, kv_send, kv_recv, perm_send, perm_recv, swap_sem, out_sem, own_sem, store_sem,
):
    rep, tp, x, z, zh, y, c = place()
    rows = hid.shape[0]
    count = hid_sem.shape[0]
    chunk = rows // count
    loads = []
    for i in range(count):
        at = pl.ds(i * chunk, chunk)
        loads.append(pltpu.make_async_copy(hidden_ref.at[at], hid.at[at], hid_sem.at[i]))
        loads[-1].start()
    own_load = pltpu.make_async_copy(wq_ref, full_q.at[rep], own_sem)
    own_load.start()

    zh_t = x // 2
    perm_dst = (y * 4 + zh_t * 2 + c, zh * 8 + ((x % 2) * 2 + z // 2) * 2 + z % 2)
    perm_src = (((z // 2) * 2 + y // 2) * 4 + (y % 2) * 2 + c, zh * 8 + x * 2 + z % 2)
    perm_away = (perm_dst[0] != rep) | (perm_dst[1] != tp)
    barrier = pltpu.get_barrier_semaphore()
    line_right, line_left = x * 4 + lax.min(z + 1, 3), x * 4 + lax.max(z - 1, 0)

    pl.when(z < 3)(lambda: signal(barrier, (line_right, tp)))
    pl.when(z > 0)(lambda: signal(barrier, (line_left, tp)))
    signal(barrier, (((x + 1) % 4) * 4 + z, tp))
    signal(barrier, (((x + 3) % 4) * 4 + z, tp))
    signal(barrier, (rep, tp + 1 - 2 * c))
    pl.when(perm_away)(lambda: signal(barrier, perm_src))
    for j in range(8):
        source = c * 8 + j
        pl.when(source != tp)(lambda source=source: signal(barrier, (rep, source)))
    shape = (4 * 16, 4 * 16)
    out_row, in_col = lax.broadcasted_iota(jnp.int32, shape, 0), lax.broadcasted_iota(jnp.int32, shape, 1)
    pick = ((out_row % 16) * KV + out_row // 16 == in_col).astype(jnp.float32).astype(jnp.bfloat16)
    turned[...] = lax.dot_general(
        pick, wkv_ref[...], (((1,), (0,)), ((), ())), preferred_element_type=jnp.float32
    ).astype(jnp.bfloat16)

    starts, first_token = [], 0
    for request in range(REQ_REP):
        starts.append(first_token)
        first_token = first_token + lens_ref[0, request]

    def angles(i, _):
        at = pl.ds(pl.multiple_of(i * 128, 128), 128)
        token = i * 128 + lax.broadcasted_iota(jnp.int32, (128, HD), 0)
        position = jnp.zeros((128, HD), jnp.int32)
        for request in range(REQ_REP):
            shift = pref_ref[request] - starts[request]
            position = jnp.where(token >= starts[request], token + shift, position)
        angle = position.astype(jnp.float32) * freq_ref[...]
        lane = lax.broadcasted_iota(jnp.int32, (128, HD), 1)
        cosine[at, :] = jnp.cos(angle)
        wave = jnp.sin(angle)
        sine[at, :] = jnp.where(lane < HD // 2, -wave, wave)
        return 0

    lax.fori_loop(0, rows // 128, angles, 0)
    gain[...] = gain_ref[...].astype(jnp.float32).reshape(1, D)

    line_peers = (lax.min(z + 1, 3) - z) + (z - lax.max(z - 1, 0))
    pl.semaphore_wait(barrier, 10 + line_peers + perm_away.astype(jnp.int32) + (c + zh) % 2)

    low, high = pl.ds(0, BLK // 2), pl.ds(BLK // 2, BLK // 2)
    stream_q = Gather(wq_ref.at[low], full_q.at[:, low], recv_q, send_q, BLK // 4)
    stream_r = Gather(wq_ref.at[high], full_q.at[:, high], recv_r, send_r, BLK // 4)
    stream_s = Gather(full_s.at[rep], full_s, recv_s, send_s, full_s.shape[1] // 2)
    stream_w = Gather(full_w.at[z], full_w, recv_w, send_w, 0, False)
    stream_q.line(0)
    stream_r.line(0)

    def piece(head, which):
        target = (head // 2) * 8 + (2 * (head % 2) + which) * 2 + zh
        from_ref = turned.at[pl.ds(head * 16, 16)]
        to_ref = full_s.at[rep, pl.ds(pl.multiple_of((tp % 8) * 16, 16), 16)]
        away = target != tp
        made = pltpu.make_async_remote_copy(
            src_ref=from_ref, dst_ref=to_ref, send_sem=kv_send.at[head * 2 + which], recv_sem=kv_recv.at[tp % 8],
            device_id=(rep, target), device_id_type=MESH,
        )
        here = pltpu.make_async_copy(from_ref, to_ref, kv_recv.at[tp % 8])
        pl.when(away)(made.start)
        pl.when(jnp.logical_not(away))(here.start)
        return made, away

    pieces = [piece(head, which) for head in range(KV) for which in range(2)]

    wo_dst = full_w.at[perm_dst[0] % 4]
    permute = pltpu.make_async_remote_copy(
        src_ref=wo_ref, dst_ref=wo_dst, send_sem=perm_send, recv_sem=perm_recv,
        device_id=perm_dst, device_id_type=MESH,
    )
    stay = pltpu.make_async_copy(wo_ref, wo_dst, perm_recv)
    pl.when(perm_away)(permute.start)
    pl.when(jnp.logical_not(perm_away))(stay.start)

    def norm(i):
        loads[i].wait()

        def some(j, _):
            at = pl.ds(pl.multiple_of(i * chunk + j * 16, 16), 16)
            wide = hid[at, :].astype(jnp.float32)
            meansq = jnp.sum(wide * wide, axis=1, keepdims=True) * (1.0 / D)
            scaled = wide * lax.rsqrt(meansq + norm_eps)
            for b in range(D // BLK):
                cols = slice(b * BLK, (b + 1) * BLK)
                x3[b, at, :] = (scaled[:, cols] * gain[:, cols]).astype(jnp.bfloat16)
            return 0

        lax.fori_loop(0, chunk // 16, some, 0)

    def use_q(block, own=False):
        for i in range(rows // BLK):
            at = pl.ds(i * BLK, BLK)
            part = jnp.dot(x3[block, at, :], full_q[block], preferred_element_type=jnp.float32)
            qacc[at, :] = part if own else qacc[at, :] + part

    def use_s(block, own=False):
        for i in range(rows // BLK):
            at = pl.ds(i * BLK, BLK)
            part = lax.dot_general(
                x3[block, at, :], full_s[block, :HD, :], (((1,), (1,)), ((), ())),
                preferred_element_type=jnp.float32,
            )
            kacc[at, :] = part if own else kacc[at, :] + part

    norm(0)
    norm(1)
    stream_q.line(1)
    stream_r.line(1)
    for j in range(8):
        ref = full_s.at[rep, pl.ds(j * 16, 16)]
        pltpu.make_async_copy(ref, ref, kv_recv.at[j]).wait()
    stream_s.line(0)
    norm(2)
    norm(3)
    stream_s.line(1)
    norm(4)
    stream_s.line(2)
    stream_q.line(2)
    stream_r.line(2)
    norm(5)
    norm(6)
    stream_s.line(3)
    stream_q.line(3)
    stream_r.line(3)
    norm(7)
    own_load.wait()
    use_q(rep, True)
    use_s(rep, True)
    for k in range(4):
        lefts_s, rights_s = stream_s.ring(k, 0), stream_s.ring(k, 1)
        lefts, rights = stream_q.ring(k, 0), stream_q.ring(k, 1)
        stream_r.ring(k, 0)
        stream_r.ring(k, 1)
        if k > 0:
            own_block = x * 4 + stream_q.order[k]
            use_q(own_block)
            use_s(own_block)
        for block in (lefts, rights):
            use_q(block)
        for block in (lefts_s, rights_s):
            use_s(block)
        if k > 0:
            stream_r.opposite(k - 1)
            use_q(stream_q.opposite(k - 1))
            use_s(stream_s.opposite(k - 1))
        if k == 0:
            own_wo = full_w.at[z]
            pltpu.make_async_copy(own_wo, own_wo, perm_recv).wait()
        stream_w.line(k)
    flush = pltpu.make_async_copy(full_w, wo_out, out_sem)
    flush.start()
    use_s(stream_s.opposite(3))

    fresh = kacc[...].astype(jnp.bfloat16).astype(jnp.float32)
    turned_key = fresh * cosine[...] + pltpu.roll(fresh, HD // 2, 1) * sine[...]
    mine[...] = jnp.where(c == 0, turned_key, fresh).astype(jnp.bfloat16)
    swap = pltpu.make_async_remote_copy(
        src_ref=mine, dst_ref=other, send_sem=swap_sem.at[0], recv_sem=swap_sem.at[1],
        device_id=(rep, tp + 1 - 2 * c), device_id_type=MESH,
    )
    stream_r.opposite(3)
    use_q(stream_q.opposite(3))
    swap.start()
    for h in range(q_ref.shape[1] // HD):
        cols = slice(h * HD, (h + 1) * HD)
        u = qacc[:, cols]
        q_ref[:, cols] = (u * cosine[...] + pltpu.roll(u, HD // 2, 1) * sine[...]).astype(jnp.bfloat16)
    store_q = pltpu.make_async_copy(q_ref, q_out, store_sem.at[0])
    store_q.start()
    for made, away in pieces:
        pl.when(away)(made.wait_send)
    pl.when(perm_away)(permute.wait_send)
    stream_q.drain()
    stream_r.drain()
    stream_s.drain()
    stream_w.drain()
    swap.wait()

    @pl.when(c == 0)
    def _():
        k_ref[...] = mine[...]
        v_ref[...] = other[...]

    @pl.when(c != 0)
    def _():
        k_ref[...] = other[...]
        v_ref[...] = mine[...]

    store_k = pltpu.make_async_copy(k_ref, k_out, store_sem.at[1])
    store_v = pltpu.make_async_copy(v_ref, v_out, store_sem.at[2])
    store_k.start()
    store_v.start()
    store_q.wait()
    store_k.wait()
    store_v.wait()
    flush.wait()


def vmem():
    return pl.BlockSpec(memory_space=pltpu.VMEM)


def smem():
    return pl.BlockSpec(memory_space=pltpu.SMEM)


def anywhere():
    return pl.BlockSpec(memory_space=pl.ANY)


def project(lengths, prefix, hidden, norm_gain, freqs, w_query, w_keyval, w_output):
    rows = hidden.shape[0]
    bf16, f32, dma = jnp.bfloat16, jnp.float32, pltpu.SemaphoreType.DMA
    return pl.pallas_call(
        project_kernel,
        out_shape=(
            jax.ShapeDtypeStruct((rows, BLK), bf16),
            jax.ShapeDtypeStruct((rows, HD), bf16),
            jax.ShapeDtypeStruct((rows, HD), bf16),
            jax.ShapeDtypeStruct((4, BLK, BLK), bf16),
        ),
        in_specs=[smem(), smem(), anywhere(), vmem(), vmem(), anywhere(), vmem(), anywhere()],
        out_specs=(anywhere(), anywhere(), anywhere(), anywhere()),
        scratch_shapes=[
            pltpu.VMEM((1, D), f32),
            pltpu.VMEM((rows, BLK), bf16),
            pltpu.VMEM((rows, HD), bf16),
            pltpu.VMEM((rows, HD), bf16),
            pltpu.VMEM((rows, D), bf16),
            pltpu.VMEM((16, rows, BLK), bf16),
            pltpu.VMEM((16, BLK, BLK), bf16),
            pltpu.VMEM((16, HD, BLK), bf16),
            pltpu.VMEM((4, BLK, BLK), bf16),
            pltpu.VMEM((64, BLK), bf16),
            pltpu.VMEM((rows, BLK), f32),
            pltpu.VMEM((rows, HD), f32),
            pltpu.VMEM((rows, HD), f32),
            pltpu.VMEM((rows, HD), f32),
            pltpu.VMEM((rows, HD), bf16),
            pltpu.VMEM((rows, HD), bf16),
            dma((8,)),
            dma((2, 16)),
            dma((24,)),
            dma((2, 16)),
            dma((24,)),
            dma((2, 16)),
            dma((24,)),
            dma((1, 4)),
            dma((24,)),
            dma((8,)),
            dma((8,)),
            dma,
            dma,
            dma((2,)),
            dma,
            dma,
            dma((3,)),
        ],
        compiler_params=pltpu.CompilerParams(collective_id=0, has_side_effects=True, vmem_limit_bytes=VMEM_ALL),
        cost_estimate=pl.CostEstimate(flops=3 * 10**9, bytes_accessed=12 * 2**20, transcendentals=10**6),
        name="project",
    )(lengths, prefix, hidden, norm_gain, freqs, w_query, w_keyval, w_output)


def attention_kernel(
    lens_ref, pref_ref, q_ref, k_ref, v_ref, cache_ref, o_ref, qs, ks, vs, stored, outs, sems, out_sem
):
    rows, width = q_ref.shape
    column = pl.multiple_of(lax.axis_index("tp") // 4 * 2 * HD, 2 * HD)
    inside = pl.ds(0, rows)
    loads = [
        pltpu.make_async_copy(q_ref, qs.at[inside], sems.at[REQ_REP]),
        pltpu.make_async_copy(k_ref, ks.at[inside], sems.at[REQ_REP + 1]),
        pltpu.make_async_copy(v_ref, vs.at[inside], sems.at[REQ_REP + 2]),
    ]

    def fetch(request):
        at = pl.ds(pl.multiple_of(request * PREF_MAX, PREF_MAX), PREF_MAX)
        return pltpu.make_async_copy(cache_ref.at[at, pl.ds(column, 2 * HD)], stored.at[at, :], sems.at[request])

    fetch(0).start()
    for load in loads:
        load.start()
    for request in range(1, REQ_REP):
        fetch(request).start()
    spare = pl.ds(rows, qs.shape[0] - rows)
    ks[spare, :] = jnp.zeros((TQ, HD), jnp.bfloat16)
    vs[spare, :] = jnp.zeros((TQ, HD), jnp.bfloat16)
    for load in loads:
        load.wait()
    factor = HD ** (-0.5) * math.log2(math.e)
    nt = (((1,), (1,)), ((), ()))
    lane = lax.broadcasted_iota(jnp.int32, (TQ, TQ), 1)
    row = lax.broadcasted_iota(jnp.int32, (TQ, TQ), 0)

    def tile(start, aligned, base, prefix, index, parts):
        rows_at = pl.ds(pl.multiple_of(aligned + index * TQ, 16), TQ)
        for h in range(width // HD):
            cols = slice(h * HD, (h + 1) * HD)
            q = qs[rows_at, cols]
            scores, values = [], []
            for part in range(parts):
                at = pl.ds(pl.multiple_of(base + part * TQ, TQ), TQ)
                score = lax.dot_general(q, stored[at, :HD], nt, preferred_element_type=jnp.float32)
                if part == parts - 1:
                    score = jnp.where(lane < prefix - part * TQ, score, NEG_MASK)
                scores.append(score)
                values.append((stored, at, slice(HD, 2 * HD)))
            for part in range(index + 1):
                at = pl.ds(pl.multiple_of(aligned + part * TQ, 16), TQ)
                score = lax.dot_general(q, ks[at, :], nt, preferred_element_type=jnp.float32)
                if part == index:
                    score = jnp.where(lane <= row, score, NEG_MASK)
                if part == 0:
                    score = jnp.where(lane >= start - aligned, score, NEG_MASK)
                scores.append(score)
                values.append((vs, at, slice(0, HD)))
            peak = scores[0]
            for score in scores[1:]:
                peak = jnp.maximum(peak, score)
            peak = jnp.max(peak, axis=1, keepdims=True)
            total, gathered = None, None
            for score, (ref, at, which) in zip(scores, values):
                e = jnp.exp2((score - peak) * factor)
                total = e if total is None else total + e
                part = jnp.dot(e.astype(jnp.bfloat16), ref[at, which], preferred_element_type=jnp.float32)
                gathered = part if gathered is None else gathered + part
            result = gathered / jnp.sum(total, axis=1, keepdims=True)
            if index == 0:
                keep = row[:, :HD] + aligned < start
                result = jnp.where(keep, outs[rows_at, cols].astype(jnp.float32), result)
            outs[rows_at, cols] = result.astype(jnp.bfloat16)

    def one(request, start):
        end, prefix = start + lens_ref[0, request], pref_ref[request]
        aligned = start // 16 * 16
        base = request * PREF_MAX
        fetch(request).wait()
        for index in range(3):
            for parts in (1, 2):
                fits = (prefix <= TQ) if parts == 1 else (prefix > TQ)
                pl.when((aligned + index * TQ < end) & fits)(
                    functools.partial(tile, start, aligned, base, prefix, index, parts)
                )
        return end

    lax.fori_loop(0, REQ_REP, one, 0)
    store = pltpu.make_async_copy(outs.at[inside], o_ref, out_sem)
    store.start()
    store.wait()


def attend(lengths, prefix, q, k, v, cache):
    rows, width = q.shape
    bf16, dma = jnp.bfloat16, pltpu.SemaphoreType.DMA
    return pl.pallas_call(
        attention_kernel,
        out_shape=jax.ShapeDtypeStruct((rows, width), bf16),
        in_specs=[smem(), smem(), anywhere(), anywhere(), anywhere(), anywhere()],
        out_specs=anywhere(),
        scratch_shapes=[
            pltpu.VMEM((rows + TQ, width), bf16),
            pltpu.VMEM((rows + TQ, HD), bf16),
            pltpu.VMEM((rows + TQ, HD), bf16),
            pltpu.VMEM((REQ_REP * PREF_MAX, 2 * HD), bf16),
            pltpu.VMEM((rows + TQ, width), bf16),
            dma((REQ_REP + 3,)),
            dma,
        ],
        compiler_params=pltpu.CompilerParams(vmem_limit_bytes=VMEM_ALL),
        cost_estimate=pl.CostEstimate(flops=2 * 10**9, bytes_accessed=3 * 2**20, transcendentals=2 * 10**6),
        name="attention",
    )(lengths, prefix, q, k, v, cache)


def output_kernel(
    att_ref, hidden_ref, wo_here,
    resid_out, inverse_ref,
    resid_ref, wo_ref, att, part_send, part_recv, own, hid, sums_mine, sums,
    hid_sem, ring_send, ring_recv, core_send, core_recv, part_sems, sum_send, sum_recv, wo_sem, own_sem, wo_send, wo_recv, store_sem,
):
    rep, tp, x, z, zh, y, c = place()
    rows, width = hid.shape
    load = pltpu.make_async_copy(
        hidden_ref.at[:, pl.ds(pl.multiple_of(tp * width, width), width)], hid, hid_sem
    )
    load.start()
    load_wo = pltpu.make_async_copy(wo_here, wo_ref.at[pl.ds(x * 4, 4)], wo_sem)
    load_wo.start()
    load_own = pltpu.make_async_copy(att_ref, att.at[0, 0], own_sem)
    load_own.start()
    barrier = pltpu.get_barrier_semaphore()
    for k in range(1, 16):
        signal(barrier, (rep, (tp + k) % 16))
    for dx in (1, 3):
        signal(barrier, ((x + dx) % 4 * 4 + z, tp))
    pl.semaphore_wait(barrier, 17)

    def at_y(to):
        return (rep, zh * 8 + (to % 4) * 2 + c)

    partner = (rep, tp + 1 - 2 * c)
    across = (rep, (tp + 8) % 16)
    size = rows // CHUNKS
    half = size // 2
    pending = []

    def send(src, dst, ssem, rsem, device):
        made = pltpu.make_async_remote_copy(
            src_ref=src, dst_ref=dst, send_sem=ssem, recv_sem=rsem, device_id=device, device_id_type=MESH
        )
        made.start()
        pending.append(made)

    def wait(ref, sem):
        pltpu.make_async_copy(ref, ref, sem).wait()

    def own_send(m):
        at = pl.ds(m * size, size)
        src = att_ref.at[at]
        send(src, att.at[0, 1, at], ring_send.at[0, m], ring_recv.at[0, m], at_y(y + 1))
        send(src, att.at[0, 2, at], ring_send.at[1, m], ring_recv.at[1, m], at_y(y + 3))
        send(src, att.at[1, 0, at], core_send.at[0, m], core_recv.at[0, m], partner)

    def ring_in(m):
        at = pl.ds(m * size, size)
        for side in range(2):
            ref = att.at[0, 1 + side, at]
            wait(ref, ring_recv.at[side, m])
            part = pl.ds(m * size + side * half, half)
            send(
                att.at[0, 1 + side, part], att.at[0, 3, part],
                ring_send.at[2 + side, m], ring_recv.at[2 + side, m], at_y(y + 1 + 2 * side),
            )
            send(ref, att.at[1, 1 + side, at], core_send.at[1 + side, m], core_recv.at[1 + side, m], partner)

    def far_in(m):
        for side in range(2):
            wait(att.at[0, 3, pl.ds(m * size + side * half, half)], ring_recv.at[2 + side, m])
        ref = att.at[0, 3, pl.ds(m * size, size)]
        send(ref, att.at[1, 3, pl.ds(m * size, size)], core_send.at[3, m], core_recv.at[3, m], partner)

    def columns(which):
        return (1 - zh if which == 0 else zh) * 2

    def beside(dx):
        return ((x + dx) % 4 * 4 + z, tp)

    def weight_out(which):
        for side, dx in enumerate((1, 3)):
            send(
                wo_here.at[pl.ds(columns(which), 2)], wo_ref.at[pl.ds(x * 4 + columns(which), 2)],
                wo_send.at[which, side], wo_recv.at[which, side], beside(dx),
            )

    def weight_relay(which):
        for side, dx in enumerate((3, 1)):
            at = pl.ds((x + dx) % 4 * 4 + columns(which), 2)
            wait(wo_ref.at[at], wo_recv.at[which, side])
            some = wo_ref.at[at, pl.ds(side * (BLK // 2), BLK // 2)]
            send(some, some, wo_send.at[which, 2 + side], wo_recv.at[which, 2 + side], beside(4 - dx))

    def weight_in(which):
        for side in range(2):
            some = pl.ds(side * (BLK // 2), BLK // 2)
            wait(wo_ref.at[pl.ds((x + 2) % 4 * 4 + columns(which), 2), some], wo_recv.at[which, 2 + side])

    def contract(at, target):
        total = None
        for side in range(2):
            for d, dy in enumerate((0, 3, 1, 2)):
                core = c if side == 0 else 1 - c
                block = ((y + dy) % 4) * 4 + target * 2 + core
                part = jnp.dot(att[side, d, at, :], wo_ref[block], preferred_element_type=jnp.float32)
                total = part if total is None else total + part
        return total

    def away(m):
        at = pl.ds(m * size, size)
        for d in range(4):
            wait(att.at[1, d, at], core_recv.at[d, m])
        part_send[at, :] = contract(at, 1 - zh).astype(jnp.bfloat16)
        send(part_send.at[at], part_recv.at[at], part_sems.at[0, m], part_sems.at[1, m], across)

    def mine(m):
        at = pl.ds(m * BLK, BLK)
        own[at, :] = contract(at, zh)

    own_send(0)
    weight_out(0)
    own_send(1)
    own_send(2)
    load_wo.wait()
    load_own.wait()
    ready = 0
    for i in range(CHUNKS + 2):
        if i < CHUNKS:
            ring_in(i)
        if i + 3 < CHUNKS:
            own_send(i + 3)
        if 1 <= i <= CHUNKS:
            far_in(i - 1)
        if i == 1:
            weight_relay(0)
        if i == WEIGHT_AT:
            weight_in(0)
            weight_out(1)
        if i == CHUNKS - 1:
            weight_relay(1)
        if i >= WEIGHT_AT:
            for _ in range(2):
                if ready <= i - 2:
                    away(ready)
                    ready += 1
        if i == CHUNKS:
            weight_in(1)
            for m in range(OWN_EARLY):
                mine(m)
    for m in range(OWN_EARLY, rows // BLK):
        mine(m)
    load.wait()
    for m in range(CHUNKS):
        at = pl.ds(m * size, size)
        wait(part_recv.at[at], part_sems.at[1, m])
        for i in range(size // HD):
            row = m * (size // HD) + i
            here = pl.ds(row * HD, HD)
            resid = (
                hid[here, :].astype(jnp.float32) + (own[here, :] + part_recv[here, :].astype(jnp.float32))
            ).astype(jnp.bfloat16)
            resid_ref[here, :] = resid
            wide = resid.astype(jnp.float32)
            total = jnp.sum(wide * wide, axis=1, keepdims=True)
            sums_mine[pl.ds(row, 1), :] = jnp.transpose(jnp.broadcast_to(total, (HD, HD)))[:1, :]
    store = pltpu.make_async_copy(resid_ref, resid_out, store_sem)
    for k in range(1, 16):
        send(sums_mine, sums.at[k], sum_send.at[k], sum_recv.at[k], (rep, (tp + k) % 16))
    store.start()
    total = sums_mine[...]
    for k in range(1, 16):
        wait(sums.at[k], sum_recv.at[k])
        total = total + sums[k]
    inverse_ref[...] = lax.rsqrt(total * (1.0 / D) + norm_eps)
    store.wait()
    for made in pending:
        made.wait_send()


def finish(attended, hidden, wo_here):
    rows, width = attended.shape
    bf16, f32, dma = jnp.bfloat16, jnp.float32, pltpu.SemaphoreType.DMA
    return pl.pallas_call(
        output_kernel,
        out_shape=(jax.ShapeDtypeStruct((rows, width), bf16), jax.ShapeDtypeStruct((rows // HD, HD), f32)),
        in_specs=[anywhere(), anywhere(), anywhere()],
        out_specs=(anywhere(), vmem()),
        scratch_shapes=[
            pltpu.VMEM((rows, width), bf16),
            pltpu.VMEM((16, BLK, BLK), bf16),
            pltpu.VMEM((2, 4, rows, width), bf16),
            pltpu.VMEM((rows, width), bf16),
            pltpu.VMEM((rows, width), bf16),
            pltpu.VMEM((rows, width), f32),
            pltpu.VMEM((rows, width), bf16),
            pltpu.VMEM((rows // HD, HD), f32),
            pltpu.VMEM((16, rows // HD, HD), f32),
            dma,
            dma((4, CHUNKS)),
            dma((4, CHUNKS)),
            dma((4, CHUNKS)),
            dma((4, CHUNKS)),
            dma((2, CHUNKS)),
            dma((16,)),
            dma((16,)),
            dma,
            dma,
            dma((2, 4)),
            dma((2, 4)),
            dma,
        ],
        compiler_params=pltpu.CompilerParams(collective_id=1, has_side_effects=True, vmem_limit_bytes=VMEM_ALL),
        cost_estimate=pl.CostEstimate(flops=2 * 10**9, bytes_accessed=6 * 2**20, transcendentals=10**4),
        name="finish",
    )(attended, hidden, wo_here)


def scale_kernel(resid_in, inverse_ref, gain_ref, resid_out, normed_out, gain_row, resid, normed, in_sem, out_sem, norm_sem):
    rows, width = resid.shape
    count = in_sem.shape[0]
    size = rows // count
    loads, stores = [], []
    for i in range(count):
        at = pl.ds(i * size, size)
        loads.append(pltpu.make_async_copy(resid_in.at[at], resid.at[at], in_sem.at[i]))
        loads[-1].start()
    gain_row[...] = gain_ref[...].astype(jnp.float32).reshape(1, D)
    gain = gain_row[:, pl.ds(pl.multiple_of(lax.axis_index("tp") * width, width), width)]
    for i in range(count):
        at = pl.ds(i * size, size)
        loads[i].wait()
        stores.append(pltpu.make_async_copy(resid.at[at], resid_out.at[at], out_sem.at[i]))
        stores[-1].start()
        for row in range(i * size // HD, (i + 1) * size // HD):
            here = pl.ds(row * HD, HD)
            column = jnp.transpose(jnp.broadcast_to(inverse_ref[row : row + 1, :], (HD, HD)))
            for h in range(width // HD):
                cols = slice(h * HD, (h + 1) * HD)
                normed[here, cols] = (
                    resid[here, cols].astype(jnp.float32) * column * gain[:, cols]
                ).astype(jnp.bfloat16)
        stores.append(pltpu.make_async_copy(normed.at[at], normed_out.at[at], norm_sem.at[i]))
        stores[-1].start()
    for store in stores:
        store.wait()


def scale(resid, inverse, out_gain):
    rows, width = resid.shape
    bf16, dma = jnp.bfloat16, pltpu.SemaphoreType.DMA
    return pl.pallas_call(
        scale_kernel,
        out_shape=(jax.ShapeDtypeStruct((rows, width), bf16), jax.ShapeDtypeStruct((rows, width), bf16)),
        in_specs=[anywhere(), vmem(), vmem()],
        out_specs=(anywhere(), anywhere()),
        scratch_shapes=[
            pltpu.VMEM((1, D), jnp.float32),
            pltpu.VMEM((rows, width), bf16),
            pltpu.VMEM((rows, width), bf16),
            dma((8,)),
            dma((8,)),
            dma((8,)),
        ],
        compiler_params=pltpu.CompilerParams(vmem_limit_bytes=VMEM_ALL),
        cost_estimate=pl.CostEstimate(flops=10**6, bytes_accessed=3 * 2**19, transcendentals=0),
        name="scale",
    )(resid, inverse, out_gain)


def body(hidden, norm_gain, w_query, w_keyval, w_output, cache, lengths, prefix, out_gain):
    powers = np.arange(HD) % (HD // 2) * 2.0 / HD
    freqs = jnp.asarray((rope_base**-powers).astype(np.float32).reshape(1, HD))
    q, k, v, wo_here = project(lengths, prefix, hidden, norm_gain, freqs, w_query, w_keyval.T, w_output)
    attended = attend(lengths, prefix, q, k, v, cache)
    resid, inverse = finish(attended, hidden, wo_here)
    return scale(resid, inverse, out_gain)


def solution(mesh):
    placed = (
        P("rep", None),
        P(),
        P("rep", "tp"),
        P("rep", "tp"),
        P("tp", "rep"),
        P("rep", None),
        P("rep", None),
        P("rep"),
        P(),
    )
    return jax.shard_map(
        body,
        mesh=mesh,
        in_specs=placed,
        out_specs=(P("rep", "tp"), P("rep", "tp")),
        check_vma=False,
    )
```
